32 devices in a mesh: group: 2 (over y), tensor: 4 (over z), dp: 4 (over x, core).
Axes of the slice: x: 2, y: 2, z: 4, core: 2. Of those that a mesh axis runs over, the one named last changes fastest.
Arguments:
- teacher_input: bfloat16 [16, 257, 6144], P(('group', 'dp')), parts along dimension 0, may hold values from -1000 to 1000
- teacher_gain: float32 [6144], replicated, may hold values from 0.5 to 2
- teacher_weight: bfloat16 [6144, 2, 6144], P('dp', None, 'tensor'), may hold values from -30 to 30
- head_counts: int32 [48, 16], replicated, may hold values from 0 to 3
- assignment: int32 [16], P(('group', 'dp')), parts along dimension 0, may hold values from 0 to 7, each once
- student_input: bfloat16 [16, 257, 1024], P(('group', 'dp')), parts along dimension 0, may hold values from -1000 to 1000
- student_gain: float32 [1024], replicated, may hold values from 0.5 to 2
- student_bias: float32 [1024], replicated, may hold values from -3 to 3
- student_weight: bfloat16 [1024, 2048], P(None, 'tensor'), may hold values from -30 to 30
Outputs:
- weight_grad: float32 [2048, 2048], P('group', 'tensor'), parts along dimension 0
The draws below stay inside these ranges and needn't reach their ends.
There are 2 independent parts, one for each index of `group`. The reference program is written for one: setup_inputs(seed, part) draws one part's arguments, and reference() takes and returns one part's arrays. A program takes and returns all parts, laid end to end along the dimension named above; an argument that names none is the same for every part. Nothing has to cross between parts.
Inputs may be any that keep to these rules, and one draw needn't show every extreme that they name: `assignment`: every image index of the group appears exactly once.
All inputs are finite; a program needn't handle non-finite values.
Results may differ from the reference program's by a relative error of at most 0.013.
The reference program's roundings to bfloat16 on the way count: a program that leaves them out, or rounds other values in their place, can miss the bound.
Values may be sent and summed in bfloat16 or wider, within the bound.
A program may use at most 192 MiB of HBM per device.

```python
import math
import jax
import jax.numpy as jnp
from jax import lax

D_T = 6144
HEADS_T = 48
HD_T = 128
D_S = 1024
HEADS_S = 16
HD_S = 64
TOKENS = 257
QROWS = 128
IMAGES = 8
DIVISOR = 72
N_TENSOR = 4


def rough_input(key, width):
    keys = jax.random.split(key, 4)
    base = jax.random.normal(keys[0], (IMAGES, TOKENS, width), jnp.float32)
    scales = jnp.exp(jax.random.uniform(keys[2], (IMAGES, TOKENS, 1), jnp.float32, 0.0, math.log(10.0)))
    columns = jnp.exp(jax.random.uniform(keys[3], (width,), jnp.float32, 0.0, math.log(10.0)))
    return jnp.clip(base, -6.0, 6.0) * columns * scales


def rough_weight(key, width, heads, size):
    keys = jax.random.split(key, 2)
    query = jnp.clip(jax.random.normal(keys[0], (width, heads, size), jnp.float32), -4.0, 4.0) / math.sqrt(width)
    other = jnp.clip(jax.random.normal(keys[1], (width, heads, size), jnp.float32), -4.0, 4.0) / math.sqrt(width)
    return (query, other)


def draw_teacher_input(key, part):
    return rough_input(key, D_T).astype(jnp.bfloat16)


def draw_student_input(key, part):
    return rough_input(jax.random.fold_in(key, 7), D_S).astype(jnp.bfloat16)


def draw_teacher_weight(key, part):
    query, other = rough_weight(jax.random.fold_in(key, 11), D_T, HEADS_T, HD_T)
    return jnp.stack([query, other], axis=1).reshape(D_T, 2, HEADS_T * HD_T).astype(jnp.bfloat16)


def draw_student_weight(key, part):
    query, other = rough_weight(jax.random.fold_in(key, 13), D_S, HEADS_S, HD_S)
    return jnp.stack([query, other], axis=2).reshape(D_S, HEADS_S * 2 * HD_S).astype(jnp.bfloat16)


def with_ends(entries, own_key, low, high):
    spot = [jax.random.randint(jax.random.fold_in(own_key, axis), (), 0, length) for axis, length in enumerate(entries.shape)]
    longest = entries.shape.index(max(entries.shape))
    next_to = spot[:longest] + [(spot[longest] + 1) % entries.shape[longest]] + spot[longest + 1:]
    return entries.at[tuple(spot)].set(low).at[tuple(next_to)].set(high)


def normal_values(own_key, shape, scale, bound, held_as=jnp.bfloat16):
    return jnp.clip(scale * jax.random.normal(own_key, shape, jnp.float32), -bound, bound).astype(held_as)


def setup_inputs(seed: int = 0, part: int = 0) -> dict:
    arg_keys = jax.random.split(jax.random.key(seed), 10)
    part_splits = jax.random.split(jax.random.fold_in(arg_keys[9], part), 10)
    teacher_input = draw_teacher_input(jax.random.fold_in(jax.random.fold_in(arg_keys[9], part), 71), part)
    teacher_gain = jnp.clip(jnp.exp(jax.random.uniform(arg_keys[1], (D_T,), jnp.float32, math.log(0.5), math.log(2.0))), 0.5, 2.0)
    teacher_weight = draw_teacher_weight(jax.random.fold_in(arg_keys[9], 71), part)
    head_counts = with_ends(jax.random.randint(arg_keys[3], (HEADS_T, HEADS_S), 0, 4), jax.random.fold_in(arg_keys[3], 1), 0, 3).astype(jnp.int32)
    assignment = jax.random.permutation(part_splits[4], IMAGES).astype(jnp.int32)
    student_input = draw_student_input(jax.random.fold_in(jax.random.fold_in(arg_keys[9], part), 71), part)
    student_gain = jnp.clip(jnp.exp(jax.random.uniform(arg_keys[6], (D_S,), jnp.float32, math.log(0.5), math.log(2.0))), 0.5, 2.0)
    student_bias = normal_values(arg_keys[7], (D_S,), 0.5, 3.0, jnp.float32)
    student_weight = draw_student_weight(jax.random.fold_in(arg_keys[9], 71), part)
    return dict(teacher_input=teacher_input, teacher_gain=teacher_gain, teacher_weight=teacher_weight, head_counts=head_counts, assignment=assignment, student_input=student_input, student_gain=student_gain, student_bias=student_bias, student_weight=student_weight)


def layer_norm(values, gain, shift):
    wide = values.astype(jnp.float32)
    center = wide - lax.optimization_barrier(jnp.mean(wide, axis=-1, keepdims=True))
    spread = lax.optimization_barrier(jnp.mean(center * center, axis=-1, keepdims=True))
    return center * lax.rsqrt(spread + 1e-06) * gain + shift

def reference(teacher_input, teacher_gain, teacher_weight, head_counts, assignment, student_input, student_gain, student_bias, student_weight):
    heads_dev = HEADS_T // N_TENSOR
    counts_grouped = head_counts.astype(jnp.float32).reshape(N_TENSOR, heads_dev, HEADS_S)

    def teacher_image(image):
        normed = layer_norm(image, teacher_gain, 0.0).astype(jnp.bfloat16)
        query = (jnp.dot(normed[:QROWS], teacher_weight[:, 0, :], preferred_element_type=jnp.float32) * HD_T ** (-0.5)).astype(jnp.bfloat16)
        keys = jnp.dot(normed, teacher_weight[:, 1, :], preferred_element_type=jnp.float32).astype(jnp.bfloat16)
        query = query.reshape(QROWS, HEADS_T, HD_T).astype(jnp.float32)
        keys = keys.reshape(TOKENS, HEADS_T, HD_T).astype(jnp.float32)
        scores = jnp.einsum('qhd,khd->hqk', query, keys)
        maps = jax.nn.softmax(scores, axis=-1).astype(jnp.bfloat16)
        grouped = maps.astype(jnp.float32).reshape(N_TENSOR, heads_dev, QROWS, TOKENS)
        partial_value = (jnp.einsum('tgqk,tgs->tsqk', grouped, counts_grouped) / DIVISOR).astype(jnp.bfloat16)
        partial_value = lax.optimization_barrier(partial_value)
        return lax.optimization_barrier(jnp.sum(partial_value.astype(jnp.float32), axis=0)).astype(jnp.bfloat16)
    folded = lax.map(teacher_image, teacher_input)
    packed = student_weight.reshape(D_S, HEADS_S, 2, HD_S)
    weight_query = packed[:, :, 0, :].reshape(D_S, HEADS_S * HD_S)
    weight_key = packed[:, :, 1, :].reshape(D_S, HEADS_S * HD_S)

    def student_image(total, slot):
        image = student_input[slot]
        target = lax.dynamic_index_in_dim(folded, assignment[slot].astype(jnp.int32), 0, keepdims=False).astype(jnp.float32)
        normed = layer_norm(image, student_gain, student_bias).astype(jnp.bfloat16)
        query = (jnp.dot(normed[:QROWS], weight_query, preferred_element_type=jnp.float32) * HD_S ** (-0.5)).astype(jnp.bfloat16)
        keys = jnp.dot(normed, weight_key, preferred_element_type=jnp.float32).astype(jnp.bfloat16)
        query = query.reshape(QROWS, HEADS_S, HD_S).astype(jnp.float32)
        keys = keys.reshape(TOKENS, HEADS_S, HD_S).astype(jnp.float32)
        probs = jax.nn.softmax(jnp.einsum('qhd,khd->hqk', query, keys), axis=-1)
        score_grad = (probs * lax.optimization_barrier(jnp.sum(target, axis=-1, keepdims=True)) - target).astype(jnp.bfloat16).astype(jnp.float32)
        query_grad = (jnp.einsum('hqk,khd->qhd', score_grad, keys) * HD_S ** (-0.5)).astype(jnp.bfloat16)
        key_grad = jnp.einsum('hqk,qhd->khd', score_grad, query).astype(jnp.bfloat16)
        grad_query = jnp.dot(normed[:QROWS].T, query_grad.reshape(QROWS, HEADS_S * HD_S), preferred_element_type=jnp.float32)
        grad_key = jnp.dot(normed.T, key_grad.reshape(TOKENS, HEADS_S * HD_S), preferred_element_type=jnp.float32)
        both = jnp.stack([grad_query.reshape(D_S, HEADS_S, HD_S), grad_key.reshape(D_S, HEADS_S, HD_S)], axis=2)
        return (total + both.reshape(D_S, HEADS_S * 2 * HD_S), None)
    start = jnp.zeros((D_S, HEADS_S * 2 * HD_S), jnp.float32)
    weight_grad, _ = lax.scan(student_image, start, jnp.arange(IMAGES, dtype=jnp.int32))
    return weight_grad
```

```python
import functools

import jax
import jax.numpy as jnp
from jax import lax
from jax.experimental import pallas as pl
from jax.experimental.pallas import tpu as pltpu
from jax.sharding import PartitionSpec as P

HD_T = 128
HD_S = 64
QROWS = 128
DIVISOR = 72
CORES = 2
MESH = pl.DeviceIdType.MESH


def layer_norm(values, gain, shift):
    wide = values.astype(jnp.float32)
    center = wide - jnp.mean(wide, axis=-1, keepdims=True)
    spread = jnp.mean(center * center, axis=-1, keepdims=True)
    return center * lax.rsqrt(spread + 1e-06) * gain + shift


def rounded_up(value, unit):
    return -(-value // unit) * unit


def teacher_kernel(
    sizes,
    counts_ref,
    slots_ref,
    x_ref,
    gain_ref,
    w_ref,
    out_ref,
    wraw,
    wsplit,
    xraw,
    normed,
    rows_in,
    stage,
    from_mate,
    x_out,
    x_in,
    held,
    acc,
    made,
    landed,
    gathered,
    w_sem,
    x_sem,
    s_row_mate,
    r_row_mate,
    s_row_x,
    r_row_x,
    s_row_z,
    r_row_z,
    s_part,
    r_part,
    s_sum,
    r_sum,
    s_map,
    r_map,
    s_goal,
    r_goal,
    s_goal_mate,
    r_goal_mate,
):
    n_dp, n_tensor, s_heads, images, tokens, pad, blocks, chunk = sizes
    n_x = n_dp // CORES
    depth = w_ref.shape[0]
    width = wsplit.shape[3]
    s_here = s_heads // n_tensor
    w_chunks = depth // chunk

    dp = lax.axis_index("dp")
    t = lax.axis_index("tensor")
    x = dp // CORES
    core = lax.rem(dp, CORES)
    mate = x * CORES + (1 - core)
    parity = lax.rem(t, 2)
    neighbour = t + 1 - 2 * parity

    def x_peer(s):
        return lax.rem(x + s, n_x)

    def x_source(s):
        return lax.rem(x + n_x - s, n_x)

    def w_copy(n):
        slot = lax.rem(n, 2)
        return pltpu.make_async_copy(
            w_ref.at[pl.ds(n * chunk, chunk)], wraw.at[slot], w_sem.at[slot]
        )

    low = QROWS
    pieces = (
        ((0, low // 2), (low // 2, low // 2)),
        ((low, (pad - low) // 32 * 16), (low + (pad - low) // 32 * 16, pad - low - (pad - low) // 32 * 16)),
    )

    def x_fetch(half):
        first = pieces[half][0][0]
        last = pieces[half][-1][0] + pieces[half][-1][1]
        many = min(last, tokens) - first
        return pltpu.make_async_copy(
            x_ref.at[pl.ds(first, many)], xraw.at[pl.ds(first, many)], x_sem.at[half]
        )

    def on_half(which, act):
        for half in range(2):

            @pl.when(which == half)
            def _():
                act(half)

    for half in range(2):
        xraw[tokens:pad] = jnp.zeros((pad - tokens,) + xraw.shape[1:], jnp.bfloat16)
    on_half(parity, lambda half: x_fetch(half).start())
    on_half(1 - parity, lambda half: x_fetch(half).start())
    w_copy(0).start()
    w_copy(1).start()
    acc[...] = jnp.zeros_like(acc)

    barrier = pltpu.get_barrier_semaphore()
    waits = 0
    for s in range(1, n_dp):
        pl.semaphore_signal(
            barrier, inc=1, device_id={"dp": lax.rem(dp + s, n_dp)}, device_id_type=MESH
        )
        waits += 1
    for s in range(1, n_tensor):
        pl.semaphore_signal(
            barrier, inc=1, device_id={"tensor": lax.rem(t + s, n_tensor)}, device_id_type=MESH
        )
        waits += 1
    pl.semaphore_wait(barrier, waits)

    def row_mate(i):
        return pltpu.make_async_remote_copy(
            src_ref=normed.at[mate, i],
            dst_ref=rows_in.at[i, dp],
            send_sem=s_row_mate.at[i],
            recv_sem=r_row_mate.at[i],
            device_id={"dp": mate},
            device_id_type=MESH,
        )

    def row_x(s, c, i, half, n):
        first, many = pieces[half][n]
        to = x_peer(s) * CORES + c
        return pltpu.make_async_remote_copy(
            src_ref=normed.at[to, i, pl.ds(first, many)],
            dst_ref=rows_in.at[i, dp, pl.ds(first, many)],
            send_sem=s_row_x.at[s - 1, c, i, n],
            recv_sem=r_row_x.at[s - 1, core, i, n],
            device_id={"dp": to},
            device_id_type=MESH,
        )

    def row_x_arrived(s, c, i, half, n):
        first, many = pieces[half][n]
        return pltpu.make_async_remote_copy(
            src_ref=normed.at[dp, i, pl.ds(first, many)],
            dst_ref=rows_in.at[i, x_source(s) * CORES + c, pl.ds(first, many)],
            send_sem=s_row_x.at[s - 1, c, i, n],
            recv_sem=r_row_x.at[s - 1, c, i, n],
            device_id={"dp": mate},
            device_id_type=MESH,
        )

    def row_z(s, c, i, half, n):
        first, many = pieces[half][n]
        where = rows_in.at[i, x_source(s) * CORES + c, pl.ds(first, many)]
        return pltpu.make_async_remote_copy(
            src_ref=where,
            dst_ref=where,
            send_sem=s_row_z.at[s - 1, c, i, n],
            recv_sem=r_row_z.at[s - 1, c, i, n],
            device_id={"tensor": neighbour},
            device_id_type=MESH,
        )

    def part_copy(u, i, b):
        return pltpu.make_async_remote_copy(
            src_ref=stage.at[u, i, b],
            dst_ref=from_mate.at[u, i, b],
            send_sem=s_part.at[u, i, b],
            recv_sem=r_part.at[u, i, b],
            device_id={"dp": mate},
            device_id_type=MESH,
        )

    def sum_copy(s, i, b):
        return pltpu.make_async_remote_copy(
            src_ref=x_out.at[s - 1, i, b],
            dst_ref=x_in.at[s - 1, i, b],
            send_sem=s_sum.at[s - 1, i, b],
            recv_sem=r_sum.at[s - 1, i, b],
            device_id={"dp": x_peer(s) * CORES + core},
            device_id_type=MESH,
        )

    def map_copy(s, i):
        to = lax.rem(t + s, n_tensor)
        return pltpu.make_async_remote_copy(
            src_ref=made.at[i, pl.ds(to * s_here, s_here)],
            dst_ref=landed.at[s - 1, i],
            send_sem=s_map.at[s - 1, i],
            recv_sem=r_map.at[s - 1, i],
            device_id={"tensor": to},
            device_id_type=MESH,
        )

    def goal_copy(s, i):
        own = gathered.at[dp * images + i]
        return pltpu.make_async_remote_copy(
            src_ref=own,
            dst_ref=own,
            send_sem=s_goal.at[s - 1, i],
            recv_sem=r_goal.at[s - 1, i],
            device_id={"dp": x_peer(s) * CORES + core},
            device_id_type=MESH,
        )

    def goal_mate(s, i):
        block = gathered.at[(x_source(s) * CORES + core) * images + i]
        return pltpu.make_async_remote_copy(
            src_ref=block,
            dst_ref=block,
            send_sem=s_goal_mate.at[s, i],
            recv_sem=r_goal_mate.at[s, i],
            device_id={"dp": mate},
            device_id_type=MESH,
        )

    def norm_piece(first, many):
        gain = gain_ref[...]

        def norm_rows(r, carry):
            spot = pl.multiple_of(first + r * 16, 16)
            both = jnp.swapaxes(xraw[pl.ds(spot, 16)], 0, 1)
            for i in range(images):
                block = layer_norm(both[i], gain, 0.0).astype(jnp.bfloat16)
                for d in range(n_dp):
                    normed[d, i, pl.ds(spot, 16), :] = block[:, d * depth : (d + 1) * depth]
            return carry

        lax.fori_loop(0, many // 16, norm_rows, 0)

    def send_half(half):
        x_fetch(half).wait()
        for n in range(2):
            norm_piece(*pieces[half][n])
            for s in range(1, n_x):
                for c in range(CORES):
                    row_x(s, c, 0, half, n).start()
        for i in range(1, images):
            for n in range(2):
                for s in range(1, n_x):
                    for c in range(CORES):
                        row_x(s, c, i, half, n).start()

    def norm_half(half):
        x_fetch(half).wait()
        for n in range(2):
            norm_piece(*pieces[half][n])

    on_half(parity, send_half)
    on_half(1 - parity, norm_half)
    for i in range(images):
        row_mate(i).start()

    def split(n, carry):
        w_copy(n).wait()
        slot = lax.rem(n, 2)
        spot = pl.ds(pl.multiple_of(n * chunk, chunk), chunk)
        for b in range(blocks):
            both = jnp.swapaxes(wraw[slot, :, :, b * width : (b + 1) * width], 0, 1)
            wsplit[0, b, spot, :] = both[0]
            wsplit[1, b, spot, :] = both[1]

        @pl.when(n + 2 < w_chunks)
        def _():
            w_copy(n + 2).start()

        return carry

    lax.fori_loop(0, w_chunks, split, 0)

    def project(lhs, b):
        keys = jnp.dot(lhs[...], wsplit[1, b], preferred_element_type=jnp.float32)
        query = jnp.dot(lhs[:QROWS], wsplit[0, b], preferred_element_type=jnp.float32)
        return keys, query

    for i in range(images):
        row_mate(i).wait_recv()

        def own_chip(b, carry):
            keys, query = project(rows_in.at[i, mate], b)
            stage[0, i, b, :pad] = keys.astype(jnp.bfloat16)
            stage[0, i, b, pad:] = query.astype(jnp.bfloat16)
            part_copy(0, i, b).start()
            return carry

        lax.fori_loop(0, blocks, own_chip, 0)

    for i in range(images):

        def pass_on(half):
            for n in range(2):
                for s in range(1, n_x):
                    for c in range(CORES):
                        row_x_arrived(s, c, i, half, n).wait_recv()
                        row_z(s, c, i, half, n).start()

        def passed_on(half):
            for n in range(2):
                for s in range(1, n_x):
                    for c in range(CORES):
                        row_z(s, c, i, half, n).wait_recv()

        on_half(parity, pass_on)
        on_half(1 - parity, passed_on)

        for s in range(1, n_x):

            def other_chip(b, carry):
                @pl.when(b < blocks)
                def _():
                    away = x_peer(s) * CORES
                    keys, query = project(rows_in.at[i, away + 1 - core], b)
                    stage[s, i, b, :pad] = keys.astype(jnp.bfloat16)
                    stage[s, i, b, pad:] = query.astype(jnp.bfloat16)
                    part_copy(s, i, b).start()
                    keys, query = project(rows_in.at[i, away + core], b)
                    held[lax.rem(b, 2), :pad] = keys
                    held[lax.rem(b, 2), pad:] = query

                @pl.when(b > 0)
                def _():
                    j = b - 1
                    part_copy(s, i, j).wait_recv()
                    total = held[lax.rem(j, 2)] + from_mate[s, i, j].astype(jnp.float32)
                    x_out[s - 1, i, j] = total.astype(jnp.bfloat16)
                    sum_copy(s, i, j).start()

                return carry

            lax.fori_loop(0, blocks + 1, other_chip, 0)

    for i in range(images):

        def attend(b, carry):
            keys, query = project(normed.at[dp, i], b)
            part_copy(0, i, b).wait_recv()
            keys += from_mate[0, i, b, :pad].astype(jnp.float32)
            query += from_mate[0, i, b, pad:].astype(jnp.float32)
            for s in range(1, n_x):
                sum_copy(s, i, b).wait_recv()
                keys += x_in[s - 1, i, b, :pad].astype(jnp.float32)
                query += x_in[s - 1, i, b, pad:].astype(jnp.float32)
            keys = keys.astype(jnp.bfloat16)
            query = (query * HD_T ** (-0.5)).astype(jnp.bfloat16)
            maps = []
            for h in range(width // HD_T):
                cols = slice(h * HD_T, (h + 1) * HD_T)
                scores = lax.dot_general(
                    keys[:, cols],
                    query[:, cols],
                    (((1,), (1,)), ((), ())),
                    preferred_element_type=jnp.float32,
                )
                spot = lax.broadcasted_iota(jnp.int32, scores.shape, 0)
                scores = jnp.where(spot < tokens, scores, -jnp.inf)
                power = jnp.exp(scores - jnp.max(scores, axis=0, keepdims=True))
                one = power / jnp.sum(power, axis=0, keepdims=True)
                maps.append(one.astype(jnp.bfloat16).astype(jnp.float32))
            first = t * (blocks * (width // HD_T)) + b * (width // HD_T)
            for s in range(s_heads):
                total = acc[s]
                for h, one in enumerate(maps):
                    total += counts_ref[first + h, s].astype(jnp.float32) * one
                acc[s] = total
            return carry

        lax.fori_loop(0, blocks, attend, 0)

        def finish(s, carry):
            made[i, s] = (acc[s] / DIVISOR).astype(jnp.bfloat16)
            acc[s] = jnp.zeros(acc.shape[1:], jnp.float32)
            return carry

        lax.fori_loop(0, s_heads, finish, 0)
        for s in range(1, n_tensor):
            map_copy(s, i).start()

    for i in range(images):
        for s in range(1, n_tensor):
            map_copy(s, i).wait_recv()
        for h in range(s_here):
            total = made[i, t * s_here + h].astype(jnp.float32)
            for s in range(1, n_tensor):
                total += landed[s - 1, i, h].astype(jnp.float32)
            gathered[dp * images + i, h] = total.astype(jnp.bfloat16)
        for s in range(1, n_x):
            goal_copy(s, i).start()
        goal_mate(0, i).start()

    for i in range(images):
        for s in range(1, n_x):
            goal_copy(s, i).wait_recv()
            goal_mate(s, i).start()

    def drain_half(half):
        for i in range(images):
            for n in range(2):
                for s in range(1, n_x):
                    for c in range(CORES):
                        row_x(s, c, i, half, n).wait_send()
                        row_z(s, c, i, half, n).wait_send()

    on_half(parity, drain_half)
    for i in range(images):
        row_mate(i).wait_send()
        for s in range(1, n_tensor):
            map_copy(s, i).wait_send()
        for s in range(1, n_x):
            goal_copy(s, i).wait_send()

        def drain(b, carry):
            part_copy(0, i, b).wait_send()
            for s in range(1, n_x):
                part_copy(s, i, b).wait_send()
                sum_copy(s, i, b).wait_send()
            return carry

        lax.fori_loop(0, blocks, drain, 0)
    for i in range(images):
        for s in range(n_x):
            goal_mate(s, i).wait()
    for j in range(images):
        out_ref[j] = gathered[slots_ref[j]]


def teacher_folded(mesh_sizes, teacher_input, teacher_gain, teacher_weight, head_counts, assignment):
    n_dp, n_group, n_tensor = mesh_sizes
    images, tokens, width = teacher_input.shape
    rows, _, width_here = teacher_weight.shape
    heads_here = width_here // HD_T
    s_heads = head_counts.shape[1]
    s_here = s_heads // n_tensor
    pad = rounded_up(tokens, 16)
    n_x = n_dp // CORES
    others = max(n_x - 1, 1)
    per_block = 2 if heads_here % 2 == 0 else 1
    blocks = heads_here // per_block
    block_width = per_block * HD_T
    chunk = 192
    both = pad + QROWS
    sizes = (n_dp, n_tensor, s_heads, images, tokens, pad, blocks, chunk)
    dma = pltpu.SemaphoreType.DMA
    half = jnp.bfloat16
    return pl.pallas_call(
        functools.partial(teacher_kernel, sizes),
        out_shape=jax.ShapeDtypeStruct((images, s_here, pad, QROWS), jnp.bfloat16),
        in_specs=[
            pl.BlockSpec(memory_space=pltpu.SMEM),
            pl.BlockSpec(memory_space=pltpu.SMEM),
            pl.BlockSpec(memory_space=pl.ANY),
            pl.BlockSpec(memory_space=pltpu.VMEM),
            pl.BlockSpec(memory_space=pl.ANY),
        ],
        out_specs=pl.BlockSpec(memory_space=pltpu.VMEM),
        scratch_shapes=[
            pltpu.VMEM((2, chunk, 2, width_here), half),
            pltpu.VMEM((2, blocks, rows, block_width), half),
            pltpu.VMEM((pad, images, width), half),
            pltpu.VMEM((n_dp, images, pad, rows), half),
            pltpu.VMEM((images, n_dp, pad, rows), half),
            pltpu.VMEM((n_x, images, blocks, both, block_width), half),
            pltpu.VMEM((n_x, images, blocks, both, block_width), half),
            pltpu.VMEM((others, images, blocks, both, block_width), half),
            pltpu.VMEM((others, images, blocks, both, block_width), half),
            pltpu.VMEM((2, both, block_width), jnp.float32),
            pltpu.VMEM((s_heads, pad, QROWS), jnp.float32),
            pltpu.VMEM((images, s_heads, pad, QROWS), half),
            pltpu.VMEM((n_tensor - 1, images, s_here, pad, QROWS), half),
            pltpu.VMEM((n_dp * images, s_here, pad, QROWS), half),
            dma((2,)),
            dma((2,)),
            dma((images,)),
            dma((images,)),
            dma((others, CORES, images, 2)),
            dma((others, CORES, images, 2)),
            dma((others, CORES, images, 2)),
            dma((others, CORES, images, 2)),
            dma((n_x, images, blocks)),
            dma((n_x, images, blocks)),
            dma((others, images, blocks)),
            dma((others, images, blocks)),
            dma((n_tensor - 1, images)),
            dma((n_tensor - 1, images)),
            dma((others, images)),
            dma((others, images)),
            dma((n_x, images)),
            dma((n_x, images)),
        ],
        compiler_params=pltpu.CompilerParams(
            collective_id=0, has_side_effects=True, vmem_limit_bytes=67043328
        ),
    )(
        head_counts,
        assignment,
        jnp.transpose(teacher_input, (1, 0, 2)),
        teacher_gain.reshape(1, width),
        teacher_weight,
    )


def sum_over_dp(local, n_dp):
    half = local.shape[0] // CORES
    core = lax.rem(lax.axis_index("dp"), CORES)
    mates = [(d, d ^ 1) for d in range(n_dp)]
    rounded = local.astype(jnp.bfloat16)
    mine = lax.dynamic_slice_in_dim(local, core * half, half, 0)
    other = lax.dynamic_slice_in_dim(rounded, (1 - core) * half, half, 0)
    mine = mine + lax.ppermute(other, "dp", mates).astype(jnp.float32)
    sent = mine.astype(jnp.bfloat16)
    for s in range(1, n_dp // CORES):
        around = [(d, (d + CORES * s) % n_dp) for d in range(n_dp)]
        mine = mine + lax.ppermute(sent, "dp", around).astype(jnp.float32)
    done = mine.astype(jnp.bfloat16)
    theirs = lax.ppermute(done, "dp", mates)
    first = jnp.where(core == 0, done, theirs)
    second = jnp.where(core == 0, theirs, done)
    return jnp.concatenate([first, second], axis=0).astype(jnp.float32)


def on_device(
    mesh_sizes,
    teacher_input,
    teacher_gain,
    teacher_weight,
    head_counts,
    assignment,
    student_input,
    student_gain,
    student_bias,
    student_weight,
):
    images, tokens, width_s = student_input.shape
    student_heads = student_weight.shape[1] // (2 * HD_S)
    target = teacher_folded(
        mesh_sizes, teacher_input, teacher_gain, teacher_weight, head_counts, assignment
    )
    target_wide = jnp.swapaxes(target, 0, 1).astype(jnp.float32)[:, :, :tokens]
    student_normed = layer_norm(student_input, student_gain, student_bias).astype(jnp.bfloat16)
    normed_front = student_normed[:, :QROWS]
    packed = student_weight.reshape(width_s, student_heads, 2, HD_S)
    weight_query = packed[:, :, 0, :].reshape(width_s, student_heads * HD_S)
    weight_key = packed[:, :, 1, :].reshape(width_s, student_heads * HD_S)
    student_query = (
        jnp.einsum("btd,dc->btc", normed_front, weight_query, preferred_element_type=jnp.float32)
        * HD_S ** (-0.5)
    ).astype(jnp.bfloat16)
    student_keys = jnp.einsum(
        "btd,dc->btc", student_normed, weight_key, preferred_element_type=jnp.float32
    ).astype(jnp.bfloat16)
    split_query = student_query.reshape(images, QROWS, student_heads, HD_S)
    split_keys = student_keys.reshape(images, tokens, student_heads, HD_S)
    probs = jax.nn.softmax(
        jnp.einsum("bqhd,bkhd->hbkq", split_query, split_keys, preferred_element_type=jnp.float32),
        axis=2,
    )
    score_grad = (probs * jnp.sum(target_wide, axis=2, keepdims=True) - target_wide).astype(
        jnp.bfloat16
    )
    query_grad = (
        jnp.einsum("hbkq,bkhd->bqhd", score_grad, split_keys, preferred_element_type=jnp.float32)
        * HD_S ** (-0.5)
    ).astype(jnp.bfloat16)
    key_grad = jnp.einsum(
        "hbkq,bqhd->bkhd", score_grad, split_query, preferred_element_type=jnp.float32
    ).astype(jnp.bfloat16)
    grad_query = jnp.einsum(
        "fkm,fkp->mp",
        normed_front,
        query_grad.reshape(images, QROWS, student_heads * HD_S),
        preferred_element_type=jnp.float32,
    )
    grad_key = jnp.einsum(
        "oip,ois->ps",
        student_normed,
        key_grad.reshape(images, tokens, student_heads * HD_S),
        preferred_element_type=jnp.float32,
    )
    local_grad = jnp.stack(
        [
            grad_query.reshape(width_s, student_heads, HD_S),
            grad_key.reshape(width_s, student_heads, HD_S),
        ],
        axis=2,
    )
    local_grad = local_grad.reshape(width_s, student_heads * 2 * HD_S)
    return sum_over_dp(local_grad, mesh_sizes[0])


def solution(mesh):
    placed = (
        P(("group", "dp"), None, None),
        P(),
        P("dp", None, "tensor"),
        P(),
        P(("group", "dp")),
        P(("group", "dp"), None, None),
        P(),
        P(),
        P(None, "tensor"),
    )
    mesh_sizes = (mesh.shape["dp"], mesh.shape["group"], mesh.shape["tensor"])
    return jax.shard_map(
        functools.partial(on_device, mesh_sizes),
        mesh=mesh,
        in_specs=placed,
        out_specs=P("group", "tensor"),
        check_vma=False,
    )
```

```python
import functools

import jax
import jax.numpy as jnp
from jax import lax
from jax.experimental import pallas as pl
from jax.experimental.pallas import tpu as pltpu
from jax.sharding import PartitionSpec as P

HD_T = 128
HD_S = 64
QROWS = 128
DIVISOR = 72
CORES = 2
SHARE = 4
MESH = pl.DeviceIdType.MESH


def layer_norm(values, gain, shift):
    wide = values.astype(jnp.float32)
    center = wide - jnp.mean(wide, axis=-1, keepdims=True)
    spread = jnp.mean(center * center, axis=-1, keepdims=True)
    return center * lax.rsqrt(spread + 1e-06) * gain + shift


def rounded_up(value, unit):
    return -(-value // unit) * unit


def key_softmax(scores, tokens):
    spot = lax.broadcasted_iota(jnp.int32, scores.shape, 0)
    scores = jnp.where(spot < tokens, scores, -jnp.inf)
    power = jnp.exp(scores - jnp.max(scores, axis=0, keepdims=True))
    return power / jnp.sum(power, axis=0, keepdims=True)


def distill_kernel(
    sizes,
    counts_ref,
    slots_ref,
    x_ref,
    gain_ref,
    w_ref,
    sx_ref,
    sgain_ref,
    sbias_ref,
    sw_ref,
    out_ref,
    wsplit,
    normed,
    rows_in,
    stage,
    from_mate,
    x_in,
    held,
    acc,
    made,
    landed,
    student,
    packed,
    probs,
    grads,
    slot_rows,
    slot_table,
    w_sem,
    x_sem,
    sx_sem,
    slot_sem,
    s_row_mate,
    r_row_mate,
    s_row_x,
    r_row_x,
    s_row_z,
    r_row_z,
    s_part,
    r_part,
    s_sum,
    r_sum,
    s_map,
    r_map,
    s_grad,
    r_grad,
    s_grad_mate,
    r_grad_mate,
    s_slot,
    r_slot,
    s_stu_mate,
    r_stu_mate,
    s_stu_x,
    r_stu_x,
    s_stu_z,
    r_stu_z,
):
    n_dp, n_tensor, s_heads, images, tokens, pad, blocks, chunk = sizes
    n_x = n_dp // CORES
    depth = w_ref.shape[0]
    width = wsplit.shape[3]
    s_here = s_heads // n_tensor
    s_cols = 2 * HD_S
    share, s_depth = student.shape[0], student.shape[3]
    w_chunks = depth // chunk

    dp = lax.axis_index("dp")
    t = lax.axis_index("tensor")
    x = dp // CORES
    core = lax.rem(dp, CORES)
    mate = x * CORES + (1 - core)
    parity = lax.rem(t, 2)
    neighbour = t + 1 - 2 * parity
    quarter = lax.rem(t, share)

    def x_peer(s):
        return lax.rem(x + s, n_x)

    def x_source(s):
        return lax.rem(x + n_x - s, n_x)

    low = QROWS
    cut = (pad - low) // 32 * 16
    pieces = (
        ((0, low // 2), (low // 2, low // 2)),
        ((low, cut), (low + cut, pad - low - cut)),
    )

    def on_half(which, act):
        for half in range(2):

            @pl.when(which == half)
            def _():
                act(half)

    def slot_copy(s):
        return pltpu.make_async_remote_copy(
            src_ref=slot_rows.at[dp],
            dst_ref=slot_rows.at[dp],
            send_sem=s_slot.at[s - 1],
            recv_sem=r_slot.at[s - 1],
            device_id={"dp": lax.rem(dp + s, n_dp)},
            device_id_type=MESH,
        )

    def own_slots(source):
        return pl.ds(source * images, images)

    def stu_mate(s):
        where = student.at[:, own_slots(x_source(s) * CORES + core)]
        return pltpu.make_async_remote_copy(
            src_ref=where,
            dst_ref=where,
            send_sem=s_stu_mate.at[s],
            recv_sem=r_stu_mate.at[s],
            device_id={"dp": mate},
            device_id_type=MESH,
        )

    def stu_x(s):
        where = student.at[quarter, own_slots(dp)]
        return pltpu.make_async_remote_copy(
            src_ref=where,
            dst_ref=where,
            send_sem=s_stu_x.at[s - 1],
            recv_sem=r_stu_x.at[s - 1],
            device_id={"dp": x_peer(s) * CORES + core},
            device_id_type=MESH,
        )

    def stu_z(s, q):
        where = student.at[quarter, own_slots(x_source(s) * CORES + core)]
        return pltpu.make_async_remote_copy(
            src_ref=where,
            dst_ref=where,
            send_sem=s_stu_z.at[s - 1, q - 1],
            recv_sem=r_stu_z.at[s - 1, q - 1],
            device_id={"tensor": t - quarter + lax.rem(quarter + q, share)},
            device_id_type=MESH,
        )

    def row_mate(i):
        return pltpu.make_async_remote_copy(
            src_ref=normed.at[mate, i],
            dst_ref=rows_in.at[i, dp],
            send_sem=s_row_mate.at[i],
            recv_sem=r_row_mate.at[i],
            device_id={"dp": mate},
            device_id_type=MESH,
        )

    def row_x(s, c, i, half, n):
        first, many = pieces[half][n]
        to = x_peer(s) * CORES + c
        return pltpu.make_async_remote_copy(
            src_ref=normed.at[to, i, pl.ds(first, many)],
            dst_ref=rows_in.at[i, dp, pl.ds(first, many)],
            send_sem=s_row_x.at[s - 1, c, i, n],
            recv_sem=r_row_x.at[s - 1, core, i, n],
            device_id={"dp": to},
            device_id_type=MESH,
        )

    def row_x_arrived(s, c, i, half, n):
        first, many = pieces[half][n]
        return pltpu.make_async_remote_copy(
            src_ref=normed.at[dp, i, pl.ds(first, many)],
            dst_ref=rows_in.at[i, x_source(s) * CORES + c, pl.ds(first, many)],
            send_sem=s_row_x.at[s - 1, c, i, n],
            recv_sem=r_row_x.at[s - 1, c, i, n],
            device_id={"dp": mate},
            device_id_type=MESH,
        )

    def row_z(s, c, i, half, n):
        first, many = pieces[half][n]
        where = rows_in.at[i, x_source(s) * CORES + c, pl.ds(first, many)]
        return pltpu.make_async_remote_copy(
            src_ref=where,
            dst_ref=where,
            send_sem=s_row_z.at[s - 1, c, i, n],
            recv_sem=r_row_z.at[s - 1, c, i, n],
            device_id={"tensor": neighbour},
            device_id_type=MESH,
        )

    def part_copy(u, i, b):
        return pltpu.make_async_remote_copy(
            src_ref=stage.at[b],
            dst_ref=from_mate.at[u, i, b],
            send_sem=s_part.at[u, i, b],
            recv_sem=r_part.at[u, i, b],
            device_id={"dp": mate},
            device_id_type=MESH,
        )

    def sum_copy(s, i, b):
        return pltpu.make_async_remote_copy(
            src_ref=from_mate.at[s, i, b],
            dst_ref=x_in.at[s - 1, i, b],
            send_sem=s_sum.at[s - 1, i, b],
            recv_sem=r_sum.at[s - 1, i, b],
            device_id={"dp": x_peer(s) * CORES + core},
            device_id_type=MESH,
        )

    def map_copy(s, i):
        to = lax.rem(t + s, n_tensor)
        return pltpu.make_async_remote_copy(
            src_ref=made.at[i, pl.ds(to * s_here, s_here)],
            dst_ref=landed.at[s - 1, i],
            send_sem=s_map.at[s - 1, i],
            recv_sem=r_map.at[s - 1, i],
            device_id={"tensor": to},
            device_id_type=MESH,
        )

    def grad_copy(s, i):
        own = grads.at[i, dp]
        return pltpu.make_async_remote_copy(
            src_ref=own,
            dst_ref=own,
            send_sem=s_grad.at[s - 1, i],
            recv_sem=r_grad.at[s - 1, i],
            device_id={"dp": x_peer(s) * CORES + core},
            device_id_type=MESH,
        )

    def grad_mate(s, i):
        block = grads.at[i, x_source(s) * CORES + core]
        return pltpu.make_async_remote_copy(
            src_ref=block,
            dst_ref=block,
            send_sem=s_grad_mate.at[s, i],
            recv_sem=r_grad_mate.at[s, i],
            device_id={"dp": mate},
            device_id_type=MESH,
        )

    def greet():
        barrier = pltpu.get_barrier_semaphore()
        waits = 0
        for s in range(1, n_dp):
            pl.semaphore_signal(
                barrier, inc=1, device_id={"dp": lax.rem(dp + s, n_dp)}, device_id_type=MESH
            )
            waits += 1
        for s in range(1, n_tensor):
            pl.semaphore_signal(
                barrier, inc=1, device_id={"tensor": lax.rem(t + s, n_tensor)}, device_id_type=MESH
            )
            waits += 1
        pl.semaphore_wait(barrier, waits)

    def prepare(xraw, wraw, sraw):
        def w_copy(n):
            slot = lax.rem(n, 2)
            return pltpu.make_async_copy(
                w_ref.at[pl.ds(n * chunk, chunk)], wraw.at[slot], w_sem.at[slot]
            )

        def x_fetch(half):
            first = pieces[half][0][0]
            last = pieces[half][-1][0] + pieces[half][-1][1]
            many = min(last, tokens) - first
            return pltpu.make_async_copy(
                x_ref.at[pl.ds(first, many)], xraw.at[pl.ds(first, many)], x_sem.at[half]
            )

        sx_fetch = pltpu.make_async_copy(sx_ref, sraw.at[pl.ds(0, tokens)], sx_sem)
        sx_fetch.start()
        on_half(parity, lambda half: x_fetch(half).start())
        on_half(1 - parity, lambda half: x_fetch(half).start())
        w_copy(0).start()
        w_copy(1).start()
        xraw[tokens:pad] = jnp.zeros((pad - tokens,) + xraw.shape[1:], jnp.bfloat16)
        sraw[tokens:pad] = jnp.zeros((pad - tokens,) + sraw.shape[1:], jnp.bfloat16)
        for j in range(images):
            slot_rows[dp, j : j + 1, :] = jnp.full((1, 128), slots_ref[j], jnp.int32)
        greet()
        for s in range(1, n_dp):
            slot_copy(s).start()

        sx_fetch.wait()

        def student_rows(r, carry):
            spot = pl.ds(pl.multiple_of(r * 16, 16), 16)
            both = jnp.swapaxes(sraw[spot], 0, 1)
            for i in range(images):
                block = layer_norm(both[i], sgain_ref[...], sbias_ref[...]).astype(jnp.bfloat16)
                for q in range(share):
                    student[q, dp * images + i, spot, :] = block[:, q * s_depth : (q + 1) * s_depth]
            return carry

        lax.fori_loop(0, pad // 16, student_rows, 0)
        for s in range(1, n_x):
            stu_x(s).start()
        stu_mate(0).start()

        def norm_piece(first, many):
            def norm_rows(r, carry):
                spot = pl.multiple_of(first + r * 16, 16)
                both = jnp.swapaxes(xraw[pl.ds(spot, 16)], 0, 1)
                for i in range(images):
                    block = layer_norm(both[i], gain_ref[...], 0.0).astype(jnp.bfloat16)
                    for d in range(n_dp):
                        normed[d, i, pl.ds(spot, 16), :] = block[:, d * depth : (d + 1) * depth]
                return carry

            lax.fori_loop(0, many // 16, norm_rows, 0)

        def send_half(half):
            x_fetch(half).wait()
            for n in range(2):
                norm_piece(*pieces[half][n])
                for s in range(1, n_x):
                    for c in range(CORES):
                        row_x(s, c, 0, half, n).start()
            for i in range(1, images):
                for n in range(2):
                    for s in range(1, n_x):
                        for c in range(CORES):
                            row_x(s, c, i, half, n).start()

        def norm_half(half):
            x_fetch(half).wait()
            for n in range(2):
                norm_piece(*pieces[half][n])

        on_half(parity, send_half)
        on_half(1 - parity, norm_half)
        for i in range(images):
            row_mate(i).start()

        def split(n, carry):
            w_copy(n).wait()
            slot = lax.rem(n, 2)
            spot = pl.ds(pl.multiple_of(n * chunk, chunk), chunk)
            for b in range(blocks):
                both = jnp.swapaxes(wraw[slot, :, :, b * width : (b + 1) * width], 0, 1)
                wsplit[0, b, spot, :] = both[0]
                wsplit[1, b, spot, :] = both[1]

            @pl.when(n + 2 < w_chunks)
            def _():
                w_copy(n + 2).start()

            return carry

        lax.fori_loop(0, w_chunks, split, 0)

    pl.run_scoped(
        prepare,
        pltpu.VMEM((pad,) + x_ref.shape[1:], jnp.bfloat16),
        pltpu.VMEM((2, chunk) + w_ref.shape[1:], jnp.bfloat16),
        pltpu.VMEM((pad,) + sx_ref.shape[1:], jnp.bfloat16),
    )

    acc[...] = jnp.zeros_like(acc)

    def project(lhs, b):
        keys = jnp.dot(lhs[...], wsplit[1, b], preferred_element_type=jnp.float32)
        query = jnp.dot(lhs[:QROWS], wsplit[0, b], preferred_element_type=jnp.float32)
        return keys, query

    def to_mate(u, i, b, before, lhs):
        keys, query = project(lhs, b)
        if before is not None:
            part_copy(*before, b).wait_send()
        stage[b, :pad] = keys.astype(jnp.bfloat16)
        stage[b, pad:] = query.astype(jnp.bfloat16)
        part_copy(u, i, b).start()

    def own_chip(i, before):
        row_mate(i).wait_recv()

        def body(b, carry):
            to_mate(0, i, b, before, rows_in.at[i, mate])
            return carry

        lax.fori_loop(0, blocks, body, 0)

    def other_chip(s, i, before, start, stop):
        def body(b, carry):
            @pl.when(b < blocks)
            def _():
                away = x_peer(s) * CORES
                to_mate(s, i, b, before, rows_in.at[i, away + 1 - core])
                keys, query = project(rows_in.at[i, away + core], b)
                held[lax.rem(b, 2), :pad] = keys
                held[lax.rem(b, 2), pad:] = query

            @pl.when(b > 0)
            def _():
                j = b - 1
                part_copy(s, i, j).wait_recv()
                total = held[lax.rem(j, 2)] + from_mate[s, i, j].astype(jnp.float32)
                from_mate[s, i, j] = total.astype(jnp.bfloat16)
                sum_copy(s, i, j).start()

            return carry

        lax.fori_loop(start, stop, body, 0)

    def pass_on(i, n):
        def act(half):
            for s in range(1, n_x):
                for c in range(CORES):
                    row_x_arrived(s, c, i, half, n).wait_recv()
                    row_z(s, c, i, half, n).start()

        on_half(parity, act)

    def passed_on(i):
        def act(half):
            for n in range(2):
                for s in range(1, n_x):
                    for c in range(CORES):
                        row_z(s, c, i, half, n).wait_recv()

        on_half(1 - parity, act)

    before = None
    for i in range(images):
        pass_on(0, i) if i < 2 else None
        own_chip(i, before)
        before = (0, i)
    for n in range(images, 2):
        pass_on(0, n)
    for i in range(images):
        if i + 1 < images:
            pass_on(i + 1, 0)
        passed_on(i)
        for s in range(1, n_x):
            early = blocks // 2 if s == 1 else 0
            other_chip(s, i, before, 0, early)
            if s == 1 and i + 1 < images:
                pass_on(i + 1, 1)
            other_chip(s, i, before, early, blocks + 1)
            before = (s, i)
        if i == 0:
            for s in range(1, n_x):
                stu_x(s).wait_recv()
                for q in range(1, share):
                    stu_z(s, q).start()

    def attend_image(i):
        def attend(b, carry):
            keys, query = project(normed.at[dp, i], b)
            part_copy(0, i, b).wait_recv()
            keys += from_mate[0, i, b, :pad].astype(jnp.float32)
            query += from_mate[0, i, b, pad:].astype(jnp.float32)
            for s in range(1, n_x):
                sum_copy(s, i, b).wait_recv()
                keys += x_in[s - 1, i, b, :pad].astype(jnp.float32)
                query += x_in[s - 1, i, b, pad:].astype(jnp.float32)
            keys = keys.astype(jnp.bfloat16)
            query = (query * HD_T ** (-0.5)).astype(jnp.bfloat16)
            maps = []
            for h in range(width // HD_T):
                cols = slice(h * HD_T, (h + 1) * HD_T)
                scores = lax.dot_general(
                    keys[:, cols],
                    query[:, cols],
                    (((1,), (1,)), ((), ())),
                    preferred_element_type=jnp.float32,
                )
                one = key_softmax(scores, tokens)
                maps.append(one.astype(jnp.bfloat16).astype(jnp.float32))
            first = t * (blocks * (width // HD_T)) + b * (width // HD_T)
            for s in range(s_heads):
                total = acc[s]
                for h, one in enumerate(maps):
                    total += counts_ref[first + h, s].astype(jnp.float32) * one
                acc[s] = total
            return carry

        lax.fori_loop(0, blocks, attend, 0)

        def finish(s, carry):
            made[i, s] = (acc[s] / DIVISOR).astype(jnp.bfloat16)
            acc[s] = jnp.zeros(acc.shape[1:], jnp.float32)
            return carry

        lax.fori_loop(0, s_heads, finish, 0)
        for s in range(1, n_tensor):
            map_copy(s, i).start()

    def slot_of(image):
        found = jnp.int32(0)
        for d in range(n_dp):
            for j in range(images):
                here = jnp.where(slot_table[d, j, 0] == image, d * images + j, 0)
                found = jnp.maximum(found, here)
        return found

    left = lax.broadcasted_iota(jnp.int32, (pad, s_cols), 1) < HD_S

    def student_forward(i):
        slot = slot_of(dp * images + i)
        total = jnp.zeros((pad, s_here * s_cols), jnp.float32)
        for q in range(share):
            total += jnp.dot(
                student[q, slot],
                sw_ref[q * s_depth : (q + 1) * s_depth, :],
                preferred_element_type=jnp.float32,
            )
        for h in range(s_here):
            one = total[:, h * s_cols : (h + 1) * s_cols]
            one = jnp.where(left, one * HD_S ** (-0.5), one).astype(jnp.bfloat16)
            packed[i, h] = one
            keys, query, _ = apart(one)
            scores = lax.dot_general(
                keys, one[:QROWS], (((1,), (1,)), ((), ())), preferred_element_type=jnp.float32
            )
            probs[i, h] = key_softmax(scores, tokens)

    def apart(one):
        wide = one.astype(jnp.float32)
        turned = jnp.concatenate([wide[:, HD_S:], wide[:, :HD_S]], axis=1)
        keys = jnp.where(left, turned, 0.0).astype(jnp.bfloat16)
        query = jnp.where(left, 0.0, turned).astype(jnp.bfloat16)[:QROWS]
        return keys, query, turned

    def student_back(i):
        for s in range(1, n_tensor):
            map_copy(s, i).wait_recv()

        def head(h, carry):
            goal = made[i, t * s_here + h].astype(jnp.float32)
            for s in range(1, n_tensor):
                goal += landed[s - 1, i, h].astype(jnp.float32)
            goal = goal.astype(jnp.bfloat16).astype(jnp.float32)
            slope = probs[i, h] * jnp.sum(goal, axis=0, keepdims=True) - goal
            slope = slope.astype(jnp.bfloat16)
            keys, query, _ = apart(packed[i, h])
            for_query = (
                lax.dot_general(
                    slope, keys, (((0,), (0,)), ((), ())), preferred_element_type=jnp.float32
                )
                * HD_S ** (-0.5)
            )
            for_keys = jnp.dot(slope, query, preferred_element_type=jnp.float32)
            grads[i, dp, h, :QROWS] = (for_query + for_keys[:QROWS]).astype(jnp.bfloat16)
            grads[i, dp, h, QROWS:] = for_keys[QROWS:].astype(jnp.bfloat16)
            return carry

        lax.fori_loop(0, s_here, head, 0)
        for s in range(1, n_x):
            grad_copy(s, i).start()
        grad_mate(0, i).start()

    def add_images(i, source):
        slot = slot_of(source * images + i)
        right = jnp.concatenate([grads[i, source, h] for h in range(s_here)], axis=1)
        for q in range(share):
            rows = pl.ds(q * s_depth, s_depth)
            out_ref[rows, :] += lax.dot_general(
                student[q, slot], right, (((0,), (0,)), ((), ())), preferred_element_type=jnp.float32
            )

    def gather_grads(i):
        add_images(i, dp)
        grad_mate(0, i).wait_recv()
        add_images(i, mate)
        for s in range(1, n_x):
            grad_copy(s, i).wait_recv()
            grad_mate(s, i).start()
            add_images(i, x_source(s) * CORES + core)
        for s in range(1, n_x):
            grad_mate(s, i).wait_recv()
            add_images(i, x_source(s) * CORES + 1 - core)

    attend_image(0)
    for s in range(1, n_dp):
        slot_copy(s).wait_recv()
    table = pltpu.make_async_copy(slot_rows, slot_table, slot_sem)
    table.start()
    for s in range(1, n_x):
        for q in range(1, share):
            stu_z(s, q).wait_recv()
        stu_mate(s).start()
    table.wait()
    for s in range(n_x):
        stu_mate(s).wait_recv()
    for i in range(images):
        student_forward(i)
    out_ref[...] = jnp.zeros_like(out_ref)
    for i in range(1, images):
        attend_image(i)
    for i in range(images):
        student_back(i)
        gather_grads(i)

    def drain_half(half):
        for i in range(images):
            for n in range(2):
                for s in range(1, n_x):
                    for c in range(CORES):
                        row_x(s, c, i, half, n).wait_send()
                        row_z(s, c, i, half, n).wait_send()

    on_half(parity, drain_half)
    for s in range(1, n_dp):
        slot_copy(s).wait_send()
    for s in range(n_x):
        stu_mate(s).wait_send()
    for s in range(1, n_x):
        stu_x(s).wait_send()
        for q in range(1, share):
            stu_z(s, q).wait_send()
    for i in range(images):
        row_mate(i).wait_send()
        for s in range(1, n_tensor):
            map_copy(s, i).wait_send()
        for s in range(1, n_x):
            grad_copy(s, i).wait_send()
        for s in range(n_x):
            grad_mate(s, i).wait_send()

        def drain(b, carry):
            if before == (before[0], i):
                part_copy(before[0], i, b).wait_send()
            for s in range(1, n_x):
                sum_copy(s, i, b).wait_send()
            return carry

        lax.fori_loop(0, blocks, drain, 0)


def on_device(
    mesh_sizes,
    teacher_input,
    teacher_gain,
    teacher_weight,
    head_counts,
    assignment,
    student_input,
    student_gain,
    student_bias,
    student_weight,
):
    n_dp, n_tensor = mesh_sizes
    images, tokens, width = teacher_input.shape
    rows, _, width_here = teacher_weight.shape
    s_width, s_width_here = student_weight.shape
    heads_here = width_here // HD_T
    s_heads = head_counts.shape[1]
    s_here = s_heads // n_tensor
    pad = rounded_up(tokens, 16)
    n_x = n_dp // CORES
    others = max(n_x - 1, 1)
    per_block = 2 if heads_here % 2 == 0 else 1
    blocks = heads_here // per_block
    block_width = per_block * HD_T
    chunk = 192
    share = min(SHARE, n_tensor)
    both = pad + QROWS
    sizes = (n_dp, n_tensor, s_heads, images, tokens, pad, blocks, chunk)
    dma = pltpu.SemaphoreType.DMA
    half = jnp.bfloat16
    in_vmem = pl.BlockSpec(memory_space=pltpu.VMEM)
    in_smem = pl.BlockSpec(memory_space=pltpu.SMEM)
    anywhere = pl.BlockSpec(memory_space=pl.ANY)
    return pl.pallas_call(
        functools.partial(distill_kernel, sizes),
        out_shape=jax.ShapeDtypeStruct((s_width, s_width_here), jnp.float32),
        in_specs=[
            in_smem,
            in_smem,
            anywhere,
            in_vmem,
            anywhere,
            anywhere,
            in_vmem,
            in_vmem,
            in_vmem,
        ],
        out_specs=in_vmem,
        scratch_shapes=[
            pltpu.VMEM((2, blocks, rows, block_width), half),
            pltpu.VMEM((n_dp, images, pad, rows), half),
            pltpu.VMEM((images, n_dp, pad, rows), half),
            pltpu.VMEM((blocks, both, block_width), half),
            pltpu.VMEM((n_x, images, blocks, both, block_width), half),
            pltpu.VMEM((others, images, blocks, both, block_width), half),
            pltpu.VMEM((2, both, block_width), jnp.float32),
            pltpu.VMEM((s_heads, pad, QROWS), jnp.float32),
            pltpu.VMEM((images, s_heads, pad, QROWS), half),
            pltpu.VMEM((n_tensor - 1, images, s_here, pad, QROWS), half),
            pltpu.VMEM((share, n_dp * images, pad, s_width // share), half),
            pltpu.VMEM((images, s_here, pad, 2 * HD_S), half),
            pltpu.VMEM((images, s_here, pad, QROWS), jnp.float32),
            pltpu.VMEM((images, n_dp, s_here, pad, 2 * HD_S), half),
            pltpu.VMEM((n_dp, 8, 128), jnp.int32),
            pltpu.SMEM((n_dp, 8, 128), jnp.int32),
            dma((2,)),
            dma((2,)),
            dma,
            dma,
            dma((images,)),
            dma((images,)),
            dma((others, CORES, images, 2)),
            dma((others, CORES, images, 2)),
            dma((others, CORES, images, 2)),
            dma((others, CORES, images, 2)),
            dma((n_x, images, blocks)),
            dma((n_x, images, blocks)),
            dma((others, images, blocks)),
            dma((others, images, blocks)),
            dma((n_tensor - 1, images)),
            dma((n_tensor - 1, images)),
            dma((others, images)),
            dma((others, images)),
            dma((n_x, images)),
            dma((n_x, images)),
            dma((n_dp - 1,)),
            dma((n_dp - 1,)),
            dma((n_x,)),
            dma((n_x,)),
            dma((others,)),
            dma((others,)),
            dma((others, share - 1)),
            dma((others, share - 1)),
        ],
        compiler_params=pltpu.CompilerParams(
            collective_id=0, has_side_effects=True, vmem_limit_bytes=67043328
        ),
    )(
        head_counts,
        assignment,
        jnp.transpose(teacher_input, (1, 0, 2)),
        teacher_gain.reshape(1, width),
        teacher_weight,
        jnp.transpose(student_input, (1, 0, 2)),
        student_gain.reshape(1, s_width),
        student_bias.reshape(1, s_width),
        student_weight,
    )


def solution(mesh):
    placed = (
        P(("group", "dp"), None, None),
        P(),
        P("dp", None, "tensor"),
        P(),
        P(("group", "dp")),
        P(("group", "dp"), None, None),
        P(),
        P(),
        P(None, "tensor"),
    )
    mesh_sizes = (mesh.shape["dp"], mesh.shape["tensor"])
    return jax.shard_map(
        functools.partial(on_device, mesh_sizes),
        mesh=mesh,
        in_specs=placed,
        out_specs=P("group", "tensor"),
        check_vma=False,
    )
```

```python
import functools

import jax
import jax.numpy as jnp
from jax import lax
from jax.experimental import pallas as pl
from jax.experimental.pallas import tpu as pltpu
from jax.sharding import PartitionSpec as P

HD_T = 128
HD_S = 64
QROWS = 128
DIVISOR = 72
CORES = 2
SHARE = 2
MESH = pl.DeviceIdType.MESH


def layer_norm(values, gain, shift):
    wide = values.astype(jnp.float32)
    center = wide - jnp.mean(wide, axis=-1, keepdims=True)
    spread = jnp.mean(center * center, axis=-1, keepdims=True)
    return center * lax.rsqrt(spread + 1e-06) * gain + shift


def rounded_up(value, unit):
    return -(-value // unit) * unit


def key_softmax(scores, tokens):
    spot = lax.broadcasted_iota(jnp.int32, scores.shape, 0)
    scores = jnp.where(spot < tokens, scores, -jnp.inf)
    power = jnp.exp(scores - jnp.max(scores, axis=0, keepdims=True))
    return power / jnp.sum(power, axis=0, keepdims=True)


def distill_by_images(
    sizes,
    counts_ref,
    slots_ref,
    x_ref,
    gain_ref,
    w_ref,
    sx_ref,
    sgain_ref,
    sbias_ref,
    sw_ref,
    out_ref,
    wsplit,
    normed,
    rows_in,
    stage,
    from_mate,
    x_in,
    held,
    acc,
    made,
    landed,
    student,
    packed,
    probs,
    grads,
    slot_rows,
    slot_table,
    w_sem,
    x_sem,
    sx_sem,
    slot_sem,
    s_row_mate,
    r_row_mate,
    s_row_x,
    r_row_x,
    s_row_z,
    r_row_z,
    s_part,
    r_part,
    s_sum,
    r_sum,
    s_map,
    r_map,
    s_grad,
    r_grad,
    s_grad_mate,
    r_grad_mate,
    s_slot,
    r_slot,
    s_stu_mate,
    r_stu_mate,
    s_stu_x,
    r_stu_x,
    s_stu_z,
    r_stu_z,
):
    n_dp, n_tensor, s_heads, images, tokens, pad, blocks, chunk = sizes
    n_x = n_dp // CORES
    depth = w_ref.shape[0]
    width = wsplit.shape[3]
    s_here = s_heads // n_tensor
    s_cols = 2 * HD_S
    share, s_depth = student.shape[0], student.shape[3]
    w_chunks = depth // chunk

    dp = lax.axis_index("dp")
    t = lax.axis_index("tensor")
    x = dp // CORES
    core = lax.rem(dp, CORES)
    mate = x * CORES + (1 - core)
    parity = lax.rem(t, 2)
    neighbour = t + 1 - 2 * parity
    quarter = lax.rem(t, share)

    def x_peer(s):
        return lax.rem(x + s, n_x)

    def x_source(s):
        return lax.rem(x + n_x - s, n_x)

    low = QROWS
    cut = (pad - low) // 32 * 16
    pieces = (
        ((0, low // 2), (low // 2, low // 2)),
        ((low, cut), (low + cut, pad - low - cut)),
    )

    def on_half(which, act):
        for half in range(2):

            @pl.when(which == half)
            def _():
                act(half)

    def slot_copy(s):
        return pltpu.make_async_remote_copy(
            src_ref=slot_rows.at[dp],
            dst_ref=slot_rows.at[dp],
            send_sem=s_slot.at[s - 1],
            recv_sem=r_slot.at[s - 1],
            device_id={"dp": lax.rem(dp + s, n_dp)},
            device_id_type=MESH,
        )

    def own_slots(source):
        return pl.ds(source * images, images)

    def stu_mate(s):
        where = student.at[:, own_slots(x_source(s) * CORES + core)]
        return pltpu.make_async_remote_copy(
            src_ref=where,
            dst_ref=where,
            send_sem=s_stu_mate.at[s],
            recv_sem=r_stu_mate.at[s],
            device_id={"dp": mate},
            device_id_type=MESH,
        )

    def stu_x(s):
        where = student.at[quarter, own_slots(dp)]
        return pltpu.make_async_remote_copy(
            src_ref=where,
            dst_ref=where,
            send_sem=s_stu_x.at[s - 1],
            recv_sem=r_stu_x.at[s - 1],
            device_id={"dp": x_peer(s) * CORES + core},
            device_id_type=MESH,
        )

    def stu_z(s, q):
        where = student.at[quarter, own_slots(x_source(s) * CORES + core)]
        return pltpu.make_async_remote_copy(
            src_ref=where,
            dst_ref=where,
            send_sem=s_stu_z.at[s - 1, q - 1],
            recv_sem=r_stu_z.at[s - 1, q - 1],
            device_id={"tensor": t - quarter + lax.rem(quarter + q, share)},
            device_id_type=MESH,
        )

    def row_mate(i):
        return pltpu.make_async_remote_copy(
            src_ref=normed.at[mate, i],
            dst_ref=rows_in.at[i, dp],
            send_sem=s_row_mate.at[i],
            recv_sem=r_row_mate.at[i],
            device_id={"dp": mate},
            device_id_type=MESH,
        )

    def row_x(s, c, i, half, n):
        first, many = pieces[half][n]
        to = x_peer(s) * CORES + c
        return pltpu.make_async_remote_copy(
            src_ref=normed.at[to, i, pl.ds(first, many)],
            dst_ref=rows_in.at[i, dp, pl.ds(first, many)],
            send_sem=s_row_x.at[s - 1, c, i, n],
            recv_sem=r_row_x.at[s - 1, core, i, n],
            device_id={"dp": to},
            device_id_type=MESH,
        )

    def row_x_arrived(s, c, i, half, n):
        first, many = pieces[half][n]
        return pltpu.make_async_remote_copy(
            src_ref=normed.at[dp, i, pl.ds(first, many)],
            dst_ref=rows_in.at[i, x_source(s) * CORES + c, pl.ds(first, many)],
            send_sem=s_row_x.at[s - 1, c, i, n],
            recv_sem=r_row_x.at[s - 1, c, i, n],
            device_id={"dp": mate},
            device_id_type=MESH,
        )

    def row_z(s, c, i, half, n):
        first, many = pieces[half][n]
        where = rows_in.at[i, x_source(s) * CORES + c, pl.ds(first, many)]
        return pltpu.make_async_remote_copy(
            src_ref=where,
            dst_ref=where,
            send_sem=s_row_z.at[s - 1, c, i, n],
            recv_sem=r_row_z.at[s - 1, c, i, n],
            device_id={"tensor": neighbour},
            device_id_type=MESH,
        )

    def part_copy(u, i, b):
        return pltpu.make_async_remote_copy(
            src_ref=stage.at[b],
            dst_ref=from_mate.at[u, i, b],
            send_sem=s_part.at[u, i, b],
            recv_sem=r_part.at[u, i, b],
            device_id={"dp": mate},
            device_id_type=MESH,
        )

    def sum_copy(s, i, b):
        return pltpu.make_async_remote_copy(
            src_ref=from_mate.at[s, i, b],
            dst_ref=x_in.at[s - 1, i, b],
            send_sem=s_sum.at[s - 1, i, b],
            recv_sem=r_sum.at[s - 1, i, b],
            device_id={"dp": x_peer(s) * CORES + core},
            device_id_type=MESH,
        )

    def map_copy(s, i):
        to = lax.rem(t + s, n_tensor)
        return pltpu.make_async_remote_copy(
            src_ref=made.at[i, pl.ds(to * s_here, s_here)],
            dst_ref=landed.at[s - 1, i],
            send_sem=s_map.at[s - 1, i],
            recv_sem=r_map.at[s - 1, i],
            device_id={"tensor": to},
            device_id_type=MESH,
        )

    def grad_copy(s, i):
        own = grads.at[i, dp]
        return pltpu.make_async_remote_copy(
            src_ref=own,
            dst_ref=own,
            send_sem=s_grad.at[s - 1, i],
            recv_sem=r_grad.at[s - 1, i],
            device_id={"dp": x_peer(s) * CORES + core},
            device_id_type=MESH,
        )

    def grad_mate(s, i):
        block = grads.at[i, x_source(s) * CORES + core]
        return pltpu.make_async_remote_copy(
            src_ref=block,
            dst_ref=block,
            send_sem=s_grad_mate.at[s, i],
            recv_sem=r_grad_mate.at[s, i],
            device_id={"dp": mate},
            device_id_type=MESH,
        )

    def greet():
        barrier = pltpu.get_barrier_semaphore()
        waits = 0
        for s in range(1, n_dp):
            pl.semaphore_signal(
                barrier, inc=1, device_id={"dp": lax.rem(dp + s, n_dp)}, device_id_type=MESH
            )
            waits += 1
        for s in range(1, n_tensor):
            pl.semaphore_signal(
                barrier, inc=1, device_id={"tensor": lax.rem(t + s, n_tensor)}, device_id_type=MESH
            )
            waits += 1
        pl.semaphore_wait(barrier, waits)

    def prepare(xraw, wraw, sraw):
        def w_copy(n):
            slot = lax.rem(n, 2)
            return pltpu.make_async_copy(
                w_ref.at[pl.ds(n * chunk, chunk)], wraw.at[slot], w_sem.at[slot]
            )

        def x_fetch(half):
            first = pieces[half][0][0]
            last = pieces[half][-1][0] + pieces[half][-1][1]
            many = min(last, tokens) - first
            return pltpu.make_async_copy(
                x_ref.at[pl.ds(first, many)], xraw.at[pl.ds(first, many)], x_sem.at[half]
            )

        sx_fetch = pltpu.make_async_copy(sx_ref, sraw.at[pl.ds(0, tokens)], sx_sem)
        sx_fetch.start()
        on_half(parity, lambda half: x_fetch(half).start())
        on_half(1 - parity, lambda half: x_fetch(half).start())
        w_copy(0).start()
        w_copy(1).start()
        xraw[tokens:pad] = jnp.zeros((pad - tokens,) + xraw.shape[1:], jnp.bfloat16)
        sraw[tokens:pad] = jnp.zeros((pad - tokens,) + sraw.shape[1:], jnp.bfloat16)
        for j in range(images):
            slot_rows[dp, j : j + 1, :] = jnp.full((1, 128), slots_ref[j], jnp.int32)
        greet()
        for s in range(1, n_dp):
            slot_copy(s).start()

        sx_fetch.wait()

        def student_rows(r, carry):
            spot = pl.ds(pl.multiple_of(r * 16, 16), 16)
            both = jnp.swapaxes(sraw[spot], 0, 1)
            for i in range(images):
                block = layer_norm(both[i], sgain_ref[...], sbias_ref[...]).astype(jnp.bfloat16)
                for q in range(share):
                    student[q, dp * images + i, spot, :] = block[:, q * s_depth : (q + 1) * s_depth]
            return carry

        lax.fori_loop(0, pad // 16, student_rows, 0)
        for s in range(1, n_x):
            stu_x(s).start()
        stu_mate(0).start()

        def norm_piece(first, many):
            def norm_rows(r, carry):
                spot = pl.multiple_of(first + r * 16, 16)
                both = jnp.swapaxes(xraw[pl.ds(spot, 16)], 0, 1)
                for i in range(images):
                    block = layer_norm(both[i], gain_ref[...], 0.0).astype(jnp.bfloat16)
                    for d in range(n_dp):
                        normed[d, i, pl.ds(spot, 16), :] = block[:, d * depth : (d + 1) * depth]
                return carry

            lax.fori_loop(0, many // 16, norm_rows, 0)

        def send_half(half):
            x_fetch(half).wait()
            for n in range(2):
                norm_piece(*pieces[half][n])
                for s in range(1, n_x):
                    for c in range(CORES):
                        row_x(s, c, 0, half, n).start()
            for i in range(1, images):
                for n in range(2):
                    for s in range(1, n_x):
                        for c in range(CORES):
                            row_x(s, c, i, half, n).start()

        def norm_half(half):
            x_fetch(half).wait()
            for n in range(2):
                norm_piece(*pieces[half][n])

        on_half(parity, send_half)
        on_half(1 - parity, norm_half)
        for i in range(images):
            row_mate(i).start()

        def split(n, carry):
            w_copy(n).wait()
            slot = lax.rem(n, 2)
            spot = pl.ds(pl.multiple_of(n * chunk, chunk), chunk)
            for b in range(blocks):
                both = jnp.swapaxes(wraw[slot, :, :, b * width : (b + 1) * width], 0, 1)
                wsplit[0, b, spot, :] = both[0]
                wsplit[1, b, spot, :] = both[1]

            @pl.when(n + 2 < w_chunks)
            def _():
                w_copy(n + 2).start()

            return carry

        lax.fori_loop(0, w_chunks, split, 0)

    pl.run_scoped(
        prepare,
        pltpu.VMEM((pad,) + x_ref.shape[1:], jnp.bfloat16),
        pltpu.VMEM((2, chunk) + w_ref.shape[1:], jnp.bfloat16),
        pltpu.VMEM((pad,) + sx_ref.shape[1:], jnp.bfloat16),
    )

    acc[...] = jnp.zeros_like(acc)

    def project(lhs, b):
        keys = jnp.dot(lhs[...], wsplit[1, b], preferred_element_type=jnp.float32)
        query = jnp.dot(lhs[:QROWS], wsplit[0, b], preferred_element_type=jnp.float32)
        return keys, query

    def to_mate(u, i, b, before, lhs):
        keys, query = project(lhs, b)
        if before is not None:
            part_copy(*before, b).wait_send()
        stage[b, :pad] = keys.astype(jnp.bfloat16)
        stage[b, pad:] = query.astype(jnp.bfloat16)
        part_copy(u, i, b).start()

    def own_chip(i, before):
        row_mate(i).wait_recv()

        def body(b, carry):
            to_mate(0, i, b, before, rows_in.at[i, mate])
            return carry

        lax.fori_loop(0, blocks, body, 0)

    def other_chip(s, i, before, start, stop):
        def body(b, carry):
            @pl.when(b < blocks)
            def _():
                away = x_peer(s) * CORES
                to_mate(s, i, b, before, rows_in.at[i, away + 1 - core])
                keys, query = project(rows_in.at[i, away + core], b)
                held[lax.rem(b, 2), :pad] = keys
                held[lax.rem(b, 2), pad:] = query

            @pl.when(b > 0)
            def _():
                j = b - 1
                part_copy(s, i, j).wait_recv()
                total = held[lax.rem(j, 2)] + from_mate[s, i, j].astype(jnp.float32)
                from_mate[s, i, j] = total.astype(jnp.bfloat16)
                sum_copy(s, i, j).start()

            return carry

        lax.fori_loop(start, stop, body, 0)

    def pass_on(i, n):
        def act(half):
            for s in range(1, n_x):
                for c in range(CORES):
                    row_x_arrived(s, c, i, half, n).wait_recv()
                    row_z(s, c, i, half, n).start()

        on_half(parity, act)

    def passed_on(i):
        def act(half):
            for n in range(2):
                for s in range(1, n_x):
                    for c in range(CORES):
                        row_z(s, c, i, half, n).wait_recv()

        on_half(1 - parity, act)

    before = None
    for i in range(images):
        pass_on(0, i) if i < 2 else None
        own_chip(i, before)
        before = (0, i)
    for n in range(images, 2):
        pass_on(0, n)
    for i in range(images):
        if i + 1 < images:
            pass_on(i + 1, 0)
        passed_on(i)
        for s in range(1, n_x):
            early = blocks // 2 if s == 1 else 0
            other_chip(s, i, before, 0, early)
            if s == 1 and i + 1 < images:
                pass_on(i + 1, 1)
            other_chip(s, i, before, early, blocks + 1)
            before = (s, i)
        if i == 0:
            for s in range(1, n_x):
                stu_x(s).wait_recv()
                for q in range(1, share):
                    stu_z(s, q).start()

    def attend_image(i):
        def attend(b, carry):
            keys, query = project(normed.at[dp, i], b)
            part_copy(0, i, b).wait_recv()
            keys += from_mate[0, i, b, :pad].astype(jnp.float32)
            query += from_mate[0, i, b, pad:].astype(jnp.float32)
            for s in range(1, n_x):
                sum_copy(s, i, b).wait_recv()
                keys += x_in[s - 1, i, b, :pad].astype(jnp.float32)
                query += x_in[s - 1, i, b, pad:].astype(jnp.float32)
            keys = keys.astype(jnp.bfloat16)
            query = (query * HD_T ** (-0.5)).astype(jnp.bfloat16)
            maps = []
            for h in range(width // HD_T):
                cols = slice(h * HD_T, (h + 1) * HD_T)
                scores = lax.dot_general(
                    keys[:, cols],
                    query[:, cols],
                    (((1,), (1,)), ((), ())),
                    preferred_element_type=jnp.float32,
                )
                one = key_softmax(scores, tokens)
                maps.append(one.astype(jnp.bfloat16).astype(jnp.float32))
            first = t * (blocks * (width // HD_T)) + b * (width // HD_T)
            for s in range(s_heads):
                total = acc[s]
                for h, one in enumerate(maps):
                    total += counts_ref[s, first + h].astype(jnp.float32) * one
                acc[s] = total
            return carry

        lax.fori_loop(0, blocks, attend, 0)

        def finish(s, carry):
            made[i, s] = (acc[s] / DIVISOR).astype(jnp.bfloat16)
            acc[s] = jnp.zeros(acc.shape[1:], jnp.float32)
            return carry

        lax.fori_loop(0, s_heads, finish, 0)
        for s in range(1, n_tensor):
            map_copy(s, i).start()

    def slot_of(image):
        found = jnp.int32(0)
        for d in range(n_dp):
            for j in range(images):
                here = jnp.where(slot_table[d, j, 0] == image, d * images + j, 0)
                found = jnp.maximum(found, here)
        return found

    left = lax.broadcasted_iota(jnp.int32, (pad, s_cols), 1) < HD_S

    def student_forward(i):
        slot = slot_of(dp * images + i)
        total = jnp.zeros((pad, s_here * s_cols), jnp.float32)
        for q in range(share):
            total += jnp.dot(
                student[q, slot],
                sw_ref[q * s_depth : (q + 1) * s_depth, :],
                preferred_element_type=jnp.float32,
            )
        for h in range(s_here):
            one = total[:, h * s_cols : (h + 1) * s_cols]
            one = jnp.where(left, one * HD_S ** (-0.5), one).astype(jnp.bfloat16)
            packed[i, h] = one
            keys, query, _ = apart(one)
            scores = lax.dot_general(
                keys, one[:QROWS], (((1,), (1,)), ((), ())), preferred_element_type=jnp.float32
            )
            probs[i, h] = key_softmax(scores, tokens)

    def apart(one):
        wide = one.astype(jnp.float32)
        turned = jnp.concatenate([wide[:, HD_S:], wide[:, :HD_S]], axis=1)
        keys = jnp.where(left, turned, 0.0).astype(jnp.bfloat16)
        query = jnp.where(left, 0.0, turned).astype(jnp.bfloat16)[:QROWS]
        return keys, query, turned

    def student_back(i):
        for s in range(1, n_tensor):
            map_copy(s, i).wait_recv()

        def head(h, carry):
            goal = made[i, t * s_here + h].astype(jnp.float32)
            for s in range(1, n_tensor):
                goal += landed[s - 1, i, h].astype(jnp.float32)
            goal = goal.astype(jnp.bfloat16).astype(jnp.float32)
            slope = probs[i, h] * jnp.sum(goal, axis=0, keepdims=True) - goal
            slope = slope.astype(jnp.bfloat16)
            keys, query, _ = apart(packed[i, h])
            for_query = (
                lax.dot_general(
                    slope, keys, (((0,), (0,)), ((), ())), preferred_element_type=jnp.float32
                )
                * HD_S ** (-0.5)
            )
            for_keys = jnp.dot(slope, query, preferred_element_type=jnp.float32)
            grads[i, dp, h, :QROWS] = (for_query + for_keys[:QROWS]).astype(jnp.bfloat16)
            grads[i, dp, h, QROWS:] = for_keys[QROWS:].astype(jnp.bfloat16)
            return carry

        lax.fori_loop(0, s_here, head, 0)
        for s in range(1, n_x):
            grad_copy(s, i).start()
        grad_mate(0, i).start()

    def add_images(i, source):
        slot = slot_of(source * images + i)
        right = jnp.concatenate([grads[i, source, h] for h in range(s_here)], axis=1)
        for q in range(share):
            rows = pl.ds(q * s_depth, s_depth)
            out_ref[rows, :] += lax.dot_general(
                student[q, slot], right, (((0,), (0,)), ((), ())), preferred_element_type=jnp.float32
            )

    def gather_grads(i):
        add_images(i, dp)
        grad_mate(0, i).wait_recv()
        add_images(i, mate)
        for s in range(1, n_x):
            grad_copy(s, i).wait_recv()
            grad_mate(s, i).start()
            add_images(i, x_source(s) * CORES + core)
        for s in range(1, n_x):
            grad_mate(s, i).wait_recv()
            add_images(i, x_source(s) * CORES + 1 - core)

    attend_image(0)
    for s in range(1, n_dp):
        slot_copy(s).wait_recv()
    table = pltpu.make_async_copy(slot_rows, slot_table, slot_sem)
    table.start()
    for s in range(1, n_x):
        for q in range(1, share):
            stu_z(s, q).wait_recv()
        stu_mate(s).start()
    table.wait()
    for s in range(n_x):
        stu_mate(s).wait_recv()
    for i in range(images):
        student_forward(i)
    out_ref[...] = jnp.zeros_like(out_ref)
    for i in range(1, images):
        attend_image(i)
    for i in range(images):
        student_back(i)
        gather_grads(i)

    def drain_half(half):
        for i in range(images):
            for n in range(2):
                for s in range(1, n_x):
                    for c in range(CORES):
                        row_x(s, c, i, half, n).wait_send()
                        row_z(s, c, i, half, n).wait_send()

    on_half(parity, drain_half)
    for s in range(1, n_dp):
        slot_copy(s).wait_send()
    for s in range(n_x):
        stu_mate(s).wait_send()
    for s in range(1, n_x):
        stu_x(s).wait_send()
        for q in range(1, share):
            stu_z(s, q).wait_send()
    for i in range(images):
        row_mate(i).wait_send()
        for s in range(1, n_tensor):
            map_copy(s, i).wait_send()
        for s in range(1, n_x):
            grad_copy(s, i).wait_send()
        for s in range(n_x):
            grad_mate(s, i).wait_send()

        def drain(b, carry):
            if before == (before[0], i):
                part_copy(before[0], i, b).wait_send()
            for s in range(1, n_x):
                sum_copy(s, i, b).wait_send()
            return carry

        lax.fori_loop(0, blocks, drain, 0)


def distill_by_heads(
    sizes,
    counts_ref,
    slots_ref,
    x_ref,
    gain_ref,
    w_ref,
    sx_ref,
    sgain_ref,
    sbias_ref,
    sw_ref,
    out_ref,
    wsplit,
    normed,
    rows_in,
    stage,
    from_mate,
    x_in,
    held,
    acc,
    made,
    landed,
    student,
    packed,
    probs,
    grads,
    slot_rows,
    slot_table,
    w_sem,
    x_sem,
    sx_sem,
    slot_sem,
    own_sem,
    s_row_mate,
    r_row_mate,
    s_row_x,
    r_row_x,
    s_row_z,
    r_row_z,
    s_part,
    r_part,
    s_sum,
    r_sum,
    s_map,
    r_map,
    s_grad,
    r_grad,
    s_grad_mate,
    r_grad_mate,
    fold_out,
    fold_in,
    s_fold,
    r_fold,
    s_slot,
    r_slot,
    s_stu_mate,
    r_stu_mate,
    s_stu_x,
    r_stu_x,
    s_stu_z,
    r_stu_z,
):
    n_dp, n_tensor, s_heads, images, tokens, pad, blocks, chunk = sizes
    n_x = n_dp // CORES
    depth = w_ref.shape[0]
    width = wsplit.shape[3]
    s_here = s_heads // n_tensor
    s_half = s_here // CORES
    mine = blocks // CORES
    everyone = images * CORES
    s_cols = 2 * HD_S
    share, s_depth = student.shape[0], student.shape[3]
    w_chunks = depth // chunk

    dp = lax.axis_index("dp")
    t = lax.axis_index("tensor")
    x = dp // CORES
    core = lax.rem(dp, CORES)
    mate = x * CORES + (1 - core)
    parity = lax.rem(t, 2)
    neighbour = t + 1 - 2 * parity
    quarter = lax.rem(t, share)

    def x_peer(s):
        return lax.rem(x + s, n_x)

    def x_source(s):
        return lax.rem(x + n_x - s, n_x)

    low = QROWS
    cut = (pad - low) // 32 * 16
    pieces = (
        ((0, low // 2), (low // 2, low // 2)),
        ((low, cut), (low + cut, pad - low - cut)),
    )

    def on_half(which, act):
        for half in range(2):

            @pl.when(which == half)
            def _():
                act(half)

    def slot_copy(s):
        return pltpu.make_async_remote_copy(
            src_ref=slot_rows.at[dp],
            dst_ref=slot_rows.at[dp],
            send_sem=s_slot.at[s - 1],
            recv_sem=r_slot.at[s - 1],
            device_id={"dp": lax.rem(dp + s, n_dp)},
            device_id_type=MESH,
        )

    def own_slots(source):
        return pl.ds(source * images, images)

    def stu_mate(s):
        where = student.at[:, own_slots(x_source(s) * CORES + core)]
        return pltpu.make_async_remote_copy(
            src_ref=where,
            dst_ref=where,
            send_sem=s_stu_mate.at[s],
            recv_sem=r_stu_mate.at[s],
            device_id={"dp": mate},
            device_id_type=MESH,
        )

    def stu_x(s):
        where = student.at[quarter, own_slots(dp)]
        return pltpu.make_async_remote_copy(
            src_ref=where,
            dst_ref=where,
            send_sem=s_stu_x.at[s - 1],
            recv_sem=r_stu_x.at[s - 1],
            device_id={"dp": x_peer(s) * CORES + core},
            device_id_type=MESH,
        )

    def stu_z(s, q):
        where = student.at[quarter, own_slots(x_source(s) * CORES + core)]
        return pltpu.make_async_remote_copy(
            src_ref=where,
            dst_ref=where,
            send_sem=s_stu_z.at[s - 1, q - 1],
            recv_sem=r_stu_z.at[s - 1, q - 1],
            device_id={"tensor": t - quarter + lax.rem(quarter + q, share)},
            device_id_type=MESH,
        )

    def row_mate(i):
        return pltpu.make_async_remote_copy(
            src_ref=normed.at[mate, i],
            dst_ref=rows_in.at[i, dp],
            send_sem=s_row_mate.at[i],
            recv_sem=r_row_mate.at[i],
            device_id={"dp": mate},
            device_id_type=MESH,
        )

    def row_own(i):
        return pltpu.make_async_copy(normed.at[dp, i], rows_in.at[i, dp], own_sem.at[i])

    def row_x(s, c, i, half, n):
        first, many = pieces[half][n]
        to = x_peer(s) * CORES + c
        return pltpu.make_async_remote_copy(
            src_ref=normed.at[to, i, pl.ds(first, many)],
            dst_ref=rows_in.at[i, dp, pl.ds(first, many)],
            send_sem=s_row_x.at[s - 1, c, i, n],
            recv_sem=r_row_x.at[s - 1, core, i, n],
            device_id={"dp": to},
            device_id_type=MESH,
        )

    def row_x_arrived(s, c, i, half, n):
        first, many = pieces[half][n]
        return pltpu.make_async_remote_copy(
            src_ref=normed.at[dp, i, pl.ds(first, many)],
            dst_ref=rows_in.at[i, x_source(s) * CORES + c, pl.ds(first, many)],
            send_sem=s_row_x.at[s - 1, c, i, n],
            recv_sem=r_row_x.at[s - 1, c, i, n],
            device_id={"dp": mate},
            device_id_type=MESH,
        )

    def row_z(s, c, i, half, n):
        first, many = pieces[half][n]
        where = rows_in.at[i, x_source(s) * CORES + c, pl.ds(first, many)]
        return pltpu.make_async_remote_copy(
            src_ref=where,
            dst_ref=where,
            send_sem=s_row_z.at[s - 1, c, i, n],
            recv_sem=r_row_z.at[s - 1, c, i, n],
            device_id={"tensor": neighbour},
            device_id_type=MESH,
        )

    def part_copy(u, i, b):
        return pltpu.make_async_remote_copy(
            src_ref=stage.at[b],
            dst_ref=from_mate.at[u, i, b],
            send_sem=s_part.at[u, i, b],
            recv_sem=r_part.at[u, i, b],
            device_id={"dp": mate},
            device_id_type=MESH,
        )

    def sum_copy(s, i, b):
        return pltpu.make_async_remote_copy(
            src_ref=from_mate.at[s, i, b],
            dst_ref=x_in.at[s - 1, i, b],
            send_sem=s_sum.at[s - 1, i, b],
            recv_sem=r_sum.at[s - 1, i, b],
            device_id={"dp": x_peer(s) * CORES + core},
            device_id_type=MESH,
        )

    def map_copy(s, i):
        to = lax.rem(t + s, n_tensor)
        return pltpu.make_async_remote_copy(
            src_ref=made.at[i, pl.ds(to * s_half, s_half)],
            dst_ref=landed.at[s - 1, i],
            send_sem=s_map.at[s - 1, i],
            recv_sem=r_map.at[s - 1, i],
            device_id={"tensor": to},
            device_id_type=MESH,
        )

    def grad_copy(s, i):
        own = grads.at[x, i, core]
        return pltpu.make_async_remote_copy(
            src_ref=own,
            dst_ref=own,
            send_sem=s_grad.at[s - 1, i],
            recv_sem=r_grad.at[s - 1, i],
            device_id={"dp": x_peer(s) * CORES + core},
            device_id_type=MESH,
        )

    def grad_mate(s, i):
        block = grads.at[x_source(s), i, core]
        return pltpu.make_async_remote_copy(
            src_ref=block,
            dst_ref=block,
            send_sem=s_grad_mate.at[s, i],
            recv_sem=r_grad_mate.at[s, i],
            device_id={"dp": mate},
            device_id_type=MESH,
        )

    def greet():
        barrier = pltpu.get_barrier_semaphore()
        waits = 0
        for s in range(1, n_dp):
            pl.semaphore_signal(
                barrier, inc=1, device_id={"dp": lax.rem(dp + s, n_dp)}, device_id_type=MESH
            )
            waits += 1
        for s in range(1, n_tensor):
            pl.semaphore_signal(
                barrier, inc=1, device_id={"tensor": lax.rem(t + s, n_tensor)}, device_id_type=MESH
            )
            waits += 1
        pl.semaphore_wait(barrier, waits)

    def prepare(xraw, wraw, sraw):
        def w_copy(n):
            slot = lax.rem(n, 2)
            return pltpu.make_async_copy(
                w_ref.at[pl.ds(n * chunk, chunk)], wraw.at[slot], w_sem.at[slot]
            )

        def x_fetch(half):
            first = pieces[half][0][0]
            last = pieces[half][-1][0] + pieces[half][-1][1]
            many = min(last, tokens) - first
            return pltpu.make_async_copy(
                x_ref.at[pl.ds(first, many)], xraw.at[pl.ds(0, many)], x_sem.at[half]
            )

        sx_fetch = pltpu.make_async_copy(sx_ref, sraw.at[pl.ds(0, tokens)], sx_sem)
        sx_fetch.start()
        on_half(parity, lambda half: x_fetch(half).start())
        w_copy(0).start()
        w_copy(1).start()
        def clear(half):
            first = pieces[half][0][0]
            stop = pieces[half][-1][0] + pieces[half][-1][1]
            if stop > tokens:
                xraw[tokens - first : stop - first] = jnp.zeros(
                    (stop - tokens,) + xraw.shape[1:], jnp.bfloat16
                )

        on_half(parity, clear)
        sraw[tokens:pad] = jnp.zeros((pad - tokens,) + sraw.shape[1:], jnp.bfloat16)
        for j in range(images):
            slot_rows[dp, j : j + 1, :] = jnp.full((1, 128), slots_ref[j], jnp.int32)
        greet()
        for s in range(1, n_dp):
            slot_copy(s).start()

        sx_fetch.wait()

        def student_rows(r, carry):
            spot = pl.ds(pl.multiple_of(r * 16, 16), 16)
            both = jnp.swapaxes(sraw[spot], 0, 1)
            for i in range(images):
                block = layer_norm(both[i], sgain_ref[...], sbias_ref[...]).astype(jnp.bfloat16)
                for q in range(share):
                    student[q, dp * images + i, spot, :] = block[:, q * s_depth : (q + 1) * s_depth]
            return carry

        lax.fori_loop(0, pad // 16, student_rows, 0)
        for s in range(1, n_x):
            stu_x(s).start()
        stu_mate(0).start()

        def norm_piece(base, first, many):
            def norm_rows(r, carry):
                spot = pl.multiple_of(first + r * 16, 16)
                both = jnp.swapaxes(xraw[pl.ds(spot - base, 16)], 0, 1)
                for i in range(images):
                    block = layer_norm(both[i], gain_ref[...], 0.0).astype(jnp.bfloat16)
                    for d in range(n_dp):
                        normed[d, i, pl.ds(spot, 16), :] = block[:, d * depth : (d + 1) * depth]
                return carry

            lax.fori_loop(0, many // 16, norm_rows, 0)

        def send_half(half):
            x_fetch(half).wait()
            for n in range(2):
                norm_piece(pieces[half][0][0], *pieces[half][n])
                for s in range(1, n_x):
                    for c in range(CORES):
                        row_x(s, c, 0, half, n).start()
            for i in range(1, images):
                for n in range(2):
                    for s in range(1, n_x):
                        for c in range(CORES):
                            row_x(s, c, i, half, n).start()

        def norm_half(half):
            x_fetch(half).wait()
            for n in range(2):
                norm_piece(pieces[half][0][0], *pieces[half][n])

        on_half(parity, send_half)

        def fetch_rest(half):
            clear(half)
            x_fetch(half).start()

        on_half(1 - parity, fetch_rest)

        def split(n, carry):
            w_copy(n).wait()
            slot = lax.rem(n, 2)
            spot = pl.ds(pl.multiple_of(n * chunk, chunk), chunk)
            for b in range(blocks):
                both = jnp.swapaxes(wraw[slot, :, :, b * width : (b + 1) * width], 0, 1)
                wsplit[0, b, spot, :] = both[0]
                wsplit[1, b, spot, :] = both[1]

            @pl.when(n + 2 < w_chunks)
            def _():
                w_copy(n + 2).start()

            return carry

        lax.fori_loop(0, w_chunks, split, 0)
        on_half(1 - parity, norm_half)
        for i in range(images):
            row_mate(i).start()
            row_own(i).start()

    pl.run_scoped(
        prepare,
        pltpu.VMEM((pad - low,) + x_ref.shape[1:], jnp.bfloat16),
        pltpu.VMEM((2, chunk) + w_ref.shape[1:], jnp.bfloat16),
        pltpu.VMEM((pad,) + sx_ref.shape[1:], jnp.bfloat16),
    )

    acc[...] = jnp.zeros_like(acc)

    def project(lhs, b):
        keys = jnp.dot(lhs[...], wsplit[1, b], preferred_element_type=jnp.float32)
        query = jnp.dot(lhs[:QROWS], wsplit[0, b], preferred_element_type=jnp.float32)
        return keys, query

    def rows_of(place, a):
        return rows_in.at[a // CORES, place * CORES + a % CORES]

    def to_mate(u, a, b, before, lhs):
        keys, query = project(lhs, (1 - core) * mine + b)
        if before is not None:
            part_copy(*before, b).wait_send()
        stage[b, :pad] = keys.astype(jnp.bfloat16)
        stage[b, pad:] = query.astype(jnp.bfloat16)
        part_copy(u, a, b).start()

    def own_chip(a, before):
        def body(b, carry):
            to_mate(0, a, b, before, rows_of(x, a))
            return carry

        lax.fori_loop(0, mine, body, 0)

    def other_chip(s, a, before):
        def body(b, carry):
            @pl.when(b < mine)
            def _():
                lhs = rows_of(x_peer(s), a)
                to_mate(s, a, b, before, lhs)
                keys, query = project(lhs, core * mine + b)
                held[lax.rem(b, 2), :pad] = keys
                held[lax.rem(b, 2), pad:] = query

            @pl.when(b > 0)
            def _():
                j = b - 1
                part_copy(s, a, j).wait_recv()
                total = held[lax.rem(j, 2)] + from_mate[s, a, j].astype(jnp.float32)
                from_mate[s, a, j] = total.astype(jnp.bfloat16)
                sum_copy(s, a, j).start()

            return carry

        lax.fori_loop(0, mine + 1, body, 0)

    def pass_on(i, n):
        def act(half):
            for s in range(1, n_x):
                for c in range(CORES):
                    row_x_arrived(s, c, i, half, n).wait_recv()
                    row_z(s, c, i, half, n).start()

        on_half(parity, act)

    def passed_on(i):
        def act(half):
            for n in range(2):
                for s in range(1, n_x):
                    for c in range(CORES):
                        row_z(s, c, i, half, n).wait_recv()

        on_half(1 - parity, act)

    for i in range(images):
        row_mate(i).wait_recv()
        row_own(i).wait()
    before = None
    for i in range(images):
        if i < 2:
            pass_on(0, i)
        for a in range(i * CORES, (i + 1) * CORES):
            own_chip(a, before)
            before = (0, a)
    for n in range(images, 2):
        pass_on(0, n)
    for i in range(images):
        if i + 1 < images:
            pass_on(i + 1, 0)
        passed_on(i)
        for s in range(1, n_x):
            for a in range(i * CORES, (i + 1) * CORES):
                other_chip(s, a, before)
                before = (s, a)
        if i + 1 < images:
            pass_on(i + 1, 1)
        if i == 0:
            for s in range(1, n_x):
                stu_x(s).wait_recv()
                for q in range(1, share):
                    stu_z(s, q).start()

    def fold_copy(a):
        return pltpu.make_async_remote_copy(
            src_ref=fold_out.at[a % 2],
            dst_ref=fold_in.at[a % 2],
            send_sem=s_fold.at[a],
            recv_sem=r_fold.at[a],
            device_id={"dp": mate},
            device_id_type=MESH,
        )

    def attend_image(a):
        def attend(b, carry):
            keys, query = project(rows_of(x, a), core * mine + b)
            part_copy(0, a, b).wait_recv()
            keys += from_mate[0, a, b, :pad].astype(jnp.float32)
            query += from_mate[0, a, b, pad:].astype(jnp.float32)
            for s in range(1, n_x):
                sum_copy(s, a, b).wait_recv()
                keys += x_in[s - 1, a, b, :pad].astype(jnp.float32)
                query += x_in[s - 1, a, b, pad:].astype(jnp.float32)
            keys = keys.astype(jnp.bfloat16)
            query = (query * HD_T ** (-0.5)).astype(jnp.bfloat16)
            maps = []
            for h in range(width // HD_T):
                cols = slice(h * HD_T, (h + 1) * HD_T)
                scores = lax.dot_general(
                    keys[:, cols],
                    query[:, cols],
                    (((1,), (1,)), ((), ())),
                    preferred_element_type=jnp.float32,
                )
                one = key_softmax(scores, tokens)
                maps.append(one.astype(jnp.bfloat16).astype(jnp.float32))
            first = (t * blocks + core * mine + b) * (width // HD_T)
            for s in range(s_heads):
                place, k = s // s_here, s % s_here
                spot = (k // s_half, place * s_half + k % s_half)
                total = jnp.where(b == 0, 0.0, acc[spot])
                for h, one in enumerate(maps):
                    total += counts_ref[s, first + h].astype(jnp.float32) * one
                acc[spot] = total
            return carry

        lax.fori_loop(0, mine, attend, 0)
        if a >= 2:
            fold_copy(a - 2).wait_send()

        def give(n, carry):
            fold_out[a % 2, n] = acc[1 - core, n].astype(jnp.bfloat16)
            return carry

        lax.fori_loop(0, n_tensor * s_half, give, 0)
        fold_copy(a).start()
        fold_copy(a).wait_recv()

        def finish(n, carry):
            total = acc[core, n] + fold_in[a % 2, n].astype(jnp.float32)
            made[a, n] = (total / DIVISOR).astype(jnp.bfloat16)
            return carry

        lax.fori_loop(0, n_tensor * s_half, finish, 0)
        for s in range(1, n_tensor):
            map_copy(s, a).start()

    def slot_of(image):
        found = jnp.int32(0)
        for d in range(n_dp):
            for j in range(images):
                here = jnp.where(slot_table[d, j, 0] == image, d * images + j, 0)
                found = jnp.maximum(found, here)
        return found

    left = lax.broadcasted_iota(jnp.int32, (pad, s_cols), 1) < HD_S

    def student_forward(a):
        slot = slot_of((x * CORES + a % CORES) * images + a // CORES)
        cols = pl.ds(pl.multiple_of(core * (s_half * s_cols), s_half * s_cols), s_half * s_cols)
        total = jnp.zeros((pad, s_half * s_cols), jnp.float32)
        for q in range(share):
            total += jnp.dot(
                student[q, slot],
                sw_ref[q * s_depth : (q + 1) * s_depth, cols],
                preferred_element_type=jnp.float32,
            )
        for h in range(s_half):
            one = total[:, h * s_cols : (h + 1) * s_cols]
            one = jnp.where(left, one * HD_S ** (-0.5), one).astype(jnp.bfloat16)
            packed[a, h] = one
            keys, query, _ = apart(one)
            scores = lax.dot_general(
                keys, one[:QROWS], (((1,), (1,)), ((), ())), preferred_element_type=jnp.float32
            )
            probs[a, h] = key_softmax(scores, tokens)

    def apart(one):
        wide = one.astype(jnp.float32)
        turned = jnp.concatenate([wide[:, HD_S:], wide[:, :HD_S]], axis=1)
        keys = jnp.where(left, turned, 0.0).astype(jnp.bfloat16)
        query = jnp.where(left, 0.0, turned).astype(jnp.bfloat16)[:QROWS]
        return keys, query, turned

    def student_back(i):
        for s in range(1, n_tensor):
            map_copy(s, i).wait_recv()

        def head(h, carry):
            goal = made[i, t * s_half + h].astype(jnp.float32)
            for s in range(1, n_tensor):
                goal += landed[s - 1, i, h].astype(jnp.float32)
            goal = goal.astype(jnp.bfloat16).astype(jnp.float32)
            slope = probs[i, h] * jnp.sum(goal, axis=0, keepdims=True) - goal
            slope = slope.astype(jnp.bfloat16)
            keys, query, _ = apart(packed[i, h])
            for_query = (
                lax.dot_general(
                    slope, keys, (((0,), (0,)), ((), ())), preferred_element_type=jnp.float32
                )
                * HD_S ** (-0.5)
            )
            for_keys = jnp.dot(slope, query, preferred_element_type=jnp.float32)
            grads[x, i, core, h, :QROWS] = (for_query + for_keys[:QROWS]).astype(jnp.bfloat16)
            grads[x, i, core, h, QROWS:] = for_keys[QROWS:].astype(jnp.bfloat16)
            return carry

        lax.fori_loop(0, s_half, head, 0)
        for s in range(1, n_x):
            grad_copy(s, i).start()
        grad_mate(0, i).start()

    def add_image(place, a):
        slot = slot_of((place * CORES + a % CORES) * images + a // CORES)
        right = jnp.concatenate(
            [grads[place, a, h // s_half, h % s_half] for h in range(s_here)], axis=1
        )
        for q in range(share):
            rows = pl.ds(q * s_depth, s_depth)
            out_ref[rows, :] += lax.dot_general(
                student[q, slot], right, (((0,), (0,)), ((), ())), preferred_element_type=jnp.float32
            )

    def gather_grads(a):
        grad_mate(0, a).wait_recv()
        add_image(x, a)
        for s in range(1, n_x):
            grad_copy(s, a).wait_recv()
            grad_mate(s, a).start()
        for s in range(1, n_x):
            grad_mate(s, a).wait_recv()
            add_image(x_source(s), a)

    attend_image(0)
    for s in range(1, n_dp):
        slot_copy(s).wait_recv()
    table = pltpu.make_async_copy(slot_rows, slot_table, slot_sem)
    table.start()
    for s in range(1, n_x):
        for q in range(1, share):
            stu_z(s, q).wait_recv()
        stu_mate(s).start()
    table.wait()
    for s in range(n_x):
        stu_mate(s).wait_recv()
    for a in range(everyone):
        student_forward(a)
    out_ref[...] = jnp.zeros_like(out_ref)
    for a in range(1, everyone):
        attend_image(a)
        student_back(a - 1)
    for a in range(everyone - 1):
        gather_grads(a)
    student_back(everyone - 1)
    gather_grads(everyone - 1)

    def drain_half(half):
        for i in range(images):
            for n in range(2):
                for s in range(1, n_x):
                    for c in range(CORES):
                        row_x(s, c, i, half, n).wait_send()
                        row_z(s, c, i, half, n).wait_send()

    on_half(parity, drain_half)
    for s in range(1, n_dp):
        slot_copy(s).wait_send()
    for s in range(n_x):
        stu_mate(s).wait_send()
    for s in range(1, n_x):
        stu_x(s).wait_send()
        for q in range(1, share):
            stu_z(s, q).wait_send()
    for i in range(images):
        row_mate(i).wait_send()
    for a in range(everyone):
        if a >= everyone - 2:
            fold_copy(a).wait_send()
        for s in range(1, n_tensor):
            map_copy(s, a).wait_send()
        for s in range(1, n_x):
            grad_copy(s, a).wait_send()
        for s in range(n_x):
            grad_mate(s, a).wait_send()

        def drain(b, carry):
            if before == (before[0], a):
                part_copy(before[0], a, b).wait_send()
            for s in range(1, n_x):
                sum_copy(s, a, b).wait_send()
            return carry

        lax.fori_loop(0, mine, drain, 0)


def on_device(
    mesh_sizes,
    teacher_input,
    teacher_gain,
    teacher_weight,
    head_counts,
    assignment,
    student_input,
    student_gain,
    student_bias,
    student_weight,
):
    n_dp, n_tensor = mesh_sizes
    images, tokens, width = teacher_input.shape
    rows, _, width_here = teacher_weight.shape
    s_width, s_width_here = student_weight.shape
    heads_here = width_here // HD_T
    s_heads = head_counts.shape[1]
    s_here = s_heads // n_tensor
    pad = rounded_up(tokens, 16)
    n_x = n_dp // CORES
    others = max(n_x - 1, 1)
    per_block = 2 if heads_here % 2 == 0 else 1
    blocks = heads_here // per_block
    block_width = per_block * HD_T
    chunk = 192
    share = min(SHARE, n_tensor)
    both = pad + QROWS
    sizes = (n_dp, n_tensor, s_heads, images, tokens, pad, blocks, chunk)
    by_heads = blocks % CORES == 0 and s_here % CORES == 0
    dma = pltpu.SemaphoreType.DMA
    half = jnp.bfloat16
    in_vmem = pl.BlockSpec(memory_space=pltpu.VMEM)
    in_smem = pl.BlockSpec(memory_space=pltpu.SMEM)
    anywhere = pl.BlockSpec(memory_space=pl.ANY)
    if by_heads:
        kernel, units, mine, s_mine = distill_by_heads, images * CORES, blocks // CORES, s_here // CORES
        grads = (n_x, units, CORES, s_mine, pad, 2 * HD_S)
        folds = (2, n_tensor * s_mine, pad, QROWS)
        acc = (CORES,) + folds[1:]
        extra_memory = [pltpu.VMEM(folds, half), pltpu.VMEM(folds, half), dma((units,)), dma((units,))]
        extra_sem = [dma((images,))]
    else:
        kernel, units, mine, s_mine = distill_by_images, images, blocks, s_here
        grads = (images, n_dp, s_here, pad, 2 * HD_S)
        acc = (s_heads, pad, QROWS)
        extra_memory, extra_sem = [], []
    return pl.pallas_call(
        functools.partial(kernel, sizes),
        out_shape=jax.ShapeDtypeStruct((s_width, s_width_here), jnp.float32),
        in_specs=[
            in_smem,
            in_smem,
            anywhere,
            in_vmem,
            anywhere,
            anywhere,
            in_vmem,
            in_vmem,
            in_vmem,
        ],
        out_specs=in_vmem,
        scratch_shapes=[
            pltpu.VMEM((2, blocks, rows, block_width), half),
            pltpu.VMEM((n_dp, images, pad, rows), half),
            pltpu.VMEM((images, n_dp, pad, rows), half),
            pltpu.VMEM((mine, both, block_width), half),
            pltpu.VMEM((n_x, units, mine, both, block_width), half),
            pltpu.VMEM((others, units, mine, both, block_width), half),
            pltpu.VMEM((2, both, block_width), jnp.float32),
            pltpu.VMEM(acc, jnp.float32),
            pltpu.VMEM((units, n_tensor * s_mine, pad, QROWS), half),
            pltpu.VMEM((n_tensor - 1, units, s_mine, pad, QROWS), half),
            pltpu.VMEM((share, n_dp * images, pad, s_width // share), half),
            pltpu.VMEM((units, s_mine, pad, 2 * HD_S), half),
            pltpu.VMEM((units, s_mine, pad, QROWS), jnp.float32),
            pltpu.VMEM(grads, half),
            pltpu.VMEM((n_dp, 8, 128), jnp.int32),
            pltpu.SMEM((n_dp, 8, 128), jnp.int32),
            dma((2,)),
            dma((2,)),
            dma,
            dma,
            *extra_sem,
            dma((images,)),
            dma((images,)),
            dma((others, CORES, images, 2)),
            dma((others, CORES, images, 2)),
            dma((others, CORES, images, 2)),
            dma((others, CORES, images, 2)),
            dma((n_x, units, mine)),
            dma((n_x, units, mine)),
            dma((others, units, mine)),
            dma((others, units, mine)),
            dma((n_tensor - 1, units)),
            dma((n_tensor - 1, units)),
            dma((others, units)),
            dma((others, units)),
            dma((n_x, units)),
            dma((n_x, units)),
            *extra_memory,
            dma((n_dp - 1,)),
            dma((n_dp - 1,)),
            dma((n_x,)),
            dma((n_x,)),
            dma((others,)),
            dma((others,)),
            dma((others, share - 1)),
            dma((others, share - 1)),
        ],
        compiler_params=pltpu.CompilerParams(
            collective_id=0, has_side_effects=True, vmem_limit_bytes=67043328
        ),
    )(
        jnp.transpose(head_counts),
        assignment,
        jnp.transpose(teacher_input, (1, 0, 2)),
        teacher_gain.reshape(1, width),
        teacher_weight,
        jnp.transpose(student_input, (1, 0, 2)),
        student_gain.reshape(1, s_width),
        student_bias.reshape(1, s_width),
        student_weight,
    )


def solution(mesh):
    placed = (
        P(("group", "dp"), None, None),
        P(),
        P("dp", None, "tensor"),
        P(),
        P(("group", "dp")),
        P(("group", "dp"), None, None),
        P(),
        P(),
        P(None, "tensor"),
    )
    mesh_sizes = (mesh.shape["dp"], mesh.shape["tensor"])
    return jax.shard_map(
        functools.partial(on_device, mesh_sizes),
        mesh=mesh,
        in_specs=placed,
        out_specs=P("group", "tensor"),
        check_vma=False,
    )
```

```python
import functools

import jax
import jax.numpy as jnp
from jax import lax
from jax.experimental import pallas as pl
from jax.experimental.pallas import tpu as pltpu
from jax.sharding import PartitionSpec as P

HD_T = 128
HD_S = 64
QROWS = 128
DIVISOR = 72
CORES = 2
SHARE = 4
MESH = pl.DeviceIdType.MESH


def layer_norm(values, gain, shift):
    wide = values.astype(jnp.float32)
    center = wide - jnp.mean(wide, axis=-1, keepdims=True)
    spread = jnp.mean(center * center, axis=-1, keepdims=True)
    return center * lax.rsqrt(spread + 1e-06) * gain + shift


def rounded_up(value, unit):
    return -(-value // unit) * unit


def key_softmax(scores, tokens):
    spot = lax.broadcasted_iota(jnp.int32, scores.shape, 0)
    scores = jnp.where(spot < tokens, scores, -jnp.inf)
    power = jnp.exp(scores - jnp.max(scores, axis=0, keepdims=True))
    return power / jnp.sum(power, axis=0, keepdims=True)


def distill_by_images(
    sizes,
    counts_ref,
    slots_ref,
    x_ref,
    gain_ref,
    w_ref,
    sx_ref,
    sgain_ref,
    sbias_ref,
    sw_ref,
    out_ref,
    wsplit,
    normed,
    rows_in,
    stage,
    from_mate,
    x_in,
    held,
    acc,
    made,
    landed,
    student,
    packed,
    probs,
    grads,
    slot_rows,
    slot_table,
    w_sem,
    x_sem,
    sx_sem,
    slot_sem,
    s_row_mate,
    r_row_mate,
    s_row_x,
    r_row_x,
    s_row_z,
    r_row_z,
    s_part,
    r_part,
    s_sum,
    r_sum,
    s_map,
    r_map,
    s_grad,
    r_grad,
    s_grad_mate,
    r_grad_mate,
    s_slot,
    r_slot,
    s_stu_mate,
    r_stu_mate,
    s_stu_x,
    r_stu_x,
    s_stu_z,
    r_stu_z,
):
    n_dp, n_tensor, s_heads, images, tokens, pad, blocks, chunk = sizes
    n_x = n_dp // CORES
    depth = w_ref.shape[0]
    width = wsplit.shape[3]
    s_here = s_heads // n_tensor
    s_cols = 2 * HD_S
    share, s_depth = student.shape[0], student.shape[3]
    w_chunks = depth // chunk

    dp = lax.axis_index("dp")
    t = lax.axis_index("tensor")
    x = dp // CORES
    core = lax.rem(dp, CORES)
    mate = x * CORES + (1 - core)
    parity = lax.rem(t, 2)
    neighbour = t + 1 - 2 * parity
    quarter = lax.rem(t, share)

    def x_peer(s):
        return lax.rem(x + s, n_x)

    def x_source(s):
        return lax.rem(x + n_x - s, n_x)

    low = QROWS
    cut = (pad - low) // 32 * 16
    pieces = (
        ((0, low // 2), (low // 2, low // 2)),
        ((low, cut), (low + cut, pad - low - cut)),
    )

    def on_half(which, act):
        for half in range(2):

            @pl.when(which == half)
            def _():
                act(half)

    def slot_copy(s):
        return pltpu.make_async_remote_copy(
            src_ref=slot_rows.at[dp],
            dst_ref=slot_rows.at[dp],
            send_sem=s_slot.at[s - 1],
            recv_sem=r_slot.at[s - 1],
            device_id={"dp": lax.rem(dp + s, n_dp)},
            device_id_type=MESH,
        )

    def own_slots(source):
        return pl.ds(source * images, images)

    def stu_mate(s):
        where = student.at[:, own_slots(x_source(s) * CORES + core)]
        return pltpu.make_async_remote_copy(
            src_ref=where,
            dst_ref=where,
            send_sem=s_stu_mate.at[s],
            recv_sem=r_stu_mate.at[s],
            device_id={"dp": mate},
            device_id_type=MESH,
        )

    def stu_x(s):
        where = student.at[quarter, own_slots(dp)]
        return pltpu.make_async_remote_copy(
            src_ref=where,
            dst_ref=where,
            send_sem=s_stu_x.at[s - 1],
            recv_sem=r_stu_x.at[s - 1],
            device_id={"dp": x_peer(s) * CORES + core},
            device_id_type=MESH,
        )

    def stu_z(s, q):
        where = student.at[quarter, own_slots(x_source(s) * CORES + core)]
        return pltpu.make_async_remote_copy(
            src_ref=where,
            dst_ref=where,
            send_sem=s_stu_z.at[s - 1, q - 1],
            recv_sem=r_stu_z.at[s - 1, q - 1],
            device_id={"tensor": t - quarter + lax.rem(quarter + q, share)},
            device_id_type=MESH,
        )

    def row_mate(i):
        return pltpu.make_async_remote_copy(
            src_ref=normed.at[mate, i],
            dst_ref=rows_in.at[i, dp],
            send_sem=s_row_mate.at[i],
            recv_sem=r_row_mate.at[i],
            device_id={"dp": mate},
            device_id_type=MESH,
        )

    def row_x(s, c, i, half, n):
        first, many = pieces[half][n]
        to = x_peer(s) * CORES + c
        return pltpu.make_async_remote_copy(
            src_ref=normed.at[to, i, pl.ds(first, many)],
            dst_ref=rows_in.at[i, dp, pl.ds(first, many)],
            send_sem=s_row_x.at[s - 1, c, i, n],
            recv_sem=r_row_x.at[s - 1, core, i, n],
            device_id={"dp": to},
            device_id_type=MESH,
        )

    def row_x_arrived(s, c, i, half, n):
        first, many = pieces[half][n]
        return pltpu.make_async_remote_copy(
            src_ref=normed.at[dp, i, pl.ds(first, many)],
            dst_ref=rows_in.at[i, x_source(s) * CORES + c, pl.ds(first, many)],
            send_sem=s_row_x.at[s - 1, c, i, n],
            recv_sem=r_row_x.at[s - 1, c, i, n],
            device_id={"dp": mate},
            device_id_type=MESH,
        )

    def row_z(s, c, i, half, n):
        first, many = pieces[half][n]
        where = rows_in.at[i, x_source(s) * CORES + c, pl.ds(first, many)]
        return pltpu.make_async_remote_copy(
            src_ref=where,
            dst_ref=where,
            send_sem=s_row_z.at[s - 1, c, i, n],
            recv_sem=r_row_z.at[s - 1, c, i, n],
            device_id={"tensor": neighbour},
            device_id_type=MESH,
        )

    def part_copy(u, i, b):
        return pltpu.make_async_remote_copy(
            src_ref=stage.at[b],
            dst_ref=from_mate.at[u, i, b],
            send_sem=s_part.at[u, i, b],
            recv_sem=r_part.at[u, i, b],
            device_id={"dp": mate},
            device_id_type=MESH,
        )

    def sum_copy(s, i, b):
        return pltpu.make_async_remote_copy(
            src_ref=from_mate.at[s, i, b],
            dst_ref=x_in.at[s - 1, i, b],
            send_sem=s_sum.at[s - 1, i, b],
            recv_sem=r_sum.at[s - 1, i, b],
            device_id={"dp": x_peer(s) * CORES + core},
            device_id_type=MESH,
        )

    def map_copy(s, i):
        to = lax.rem(t + s, n_tensor)
        return pltpu.make_async_remote_copy(
            src_ref=made.at[i, pl.ds(to * s_here, s_here)],
            dst_ref=landed.at[s - 1, i],
            send_sem=s_map.at[s - 1, i],
            recv_sem=r_map.at[s - 1, i],
            device_id={"tensor": to},
            device_id_type=MESH,
        )

    def grad_copy(s, i):
        own = grads.at[i, dp]
        return pltpu.make_async_remote_copy(
            src_ref=own,
            dst_ref=own,
            send_sem=s_grad.at[s - 1, i],
            recv_sem=r_grad.at[s - 1, i],
            device_id={"dp": x_peer(s) * CORES + core},
            device_id_type=MESH,
        )

    def grad_mate(s, i):
        block = grads.at[i, x_source(s) * CORES + core]
        return pltpu.make_async_remote_copy(
            src_ref=block,
            dst_ref=block,
            send_sem=s_grad_mate.at[s, i],
            recv_sem=r_grad_mate.at[s, i],
            device_id={"dp": mate},
            device_id_type=MESH,
        )

    def greet():
        barrier = pltpu.get_barrier_semaphore()
        waits = 0
        for s in range(1, n_dp):
            pl.semaphore_signal(
                barrier, inc=1, device_id={"dp": lax.rem(dp + s, n_dp)}, device_id_type=MESH
            )
            waits += 1
        for s in range(1, n_tensor):
            pl.semaphore_signal(
                barrier, inc=1, device_id={"tensor": lax.rem(t + s, n_tensor)}, device_id_type=MESH
            )
            waits += 1
        pl.semaphore_wait(barrier, waits)

    def prepare(xraw, wraw, sraw):
        def w_copy(n):
            slot = lax.rem(n, 2)
            return pltpu.make_async_copy(
                w_ref.at[pl.ds(n * chunk, chunk)], wraw.at[slot], w_sem.at[slot]
            )

        def x_fetch(half):
            first = pieces[half][0][0]
            last = pieces[half][-1][0] + pieces[half][-1][1]
            many = min(last, tokens) - first
            return pltpu.make_async_copy(
                x_ref.at[pl.ds(first, many)], xraw.at[pl.ds(first, many)], x_sem.at[half]
            )

        sx_fetch = pltpu.make_async_copy(sx_ref, sraw.at[pl.ds(0, tokens)], sx_sem)
        sx_fetch.start()
        on_half(parity, lambda half: x_fetch(half).start())
        on_half(1 - parity, lambda half: x_fetch(half).start())
        w_copy(0).start()
        w_copy(1).start()
        xraw[tokens:pad] = jnp.zeros((pad - tokens,) + xraw.shape[1:], jnp.bfloat16)
        sraw[tokens:pad] = jnp.zeros((pad - tokens,) + sraw.shape[1:], jnp.bfloat16)
        for j in range(images):
            slot_rows[dp, j : j + 1, :] = jnp.full((1, 128), slots_ref[j], jnp.int32)
        greet()
        for s in range(1, n_dp):
            slot_copy(s).start()

        sx_fetch.wait()

        def student_rows(r, carry):
            spot = pl.ds(pl.multiple_of(r * 16, 16), 16)
            both = jnp.swapaxes(sraw[spot], 0, 1)
            for i in range(images):
                block = layer_norm(both[i], sgain_ref[...], sbias_ref[...]).astype(jnp.bfloat16)
                for q in range(share):
                    student[q, dp * images + i, spot, :] = block[:, q * s_depth : (q + 1) * s_depth]
            return carry

        lax.fori_loop(0, pad // 16, student_rows, 0)
        for s in range(1, n_x):
            stu_x(s).start()
        stu_mate(0).start()

        def norm_piece(first, many):
            def norm_rows(r, carry):
                spot = pl.multiple_of(first + r * 16, 16)
                both = jnp.swapaxes(xraw[pl.ds(spot, 16)], 0, 1)
                for i in range(images):
                    block = layer_norm(both[i], gain_ref[...], 0.0).astype(jnp.bfloat16)
                    for d in range(n_dp):
                        normed[d, i, pl.ds(spot, 16), :] = block[:, d * depth : (d + 1) * depth]
                return carry

            lax.fori_loop(0, many // 16, norm_rows, 0)

        def send_half(half):
            x_fetch(half).wait()
            for n in range(2):
                norm_piece(*pieces[half][n])
                for s in range(1, n_x):
                    for c in range(CORES):
                        row_x(s, c, 0, half, n).start()
            for i in range(1, images):
                for n in range(2):
                    for s in range(1, n_x):
                        for c in range(CORES):
                            row_x(s, c, i, half, n).start()

        def norm_half(half):
            x_fetch(half).wait()
            for n in range(2):
                norm_piece(*pieces[half][n])

        on_half(parity, send_half)
        on_half(1 - parity, norm_half)
        for i in range(images):
            row_mate(i).start()

        def split(n, carry):
            w_copy(n).wait()
            slot = lax.rem(n, 2)
            spot = pl.ds(pl.multiple_of(n * chunk, chunk), chunk)
            for b in range(blocks):
                both = jnp.swapaxes(wraw[slot, :, :, b * width : (b + 1) * width], 0, 1)
                wsplit[0, b, spot, :] = both[0]
                wsplit[1, b, spot, :] = both[1]

            @pl.when(n + 2 < w_chunks)
            def _():
                w_copy(n + 2).start()

            return carry

        lax.fori_loop(0, w_chunks, split, 0)

    pl.run_scoped(
        prepare,
        pltpu.VMEM((pad,) + x_ref.shape[1:], jnp.bfloat16),
        pltpu.VMEM((2, chunk) + w_ref.shape[1:], jnp.bfloat16),
        pltpu.VMEM((pad,) + sx_ref.shape[1:], jnp.bfloat16),
    )

    acc[...] = jnp.zeros_like(acc)

    def project(lhs, b):
        keys = jnp.dot(lhs[...], wsplit[1, b], preferred_element_type=jnp.float32)
        query = jnp.dot(lhs[:QROWS], wsplit[0, b], preferred_element_type=jnp.float32)
        return keys, query

    def to_mate(u, i, b, before, lhs):
        keys, query = project(lhs, b)
        if before is not None:
            part_copy(*before, b).wait_send()
        stage[b, :pad] = keys.astype(jnp.bfloat16)
        stage[b, pad:] = query.astype(jnp.bfloat16)
        part_copy(u, i, b).start()

    def own_chip(i, before):
        row_mate(i).wait_recv()

        def body(b, carry):
            to_mate(0, i, b, before, rows_in.at[i, mate])
            return carry

        lax.fori_loop(0, blocks, body, 0)

    def other_chip(s, i, before, start, stop):
        def body(b, carry):
            @pl.when(b < blocks)
            def _():
                away = x_peer(s) * CORES
                to_mate(s, i, b, before, rows_in.at[i, away + 1 - core])
                keys, query = project(rows_in.at[i, away + core], b)
                held[lax.rem(b, 2), :pad] = keys
                held[lax.rem(b, 2), pad:] = query

            @pl.when(b > 0)
            def _():
                j = b - 1
                part_copy(s, i, j).wait_recv()
                total = held[lax.rem(j, 2)] + from_mate[s, i, j].astype(jnp.float32)
                from_mate[s, i, j] = total.astype(jnp.bfloat16)
                sum_copy(s, i, j).start()

            return carry

        lax.fori_loop(start, stop, body, 0)

    def pass_on(i, n):
        def act(half):
            for s in range(1, n_x):
                for c in range(CORES):
                    row_x_arrived(s, c, i, half, n).wait_recv()
                    row_z(s, c, i, half, n).start()

        on_half(parity, act)

    def passed_on(i):
        def act(half):
            for n in range(2):
                for s in range(1, n_x):
                    for c in range(CORES):
                        row_z(s, c, i, half, n).wait_recv()

        on_half(1 - parity, act)

    before = None
    for i in range(images):
        pass_on(0, i) if i < 2 else None
        own_chip(i, before)
        before = (0, i)
    for n in range(images, 2):
        pass_on(0, n)
    for i in range(images):
        if i + 1 < images:
            pass_on(i + 1, 0)
        passed_on(i)
        for s in range(1, n_x):
            early = blocks // 2 if s == 1 else 0
            other_chip(s, i, before, 0, early)
            if s == 1 and i + 1 < images:
                pass_on(i + 1, 1)
            other_chip(s, i, before, early, blocks + 1)
            before = (s, i)
        if i == 0:
            for s in range(1, n_x):
                stu_x(s).wait_recv()
                for q in range(1, share):
                    stu_z(s, q).start()

    def attend_image(i):
        def attend(b, carry):
            keys, query = project(normed.at[dp, i], b)
            part_copy(0, i, b).wait_recv()
            keys += from_mate[0, i, b, :pad].astype(jnp.float32)
            query += from_mate[0, i, b, pad:].astype(jnp.float32)
            for s in range(1, n_x):
                sum_copy(s, i, b).wait_recv()
                keys += x_in[s - 1, i, b, :pad].astype(jnp.float32)
                query += x_in[s - 1, i, b, pad:].astype(jnp.float32)
            keys = keys.astype(jnp.bfloat16)
            query = (query * HD_T ** (-0.5)).astype(jnp.bfloat16)
            maps = []
            for h in range(width // HD_T):
                cols = slice(h * HD_T, (h + 1) * HD_T)
                scores = lax.dot_general(
                    keys[:, cols],
                    query[:, cols],
                    (((1,), (1,)), ((), ())),
                    preferred_element_type=jnp.float32,
                )
                one = key_softmax(scores, tokens)
                maps.append(one.astype(jnp.bfloat16).astype(jnp.float32))
            first = t * (blocks * (width // HD_T)) + b * (width // HD_T)
            for s in range(s_heads):
                total = acc[s]
                for h, one in enumerate(maps):
                    total += counts_ref[s, first + h].astype(jnp.float32) * one
                acc[s] = total
            return carry

        lax.fori_loop(0, blocks, attend, 0)

        def finish(s, carry):
            made[i, s] = (acc[s] / DIVISOR).astype(jnp.bfloat16)
            acc[s] = jnp.zeros(acc.shape[1:], jnp.float32)
            return carry

        lax.fori_loop(0, s_heads, finish, 0)
        for s in range(1, n_tensor):
            map_copy(s, i).start()

    def slot_of(image):
        found = jnp.int32(0)
        for d in range(n_dp):
            for j in range(images):
                here = jnp.where(slot_table[d, j, 0] == image, d * images + j, 0)
                found = jnp.maximum(found, here)
        return found

    left = lax.broadcasted_iota(jnp.int32, (pad, s_cols), 1) < HD_S

    def student_forward(i):
        slot = slot_of(dp * images + i)
        total = jnp.zeros((pad, s_here * s_cols), jnp.float32)
        for q in range(share):
            total += jnp.dot(
                student[q, slot],
                sw_ref[q * s_depth : (q + 1) * s_depth, :],
                preferred_element_type=jnp.float32,
            )
        for h in range(s_here):
            one = total[:, h * s_cols : (h + 1) * s_cols]
            one = jnp.where(left, one * HD_S ** (-0.5), one).astype(jnp.bfloat16)
            packed[i, h] = one
            keys, query, _ = apart(one)
            scores = lax.dot_general(
                keys, one[:QROWS], (((1,), (1,)), ((), ())), preferred_element_type=jnp.float32
            )
            probs[i, h] = key_softmax(scores, tokens)

    def apart(one):
        wide = one.astype(jnp.float32)
        turned = jnp.concatenate([wide[:, HD_S:], wide[:, :HD_S]], axis=1)
        keys = jnp.where(left, turned, 0.0).astype(jnp.bfloat16)
        query = jnp.where(left, 0.0, turned).astype(jnp.bfloat16)[:QROWS]
        return keys, query, turned

    def student_back(i):
        for s in range(1, n_tensor):
            map_copy(s, i).wait_recv()

        def head(h, carry):
            goal = made[i, t * s_here + h].astype(jnp.float32)
            for s in range(1, n_tensor):
                goal += landed[s - 1, i, h].astype(jnp.float32)
            goal = goal.astype(jnp.bfloat16).astype(jnp.float32)
            slope = probs[i, h] * jnp.sum(goal, axis=0, keepdims=True) - goal
            slope = slope.astype(jnp.bfloat16)
            keys, query, _ = apart(packed[i, h])
            for_query = (
                lax.dot_general(
                    slope, keys, (((0,), (0,)), ((), ())), preferred_element_type=jnp.float32
                )
                * HD_S ** (-0.5)
            )
            for_keys = jnp.dot(slope, query, preferred_element_type=jnp.float32)
            grads[i, dp, h, :QROWS] = (for_query + for_keys[:QROWS]).astype(jnp.bfloat16)
            grads[i, dp, h, QROWS:] = for_keys[QROWS:].astype(jnp.bfloat16)
            return carry

        lax.fori_loop(0, s_here, head, 0)
        for s in range(1, n_x):
            grad_copy(s, i).start()
        grad_mate(0, i).start()

    def add_images(i, source):
        slot = slot_of(source * images + i)
        right = jnp.concatenate([grads[i, source, h] for h in range(s_here)], axis=1)
        for q in range(share):
            rows = pl.ds(q * s_depth, s_depth)
            out_ref[rows, :] += lax.dot_general(
                student[q, slot], right, (((0,), (0,)), ((), ())), preferred_element_type=jnp.float32
            )

    def gather_grads(i):
        add_images(i, dp)
        grad_mate(0, i).wait_recv()
        add_images(i, mate)
        for s in range(1, n_x):
            grad_copy(s, i).wait_recv()
            grad_mate(s, i).start()
            add_images(i, x_source(s) * CORES + core)
        for s in range(1, n_x):
            grad_mate(s, i).wait_recv()
            add_images(i, x_source(s) * CORES + 1 - core)

    attend_image(0)
    for s in range(1, n_dp):
        slot_copy(s).wait_recv()
    table = pltpu.make_async_copy(slot_rows, slot_table, slot_sem)
    table.start()
    for s in range(1, n_x):
        for q in range(1, share):
            stu_z(s, q).wait_recv()
        stu_mate(s).start()
    table.wait()
    for s in range(n_x):
        stu_mate(s).wait_recv()
    for i in range(images):
        student_forward(i)
    out_ref[...] = jnp.zeros_like(out_ref)
    for i in range(1, images):
        attend_image(i)
    for i in range(images):
        student_back(i)
        gather_grads(i)

    def drain_half(half):
        for i in range(images):
            for n in range(2):
                for s in range(1, n_x):
                    for c in range(CORES):
                        row_x(s, c, i, half, n).wait_send()
                        row_z(s, c, i, half, n).wait_send()

    on_half(parity, drain_half)
    for s in range(1, n_dp):
        slot_copy(s).wait_send()
    for s in range(n_x):
        stu_mate(s).wait_send()
    for s in range(1, n_x):
        stu_x(s).wait_send()
        for q in range(1, share):
            stu_z(s, q).wait_send()
    for i in range(images):
        row_mate(i).wait_send()
        for s in range(1, n_tensor):
            map_copy(s, i).wait_send()
        for s in range(1, n_x):
            grad_copy(s, i).wait_send()
        for s in range(n_x):
            grad_mate(s, i).wait_send()

        def drain(b, carry):
            if before == (before[0], i):
                part_copy(before[0], i, b).wait_send()
            for s in range(1, n_x):
                sum_copy(s, i, b).wait_send()
            return carry

        lax.fori_loop(0, blocks, drain, 0)


def distill_by_heads(
    sizes,
    counts_ref,
    slots_ref,
    x_ref,
    gain_ref,
    w_ref,
    sx_ref,
    sgain_ref,
    sbias_ref,
    sw_ref,
    out_ref,
    wsplit,
    normed,
    rows_in,
    stage,
    from_mate,
    x_in,
    held,
    acc,
    made,
    landed,
    student,
    packed,
    probs,
    grads,
    slot_rows,
    slot_table,
    w_sem,
    x_sem,
    sx_sem,
    slot_sem,
    own_sem,
    s_row_mate,
    r_row_mate,
    s_row_x,
    r_row_x,
    s_row_z,
    r_row_z,
    s_part,
    r_part,
    s_sum,
    r_sum,
    s_map,
    r_map,
    s_grad,
    r_grad,
    s_grad_mate,
    r_grad_mate,
    fold_out,
    fold_in,
    s_fold,
    r_fold,
    s_slot,
    r_slot,
    s_stu_mate,
    r_stu_mate,
    s_stu_x,
    r_stu_x,
    s_stu_z,
    r_stu_z,
):
    n_dp, n_tensor, s_heads, images, tokens, pad, blocks, chunk = sizes
    n_x = n_dp // CORES
    depth = w_ref.shape[0]
    width = wsplit.shape[3]
    s_here = s_heads // n_tensor
    s_half = s_here // CORES
    mine = blocks // CORES
    everyone = images * CORES
    s_cols = 2 * HD_S
    share, s_depth = student.shape[0], student.shape[3]
    w_chunks = depth // chunk

    dp = lax.axis_index("dp")
    t = lax.axis_index("tensor")
    x = dp // CORES
    core = lax.rem(dp, CORES)
    mate = x * CORES + (1 - core)
    parity = lax.rem(t, 2)
    neighbour = t + 1 - 2 * parity
    quarter = lax.rem(t, share)

    def x_peer(s):
        return lax.rem(x + s, n_x)

    def x_source(s):
        return lax.rem(x + n_x - s, n_x)

    low = QROWS
    cut = (pad - low) // 32 * 16
    pieces = (
        ((0, low // 2), (low // 2, low // 2)),
        ((low, cut), (low + cut, pad - low - cut)),
    )

    def on_half(which, act):
        for half in range(2):

            @pl.when(which == half)
            def _():
                act(half)

    def slot_copy(s):
        return pltpu.make_async_remote_copy(
            src_ref=slot_rows.at[dp],
            dst_ref=slot_rows.at[dp],
            send_sem=s_slot.at[s - 1],
            recv_sem=r_slot.at[s - 1],
            device_id={"dp": lax.rem(dp + s, n_dp)},
            device_id_type=MESH,
        )

    def own_slots(source):
        return pl.ds(source * images, images)

    def stu_mate(s):
        where = student.at[:, own_slots(x_source(s) * CORES + core)]
        return pltpu.make_async_remote_copy(
            src_ref=where,
            dst_ref=where,
            send_sem=s_stu_mate.at[s],
            recv_sem=r_stu_mate.at[s],
            device_id={"dp": mate},
            device_id_type=MESH,
        )

    def stu_x(s):
        where = student.at[quarter, own_slots(dp)]
        return pltpu.make_async_remote_copy(
            src_ref=where,
            dst_ref=where,
            send_sem=s_stu_x.at[s - 1],
            recv_sem=r_stu_x.at[s - 1],
            device_id={"dp": x_peer(s) * CORES + core},
            device_id_type=MESH,
        )

    def stu_z(s, q):
        where = student.at[quarter, own_slots(x_source(s) * CORES + core)]
        return pltpu.make_async_remote_copy(
            src_ref=where,
            dst_ref=where,
            send_sem=s_stu_z.at[s - 1, q - 1],
            recv_sem=r_stu_z.at[s - 1, q - 1],
            device_id={"tensor": t - quarter + lax.rem(quarter + q, share)},
            device_id_type=MESH,
        )

    def row_mate(i):
        return pltpu.make_async_remote_copy(
            src_ref=normed.at[mate, i],
            dst_ref=rows_in.at[i, dp],
            send_sem=s_row_mate.at[i],
            recv_sem=r_row_mate.at[i],
            device_id={"dp": mate},
            device_id_type=MESH,
        )

    def row_own(i):
        return pltpu.make_async_copy(normed.at[dp, i], rows_in.at[i, dp], own_sem.at[i])

    def row_x(s, c, i, half, n):
        first, many = pieces[half][n]
        to = x_peer(s) * CORES + c
        return pltpu.make_async_remote_copy(
            src_ref=normed.at[to, i, pl.ds(first, many)],
            dst_ref=rows_in.at[i, dp, pl.ds(first, many)],
            send_sem=s_row_x.at[s - 1, c, i, n],
            recv_sem=r_row_x.at[s - 1, core, i, n],
            device_id={"dp": to},
            device_id_type=MESH,
        )

    def row_x_arrived(s, c, i, half, n):
        first, many = pieces[half][n]
        return pltpu.make_async_remote_copy(
            src_ref=normed.at[dp, i, pl.ds(first, many)],
            dst_ref=rows_in.at[i, x_source(s) * CORES + c, pl.ds(first, many)],
            send_sem=s_row_x.at[s - 1, c, i, n],
            recv_sem=r_row_x.at[s - 1, c, i, n],
            device_id={"dp": mate},
            device_id_type=MESH,
        )

    def row_z(s, c, i, half, n):
        first, many = pieces[half][n]
        where = rows_in.at[i, x_source(s) * CORES + c, pl.ds(first, many)]
        return pltpu.make_async_remote_copy(
            src_ref=where,
            dst_ref=where,
            send_sem=s_row_z.at[s - 1, c, i, n],
            recv_sem=r_row_z.at[s - 1, c, i, n],
            device_id={"tensor": neighbour},
            device_id_type=MESH,
        )

    def part_copy(u, i, b):
        return pltpu.make_async_remote_copy(
            src_ref=stage.at[b],
            dst_ref=from_mate.at[u, i, b],
            send_sem=s_part.at[u, i, b],
            recv_sem=r_part.at[u, i, b],
            device_id={"dp": mate},
            device_id_type=MESH,
        )

    def sum_copy(s, i, b):
        return pltpu.make_async_remote_copy(
            src_ref=from_mate.at[s, i, b],
            dst_ref=x_in.at[s - 1, i, b],
            send_sem=s_sum.at[s - 1, i, b],
            recv_sem=r_sum.at[s - 1, i, b],
            device_id={"dp": x_peer(s) * CORES + core},
            device_id_type=MESH,
        )

    def map_copy(s, i):
        to = lax.rem(t + s, n_tensor)
        return pltpu.make_async_remote_copy(
            src_ref=made.at[i, pl.ds(to * s_half, s_half)],
            dst_ref=landed.at[s - 1, i],
            send_sem=s_map.at[s - 1, i],
            recv_sem=r_map.at[s - 1, i],
            device_id={"tensor": to},
            device_id_type=MESH,
        )

    def grad_copy(s, i):
        own = grads.at[x, i, core]
        return pltpu.make_async_remote_copy(
            src_ref=own,
            dst_ref=own,
            send_sem=s_grad.at[s - 1, i],
            recv_sem=r_grad.at[s - 1, i],
            device_id={"dp": x_peer(s) * CORES + core},
            device_id_type=MESH,
        )

    def grad_mate(s, i):
        block = grads.at[x_source(s), i, core]
        return pltpu.make_async_remote_copy(
            src_ref=block,
            dst_ref=block,
            send_sem=s_grad_mate.at[s, i],
            recv_sem=r_grad_mate.at[s, i],
            device_id={"dp": mate},
            device_id_type=MESH,
        )

    def greet():
        barrier = pltpu.get_barrier_semaphore()
        waits = 0
        for s in range(1, n_dp):
            pl.semaphore_signal(
                barrier, inc=1, device_id={"dp": lax.rem(dp + s, n_dp)}, device_id_type=MESH
            )
            waits += 1
        for s in range(1, n_tensor):
            pl.semaphore_signal(
                barrier, inc=1, device_id={"tensor": lax.rem(t + s, n_tensor)}, device_id_type=MESH
            )
            waits += 1
        pl.semaphore_wait(barrier, waits)

    def prepare(xraw, wraw, sraw):
        def w_copy(n):
            slot = lax.rem(n, 2)
            return pltpu.make_async_copy(
                w_ref.at[pl.ds(n * chunk, chunk)], wraw.at[slot], w_sem.at[slot]
            )

        def x_fetch(half):
            first = pieces[half][0][0]
            last = pieces[half][-1][0] + pieces[half][-1][1]
            many = min(last, tokens) - first
            return pltpu.make_async_copy(
                x_ref.at[pl.ds(first, many)], xraw.at[pl.ds(0, many)], x_sem.at[half]
            )

        sx_fetch = pltpu.make_async_copy(sx_ref, sraw.at[pl.ds(0, tokens)], sx_sem)
        sx_fetch.start()
        on_half(parity, lambda half: x_fetch(half).start())
        w_copy(0).start()
        w_copy(1).start()
        def clear(half):
            first = pieces[half][0][0]
            stop = pieces[half][-1][0] + pieces[half][-1][1]
            if stop > tokens:
                xraw[tokens - first : stop - first] = jnp.zeros(
                    (stop - tokens,) + xraw.shape[1:], jnp.bfloat16
                )

        on_half(parity, clear)
        sraw[tokens:pad] = jnp.zeros((pad - tokens,) + sraw.shape[1:], jnp.bfloat16)
        for j in range(images):
            slot_rows[dp, j : j + 1, :] = jnp.full((1, 128), slots_ref[j], jnp.int32)
        greet()
        for s in range(1, n_dp):
            slot_copy(s).start()

        sx_fetch.wait()

        def student_rows(r, carry):
            spot = pl.ds(pl.multiple_of(r * 16, 16), 16)
            both = jnp.swapaxes(sraw[spot], 0, 1)
            for i in range(images):
                block = layer_norm(both[i], sgain_ref[...], sbias_ref[...]).astype(jnp.bfloat16)
                for q in range(share):
                    student[q, dp * images + i, spot, :] = block[:, q * s_depth : (q + 1) * s_depth]
            return carry

        lax.fori_loop(0, pad // 16, student_rows, 0)
        for s in range(1, n_x):
            stu_x(s).start()
        stu_mate(0).start()

        def norm_piece(base, first, many):
            def norm_rows(r, carry):
                spot = pl.multiple_of(first + r * 16, 16)
                both = jnp.swapaxes(xraw[pl.ds(spot - base, 16)], 0, 1)
                for i in range(images):
                    block = layer_norm(both[i], gain_ref[...], 0.0).astype(jnp.bfloat16)
                    for d in range(n_dp):
                        normed[d, i, pl.ds(spot, 16), :] = block[:, d * depth : (d + 1) * depth]
                return carry

            lax.fori_loop(0, many // 16, norm_rows, 0)

        def send_half(half):
            x_fetch(half).wait()
            for n in range(2):
                norm_piece(pieces[half][0][0], *pieces[half][n])
                for s in range(1, n_x):
                    for c in range(CORES):
                        row_x(s, c, 0, half, n).start()
            for i in range(1, images):
                for n in range(2):
                    for s in range(1, n_x):
                        for c in range(CORES):
                            row_x(s, c, i, half, n).start()

        def norm_half(half):
            x_fetch(half).wait()
            for n in range(2):
                norm_piece(pieces[half][0][0], *pieces[half][n])

        on_half(parity, send_half)
        for s in range(1, n_x):
            stu_x(s).wait_recv()
            for q in range(1, share):
                stu_z(s, q).start()

        def fetch_rest(half):
            clear(half)
            x_fetch(half).start()

        on_half(1 - parity, fetch_rest)

        def split(n, carry):
            w_copy(n).wait()
            slot = lax.rem(n, 2)
            spot = pl.ds(pl.multiple_of(n * chunk, chunk), chunk)
            for b in range(blocks):
                both = jnp.swapaxes(wraw[slot, :, :, b * width : (b + 1) * width], 0, 1)
                wsplit[0, b, spot, :] = both[0]
                wsplit[1, b, spot, :] = both[1]

            @pl.when(n + 2 < w_chunks)
            def _():
                w_copy(n + 2).start()

            return carry

        lax.fori_loop(0, w_chunks, split, 0)
        on_half(1 - parity, norm_half)
        for i in range(images):
            row_mate(i).start()
            row_own(i).start()

    pl.run_scoped(
        prepare,
        pltpu.VMEM((pad - low,) + x_ref.shape[1:], jnp.bfloat16),
        pltpu.VMEM((2, chunk) + w_ref.shape[1:], jnp.bfloat16),
        pltpu.VMEM((pad,) + sx_ref.shape[1:], jnp.bfloat16),
    )

    acc[...] = jnp.zeros_like(acc)

    def project(lhs, b):
        keys = jnp.dot(lhs[...], wsplit[1, b], preferred_element_type=jnp.float32)
        query = jnp.dot(lhs[:QROWS], wsplit[0, b], preferred_element_type=jnp.float32)
        return keys, query

    def rows_of(place, a):
        return rows_in.at[a // CORES, place * CORES + a % CORES]

    def to_mate(u, a, b, before, lhs):
        keys, query = project(lhs, (1 - core) * mine + b)
        if before is not None:
            part_copy(*before, b).wait_send()
        stage[b, :pad] = keys.astype(jnp.bfloat16)
        stage[b, pad:] = query.astype(jnp.bfloat16)
        part_copy(u, a, b).start()

    def own_chip(a, before):
        def body(b, carry):
            to_mate(0, a, b, before, rows_of(x, a))
            return carry

        lax.fori_loop(0, mine, body, 0)

    def other_chip(s, a, before):
        def body(b, carry):
            @pl.when(b < mine)
            def _():
                lhs = rows_of(x_peer(s), a)
                to_mate(s, a, b, before, lhs)
                keys, query = project(lhs, core * mine + b)
                held[lax.rem(b, 2), :pad] = keys
                held[lax.rem(b, 2), pad:] = query

            @pl.when(b > 0)
            def _():
                j = b - 1
                part_copy(s, a, j).wait_recv()
                total = held[lax.rem(j, 2)] + from_mate[s, a, j].astype(jnp.float32)
                from_mate[s, a, j] = total.astype(jnp.bfloat16)
                sum_copy(s, a, j).start()

            return carry

        lax.fori_loop(0, mine + 1, body, 0)

    def pass_on(i, n):
        def act(half):
            for s in range(1, n_x):
                for c in range(CORES):
                    row_x_arrived(s, c, i, half, n).wait_recv()
                    row_z(s, c, i, half, n).start()

        on_half(parity, act)

    def passed_on(i):
        def act(half):
            for n in range(2):
                for s in range(1, n_x):
                    for c in range(CORES):
                        row_z(s, c, i, half, n).wait_recv()

        on_half(1 - parity, act)

    for i in range(images):
        row_mate(i).wait_recv()
        row_own(i).wait()
    before = None
    for i in range(images):
        if i < 2:
            pass_on(0, i)
        for a in range(i * CORES, (i + 1) * CORES):
            own_chip(a, before)
            before = (0, a)
    for n in range(images, 2):
        pass_on(0, n)
    def fold_copy(a):
        return pltpu.make_async_remote_copy(
            src_ref=fold_out.at[a % 2],
            dst_ref=fold_in.at[a % 2],
            send_sem=s_fold.at[a],
            recv_sem=r_fold.at[a],
            device_id={"dp": mate},
            device_id_type=MESH,
        )

    def attend_image(a):
        def attend(b, carry):
            keys, query = project(rows_of(x, a), core * mine + b)
            part_copy(0, a, b).wait_recv()
            keys += from_mate[0, a, b, :pad].astype(jnp.float32)
            query += from_mate[0, a, b, pad:].astype(jnp.float32)
            for s in range(1, n_x):
                sum_copy(s, a, b).wait_recv()
                keys += x_in[s - 1, a, b, :pad].astype(jnp.float32)
                query += x_in[s - 1, a, b, pad:].astype(jnp.float32)
            keys = keys.astype(jnp.bfloat16)
            query = (query * HD_T ** (-0.5)).astype(jnp.bfloat16)
            maps = []
            for h in range(width // HD_T):
                cols = slice(h * HD_T, (h + 1) * HD_T)
                scores = lax.dot_general(
                    keys[:, cols],
                    query[:, cols],
                    (((1,), (1,)), ((), ())),
                    preferred_element_type=jnp.float32,
                )
                one = key_softmax(scores, tokens)
                maps.append(one.astype(jnp.bfloat16).astype(jnp.float32))
            first = (t * blocks + core * mine + b) * (width // HD_T)
            for s in range(s_heads):
                place, k = s // s_here, s % s_here
                spot = (k // s_half, place * s_half + k % s_half)
                total = jnp.where(b == 0, 0.0, acc[spot])
                for h, one in enumerate(maps):
                    total += counts_ref[s, first + h].astype(jnp.float32) * one
                acc[spot] = total
            return carry

        lax.fori_loop(0, mine, attend, 0)
        if a >= 2:
            fold_copy(a - 2).wait_send()

        def give(n, carry):
            fold_out[a % 2, n] = acc[1 - core, n].astype(jnp.bfloat16)
            return carry

        lax.fori_loop(0, n_tensor * s_half, give, 0)
        fold_copy(a).start()
        fold_copy(a).wait_recv()

        def finish(n, carry):
            total = acc[core, n] + fold_in[a % 2, n].astype(jnp.float32)
            made[a, n] = (total / DIVISOR).astype(jnp.bfloat16)
            return carry

        lax.fori_loop(0, n_tensor * s_half, finish, 0)
        for s in range(1, n_tensor):
            map_copy(s, a).start()

    def slot_of(image):
        found = jnp.int32(0)
        for d in range(n_dp):
            for j in range(images):
                here = jnp.where(slot_table[d, j, 0] == image, d * images + j, 0)
                found = jnp.maximum(found, here)
        return found

    left = lax.broadcasted_iota(jnp.int32, (pad, s_cols), 1) < HD_S

    def student_forward(a):
        slot = slot_of((x * CORES + a % CORES) * images + a // CORES)
        cols = pl.ds(pl.multiple_of(core * (s_half * s_cols), s_half * s_cols), s_half * s_cols)
        total = jnp.zeros((pad, s_half * s_cols), jnp.float32)
        for q in range(share):
            total += jnp.dot(
                student[q, slot],
                sw_ref[q * s_depth : (q + 1) * s_depth, cols],
                preferred_element_type=jnp.float32,
            )
        for h in range(s_half):
            one = total[:, h * s_cols : (h + 1) * s_cols]
            one = jnp.where(left, one * HD_S ** (-0.5), one).astype(jnp.bfloat16)
            packed[a, h] = one
            keys, query, _ = apart(one)
            scores = lax.dot_general(
                keys, one[:QROWS], (((1,), (1,)), ((), ())), preferred_element_type=jnp.float32
            )
            probs[a, h] = key_softmax(scores, tokens)

    def apart(one):
        wide = one.astype(jnp.float32)
        turned = jnp.concatenate([wide[:, HD_S:], wide[:, :HD_S]], axis=1)
        keys = jnp.where(left, turned, 0.0).astype(jnp.bfloat16)
        query = jnp.where(left, 0.0, turned).astype(jnp.bfloat16)[:QROWS]
        return keys, query, turned

    def student_back(i):
        for s in range(1, n_tensor):
            map_copy(s, i).wait_recv()

        def head(h, carry):
            goal = made[i, t * s_half + h].astype(jnp.float32)
            for s in range(1, n_tensor):
                goal += landed[s - 1, i, h].astype(jnp.float32)
            goal = goal.astype(jnp.bfloat16).astype(jnp.float32)
            slope = probs[i, h] * jnp.sum(goal, axis=0, keepdims=True) - goal
            slope = slope.astype(jnp.bfloat16)
            keys, query, _ = apart(packed[i, h])
            for_query = (
                lax.dot_general(
                    slope, keys, (((0,), (0,)), ((), ())), preferred_element_type=jnp.float32
                )
                * HD_S ** (-0.5)
            )
            for_keys = jnp.dot(slope, query, preferred_element_type=jnp.float32)
            grads[x, i, core, h, :QROWS] = (for_query + for_keys[:QROWS]).astype(jnp.bfloat16)
            grads[x, i, core, h, QROWS:] = for_keys[QROWS:].astype(jnp.bfloat16)
            return carry

        lax.fori_loop(0, s_half, head, 0)
        for s in range(1, n_x):
            grad_copy(s, i).start()
        grad_mate(0, i).start()

    def add_image(place, a):
        slot = slot_of((place * CORES + a % CORES) * images + a // CORES)
        right = jnp.concatenate(
            [grads[place, a, h // s_half, h % s_half] for h in range(s_here)], axis=1
        )
        for q in range(share):
            rows = pl.ds(q * s_depth, s_depth)
            out_ref[rows, :] += lax.dot_general(
                student[q, slot], right, (((0,), (0,)), ((), ())), preferred_element_type=jnp.float32
            )

    def gather_grads(a):
        grad_mate(0, a).wait_recv()
        add_image(x, a)
        for s in range(1, n_x):
            grad_copy(s, a).wait_recv()
            grad_mate(s, a).start()
        for s in range(1, n_x):
            grad_mate(s, a).wait_recv()
            add_image(x_source(s), a)

    def student_begin():
        for s in range(1, n_dp):
            slot_copy(s).wait_recv()
        table = pltpu.make_async_copy(slot_rows, slot_table, slot_sem)
        table.start()
        for s in range(1, n_x):
            for q in range(1, share):
                stu_z(s, q).wait_recv()
            stu_mate(s).start()
        table.wait()
        out_ref[...] = jnp.zeros_like(out_ref)
        for s in range(n_x):
            stu_mate(s).wait_recv()
        for a in range(everyone):
            student_forward(a)

    for i in range(images):
        if i + 1 < images:
            pass_on(i + 1, 0)
        if i == 0:
            student_begin()
        passed_on(i)
        for a in range(i * CORES, (i + 1) * CORES):
            for s in range(1, n_x):
                other_chip(s, a, before)
                before = (s, a)
            if a == i * CORES and i + 1 < images:
                pass_on(i + 1, 1)
        if i == 0:
            attend_image(0)
    for a in range(1, everyone):
        attend_image(a)
        student_back(a - 1)
    for a in range(everyone - 1):
        gather_grads(a)
    student_back(everyone - 1)
    gather_grads(everyone - 1)

    def drain_half(half):
        for i in range(images):
            for n in range(2):
                for s in range(1, n_x):
                    for c in range(CORES):
                        row_x(s, c, i, half, n).wait_send()
                        row_z(s, c, i, half, n).wait_send()

    on_half(parity, drain_half)
    for s in range(1, n_dp):
        slot_copy(s).wait_send()
    for s in range(n_x):
        stu_mate(s).wait_send()
    for s in range(1, n_x):
        stu_x(s).wait_send()
        for q in range(1, share):
            stu_z(s, q).wait_send()
    for i in range(images):
        row_mate(i).wait_send()
    for a in range(everyone):
        if a >= everyone - 2:
            fold_copy(a).wait_send()
        for s in range(1, n_tensor):
            map_copy(s, a).wait_send()
        for s in range(1, n_x):
            grad_copy(s, a).wait_send()
        for s in range(n_x):
            grad_mate(s, a).wait_send()

        def drain(b, carry):
            if before == (before[0], a):
                part_copy(before[0], a, b).wait_send()
            for s in range(1, n_x):
                sum_copy(s, a, b).wait_send()
            return carry

        lax.fori_loop(0, mine, drain, 0)


def on_device(
    mesh_sizes,
    teacher_input,
    teacher_gain,
    teacher_weight,
    head_counts,
    assignment,
    student_input,
    student_gain,
    student_bias,
    student_weight,
):
    n_dp, n_tensor = mesh_sizes
    images, tokens, width = teacher_input.shape
    rows, _, width_here = teacher_weight.shape
    s_width, s_width_here = student_weight.shape
    heads_here = width_here // HD_T
    s_heads = head_counts.shape[1]
    s_here = s_heads // n_tensor
    pad = rounded_up(tokens, 16)
    n_x = n_dp // CORES
    others = max(n_x - 1, 1)
    per_block = 2 if heads_here % 2 == 0 else 1
    blocks = heads_here // per_block
    block_width = per_block * HD_T
    chunk = 192
    share = min(SHARE, n_tensor)
    both = pad + QROWS
    sizes = (n_dp, n_tensor, s_heads, images, tokens, pad, blocks, chunk)
    by_heads = blocks % CORES == 0 and s_here % CORES == 0
    dma = pltpu.SemaphoreType.DMA
    half = jnp.bfloat16
    in_vmem = pl.BlockSpec(memory_space=pltpu.VMEM)
    in_smem = pl.BlockSpec(memory_space=pltpu.SMEM)
    anywhere = pl.BlockSpec(memory_space=pl.ANY)
    if by_heads:
        kernel, units, mine, s_mine = distill_by_heads, images * CORES, blocks // CORES, s_here // CORES
        grads = (n_x, units, CORES, s_mine, pad, 2 * HD_S)
        folds = (2, n_tensor * s_mine, pad, QROWS)
        acc = (CORES,) + folds[1:]
        extra_memory = [pltpu.VMEM(folds, half), pltpu.VMEM(folds, half), dma((units,)), dma((units,))]
        extra_sem = [dma((images,))]
    else:
        kernel, units, mine, s_mine = distill_by_images, images, blocks, s_here
        grads = (images, n_dp, s_here, pad, 2 * HD_S)
        acc = (s_heads, pad, QROWS)
        extra_memory, extra_sem = [], []
    return pl.pallas_call(
        functools.partial(kernel, sizes),
        out_shape=jax.ShapeDtypeStruct((s_width, s_width_here), jnp.float32),
        in_specs=[
            in_smem,
            in_smem,
            anywhere,
            in_vmem,
            anywhere,
            anywhere,
            in_vmem,
            in_vmem,
            in_vmem,
        ],
        out_specs=in_vmem,
        scratch_shapes=[
            pltpu.VMEM((2, blocks, rows, block_width), half),
            pltpu.VMEM((n_dp, images, pad, rows), half),
            pltpu.VMEM((images, n_dp, pad, rows), half),
            pltpu.VMEM((mine, both, block_width), half),
            pltpu.VMEM((n_x, units, mine, both, block_width), half),
            pltpu.VMEM((others, units, mine, both, block_width), half),
            pltpu.VMEM((2, both, block_width), jnp.float32),
            pltpu.VMEM(acc, jnp.float32),
            pltpu.VMEM((units, n_tensor * s_mine, pad, QROWS), half),
            pltpu.VMEM((n_tensor - 1, units, s_mine, pad, QROWS), half),
            pltpu.VMEM((share, n_dp * images, pad, s_width // share), half),
            pltpu.VMEM((units, s_mine, pad, 2 * HD_S), half),
            pltpu.VMEM((units, s_mine, pad, QROWS), jnp.float32),
            pltpu.VMEM(grads, half),
            pltpu.VMEM((n_dp, 8, 128), jnp.int32),
            pltpu.SMEM((n_dp, 8, 128), jnp.int32),
            dma((2,)),
            dma((2,)),
            dma,
            dma,
            *extra_sem,
            dma((images,)),
            dma((images,)),
            dma((others, CORES, images, 2)),
            dma((others, CORES, images, 2)),
            dma((others, CORES, images, 2)),
            dma((others, CORES, images, 2)),
            dma((n_x, units, mine)),
            dma((n_x, units, mine)),
            dma((others, units, mine)),
            dma((others, units, mine)),
            dma((n_tensor - 1, units)),
            dma((n_tensor - 1, units)),
            dma((others, units)),
            dma((others, units)),
            dma((n_x, units)),
            dma((n_x, units)),
            *extra_memory,
            dma((n_dp - 1,)),
            dma((n_dp - 1,)),
            dma((n_x,)),
            dma((n_x,)),
            dma((others,)),
            dma((others,)),
            dma((others, share - 1)),
            dma((others, share - 1)),
        ],
        compiler_params=pltpu.CompilerParams(
            collective_id=0, has_side_effects=True, vmem_limit_bytes=67043328
        ),
    )(
        jnp.transpose(head_counts),
        assignment,
        jnp.transpose(teacher_input, (1, 0, 2)),
        teacher_gain.reshape(1, width),
        teacher_weight,
        jnp.transpose(student_input, (1, 0, 2)),
        student_gain.reshape(1, s_width),
        student_bias.reshape(1, s_width),
        student_weight,
    )


def solution(mesh):
    placed = (
        P(("group", "dp"), None, None),
        P(),
        P("dp", None, "tensor"),
        P(),
        P(("group", "dp")),
        P(("group", "dp"), None, None),
        P(),
        P(),
        P(None, "tensor"),
    )
    mesh_sizes = (mesh.shape["dp"], mesh.shape["tensor"])
    return jax.shard_map(
        functools.partial(on_device, mesh_sizes),
        mesh=mesh,
        in_specs=placed,
        out_specs=P("group", "tensor"),
        check_vma=False,
    )
```

```python
import functools

import jax
import jax.numpy as jnp
from jax import lax
from jax.experimental import pallas as pl
from jax.experimental.pallas import tpu as pltpu
from jax.sharding import PartitionSpec as P

HD_T = 128
HD_S = 64
QROWS = 128
DIVISOR = 72
CORES = 2
SHARE = 4
MESH = pl.DeviceIdType.MESH


def layer_norm(values, gain, shift):
    wide = values.astype(jnp.float32)
    center = wide - jnp.mean(wide, axis=-1, keepdims=True)
    spread = jnp.mean(center * center, axis=-1, keepdims=True)
    return center * lax.rsqrt(spread + 1e-06) * gain + shift


def rounded_up(value, unit):
    return -(-value // unit) * unit


def key_softmax(scores, tokens):
    spot = lax.broadcasted_iota(jnp.int32, scores.shape, 0)
    scores = jnp.where(spot < tokens, scores, -jnp.inf)
    power = jnp.exp(scores - jnp.max(scores, axis=0, keepdims=True))
    return power / jnp.sum(power, axis=0, keepdims=True)


def distill_by_images(
    sizes,
    counts_ref,
    slots_ref,
    x_ref,
    gain_ref,
    w_ref,
    sx_ref,
    sgain_ref,
    sbias_ref,
    sw_ref,
    out_ref,
    wsplit,
    normed,
    rows_in,
    stage,
    from_mate,
    x_in,
    held,
    acc,
    made,
    landed,
    student,
    packed,
    probs,
    grads,
    slot_rows,
    slot_table,
    w_sem,
    x_sem,
    sx_sem,
    slot_sem,
    s_row_mate,
    r_row_mate,
    s_row_x,
    r_row_x,
    s_row_z,
    r_row_z,
    s_part,
    r_part,
    s_sum,
    r_sum,
    s_map,
    r_map,
    s_grad,
    r_grad,
    s_grad_mate,
    r_grad_mate,
    s_slot,
    r_slot,
    s_stu_mate,
    r_stu_mate,
    s_stu_x,
    r_stu_x,
    s_stu_z,
    r_stu_z,
):
    n_dp, n_tensor, s_heads, images, tokens, pad, blocks, chunk = sizes
    n_x = n_dp // CORES
    depth = w_ref.shape[0]
    width = wsplit.shape[3]
    s_here = s_heads // n_tensor
    s_cols = 2 * HD_S
    share, s_depth = student.shape[0], student.shape[3]
    w_chunks = depth // chunk

    dp = lax.axis_index("dp")
    t = lax.axis_index("tensor")
    x = dp // CORES
    core = lax.rem(dp, CORES)
    mate = x * CORES + (1 - core)
    parity = lax.rem(t, 2)
    neighbour = t + 1 - 2 * parity
    quarter = lax.rem(t, share)

    def x_peer(s):
        return lax.rem(x + s, n_x)

    def x_source(s):
        return lax.rem(x + n_x - s, n_x)

    low = QROWS
    cut = (pad - low) // 32 * 16
    pieces = (
        ((0, low // 2), (low // 2, low // 2)),
        ((low, cut), (low + cut, pad - low - cut)),
    )

    def on_half(which, act):
        for half in range(2):

            @pl.when(which == half)
            def _():
                act(half)

    def slot_copy(s):
        return pltpu.make_async_remote_copy(
            src_ref=slot_rows.at[dp],
            dst_ref=slot_rows.at[dp],
            send_sem=s_slot.at[s - 1],
            recv_sem=r_slot.at[s - 1],
            device_id={"dp": lax.rem(dp + s, n_dp)},
            device_id_type=MESH,
        )

    def own_slots(source):
        return pl.ds(source * images, images)

    def stu_mate(s):
        where = student.at[:, own_slots(x_source(s) * CORES + core)]
        return pltpu.make_async_remote_copy(
            src_ref=where,
            dst_ref=where,
            send_sem=s_stu_mate.at[s],
            recv_sem=r_stu_mate.at[s],
            device_id={"dp": mate},
            device_id_type=MESH,
        )

    def stu_x(s):
        where = student.at[quarter, own_slots(dp)]
        return pltpu.make_async_remote_copy(
            src_ref=where,
            dst_ref=where,
            send_sem=s_stu_x.at[s - 1],
            recv_sem=r_stu_x.at[s - 1],
            device_id={"dp": x_peer(s) * CORES + core},
            device_id_type=MESH,
        )

    def stu_z(s, q):
        where = student.at[quarter, own_slots(x_source(s) * CORES + core)]
        return pltpu.make_async_remote_copy(
            src_ref=where,
            dst_ref=where,
            send_sem=s_stu_z.at[s - 1, q - 1],
            recv_sem=r_stu_z.at[s - 1, q - 1],
            device_id={"tensor": t - quarter + lax.rem(quarter + q, share)},
            device_id_type=MESH,
        )

    def row_mate(i):
        return pltpu.make_async_remote_copy(
            src_ref=normed.at[mate, i],
            dst_ref=rows_in.at[i, dp],
            send_sem=s_row_mate.at[i],
            recv_sem=r_row_mate.at[i],
            device_id={"dp": mate},
            device_id_type=MESH,
        )

    def row_x(s, c, i, half, n):
        first, many = pieces[half][n]
        to = x_peer(s) * CORES + c
        return pltpu.make_async_remote_copy(
            src_ref=normed.at[to, i, pl.ds(first, many)],
            dst_ref=rows_in.at[i, dp, pl.ds(first, many)],
            send_sem=s_row_x.at[s - 1, c, i, n],
            recv_sem=r_row_x.at[s - 1, core, i, n],
            device_id={"dp": to},
            device_id_type=MESH,
        )

    def row_x_arrived(s, c, i, half, n):
        first, many = pieces[half][n]
        return pltpu.make_async_remote_copy(
            src_ref=normed.at[dp, i, pl.ds(first, many)],
            dst_ref=rows_in.at[i, x_source(s) * CORES + c, pl.ds(first, many)],
            send_sem=s_row_x.at[s - 1, c, i, n],
            recv_sem=r_row_x.at[s - 1, c, i, n],
            device_id={"dp": mate},
            device_id_type=MESH,
        )

    def row_z(s, c, i, half, n):
        first, many = pieces[half][n]
        where = rows_in.at[i, x_source(s) * CORES + c, pl.ds(first, many)]
        return pltpu.make_async_remote_copy(
            src_ref=where,
            dst_ref=where,
            send_sem=s_row_z.at[s - 1, c, i, n],
            recv_sem=r_row_z.at[s - 1, c, i, n],
            device_id={"tensor": neighbour},
            device_id_type=MESH,
        )

    def part_copy(u, i, b):
        return pltpu.make_async_remote_copy(
            src_ref=stage.at[b],
            dst_ref=from_mate.at[u, i, b],
            send_sem=s_part.at[u, i, b],
            recv_sem=r_part.at[u, i, b],
            device_id={"dp": mate},
            device_id_type=MESH,
        )

    def sum_copy(s, i, b):
        return pltpu.make_async_remote_copy(
            src_ref=from_mate.at[s, i, b],
            dst_ref=x_in.at[s - 1, i, b],
            send_sem=s_sum.at[s - 1, i, b],
            recv_sem=r_sum.at[s - 1, i, b],
            device_id={"dp": x_peer(s) * CORES + core},
            device_id_type=MESH,
        )

    def map_copy(s, i):
        to = lax.rem(t + s, n_tensor)
        return pltpu.make_async_remote_copy(
            src_ref=made.at[i, pl.ds(to * s_here, s_here)],
            dst_ref=landed.at[s - 1, i],
            send_sem=s_map.at[s - 1, i],
            recv_sem=r_map.at[s - 1, i],
            device_id={"tensor": to},
            device_id_type=MESH,
        )

    def grad_copy(s, i):
        own = grads.at[i, dp]
        return pltpu.make_async_remote_copy(
            src_ref=own,
            dst_ref=own,
            send_sem=s_grad.at[s - 1, i],
            recv_sem=r_grad.at[s - 1, i],
            device_id={"dp": x_peer(s) * CORES + core},
            device_id_type=MESH,
        )

    def grad_mate(s, i):
        block = grads.at[i, x_source(s) * CORES + core]
        return pltpu.make_async_remote_copy(
            src_ref=block,
            dst_ref=block,
            send_sem=s_grad_mate.at[s, i],
            recv_sem=r_grad_mate.at[s, i],
            device_id={"dp": mate},
            device_id_type=MESH,
        )

    def greet():
        barrier = pltpu.get_barrier_semaphore()
        waits = 0
        for s in range(1, n_dp):
            pl.semaphore_signal(
                barrier, inc=1, device_id={"dp": lax.rem(dp + s, n_dp)}, device_id_type=MESH
            )
            waits += 1
        for s in range(1, n_tensor):
            pl.semaphore_signal(
                barrier, inc=1, device_id={"tensor": lax.rem(t + s, n_tensor)}, device_id_type=MESH
            )
            waits += 1
        pl.semaphore_wait(barrier, waits)

    def prepare(xraw, wraw, sraw):
        def w_copy(n):
            slot = lax.rem(n, 2)
            return pltpu.make_async_copy(
                w_ref.at[pl.ds(n * chunk, chunk)], wraw.at[slot], w_sem.at[slot]
            )

        def x_fetch(half):
            first = pieces[half][0][0]
            last = pieces[half][-1][0] + pieces[half][-1][1]
            many = min(last, tokens) - first
            return pltpu.make_async_copy(
                x_ref.at[pl.ds(first, many)], xraw.at[pl.ds(first, many)], x_sem.at[half]
            )

        sx_fetch = pltpu.make_async_copy(sx_ref, sraw.at[pl.ds(0, tokens)], sx_sem)
        sx_fetch.start()
        on_half(parity, lambda half: x_fetch(half).start())
        on_half(1 - parity, lambda half: x_fetch(half).start())
        w_copy(0).start()
        w_copy(1).start()
        xraw[tokens:pad] = jnp.zeros((pad - tokens,) + xraw.shape[1:], jnp.bfloat16)
        sraw[tokens:pad] = jnp.zeros((pad - tokens,) + sraw.shape[1:], jnp.bfloat16)
        for j in range(images):
            slot_rows[dp, j : j + 1, :] = jnp.full((1, 128), slots_ref[j], jnp.int32)
        greet()
        for s in range(1, n_dp):
            slot_copy(s).start()

        sx_fetch.wait()

        def student_rows(r, carry):
            spot = pl.ds(pl.multiple_of(r * 16, 16), 16)
            both = jnp.swapaxes(sraw[spot], 0, 1)
            for i in range(images):
                block = layer_norm(both[i], sgain_ref[...], sbias_ref[...]).astype(jnp.bfloat16)
                for q in range(share):
                    student[q, dp * images + i, spot, :] = block[:, q * s_depth : (q + 1) * s_depth]
            return carry

        lax.fori_loop(0, pad // 16, student_rows, 0)
        for s in range(1, n_x):
            stu_x(s).start()
        stu_mate(0).start()

        def norm_piece(first, many):
            def norm_rows(r, carry):
                spot = pl.multiple_of(first + r * 16, 16)
                both = jnp.swapaxes(xraw[pl.ds(spot, 16)], 0, 1)
                for i in range(images):
                    block = layer_norm(both[i], gain_ref[...], 0.0).astype(jnp.bfloat16)
                    for d in range(n_dp):
                        normed[d, i, pl.ds(spot, 16), :] = block[:, d * depth : (d + 1) * depth]
                return carry

            lax.fori_loop(0, many // 16, norm_rows, 0)

        def send_half(half):
            x_fetch(half).wait()
            for n in range(2):
                norm_piece(*pieces[half][n])
                for s in range(1, n_x):
                    for c in range(CORES):
                        row_x(s, c, 0, half, n).start()
            for i in range(1, images):
                for n in range(2):
                    for s in range(1, n_x):
                        for c in range(CORES):
                            row_x(s, c, i, half, n).start()

        def norm_half(half):
            x_fetch(half).wait()
            for n in range(2):
                norm_piece(*pieces[half][n])

        on_half(parity, send_half)
        on_half(1 - parity, norm_half)
        for i in range(images):
            row_mate(i).start()

        def split(n, carry):
            w_copy(n).wait()
            slot = lax.rem(n, 2)
            spot = pl.ds(pl.multiple_of(n * chunk, chunk), chunk)
            for b in range(blocks):
                both = jnp.swapaxes(wraw[slot, :, :, b * width : (b + 1) * width], 0, 1)
                wsplit[0, b, spot, :] = both[0]
                wsplit[1, b, spot, :] = both[1]

            @pl.when(n + 2 < w_chunks)
            def _():
                w_copy(n + 2).start()

            return carry

        lax.fori_loop(0, w_chunks, split, 0)

    pl.run_scoped(
        prepare,
        pltpu.VMEM((pad,) + x_ref.shape[1:], jnp.bfloat16),
        pltpu.VMEM((2, chunk) + w_ref.shape[1:], jnp.bfloat16),
        pltpu.VMEM((pad,) + sx_ref.shape[1:], jnp.bfloat16),
    )

    acc[...] = jnp.zeros_like(acc)

    def project(lhs, b):
        keys = jnp.dot(lhs[...], wsplit[1, b], preferred_element_type=jnp.float32)
        query = jnp.dot(lhs[:QROWS], wsplit[0, b], preferred_element_type=jnp.float32)
        return keys, query

    def to_mate(u, i, b, before, lhs):
        keys, query = project(lhs, b)
        if before is not None:
            part_copy(*before, b).wait_send()
        stage[b, :pad] = keys.astype(jnp.bfloat16)
        stage[b, pad:] = query.astype(jnp.bfloat16)
        part_copy(u, i, b).start()

    def own_chip(i, before):
        row_mate(i).wait_recv()

        def body(b, carry):
            to_mate(0, i, b, before, rows_in.at[i, mate])
            return carry

        lax.fori_loop(0, blocks, body, 0)

    def other_chip(s, i, before, start, stop):
        def body(b, carry):
            @pl.when(b < blocks)
            def _():
                away = x_peer(s) * CORES
                to_mate(s, i, b, before, rows_in.at[i, away + 1 - core])
                keys, query = project(rows_in.at[i, away + core], b)
                held[lax.rem(b, 2), :pad] = keys
                held[lax.rem(b, 2), pad:] = query

            @pl.when(b > 0)
            def _():
                j = b - 1
                part_copy(s, i, j).wait_recv()
                total = held[lax.rem(j, 2)] + from_mate[s, i, j].astype(jnp.float32)
                from_mate[s, i, j] = total.astype(jnp.bfloat16)
                sum_copy(s, i, j).start()

            return carry

        lax.fori_loop(start, stop, body, 0)

    def pass_on(i, n):
        def act(half):
            for s in range(1, n_x):
                for c in range(CORES):
                    row_x_arrived(s, c, i, half, n).wait_recv()
                    row_z(s, c, i, half, n).start()

        on_half(parity, act)

    def passed_on(i):
        def act(half):
            for n in range(2):
                for s in range(1, n_x):
                    for c in range(CORES):
                        row_z(s, c, i, half, n).wait_recv()

        on_half(1 - parity, act)

    before = None
    for i in range(images):
        pass_on(0, i) if i < 2 else None
        own_chip(i, before)
        before = (0, i)
    for n in range(images, 2):
        pass_on(0, n)
    for i in range(images):
        if i + 1 < images:
            pass_on(i + 1, 0)
        passed_on(i)
        for s in range(1, n_x):
            early = blocks // 2 if s == 1 else 0
            other_chip(s, i, before, 0, early)
            if s == 1 and i + 1 < images:
                pass_on(i + 1, 1)
            other_chip(s, i, before, early, blocks + 1)
            before = (s, i)
        if i == 0:
            for s in range(1, n_x):
                stu_x(s).wait_recv()
                for q in range(1, share):
                    stu_z(s, q).start()

    def attend_image(i):
        def attend(b, carry):
            keys, query = project(normed.at[dp, i], b)
            part_copy(0, i, b).wait_recv()
            keys += from_mate[0, i, b, :pad].astype(jnp.float32)
            query += from_mate[0, i, b, pad:].astype(jnp.float32)
            for s in range(1, n_x):
                sum_copy(s, i, b).wait_recv()
                keys += x_in[s - 1, i, b, :pad].astype(jnp.float32)
                query += x_in[s - 1, i, b, pad:].astype(jnp.float32)
            keys = keys.astype(jnp.bfloat16)
            query = (query * HD_T ** (-0.5)).astype(jnp.bfloat16)
            maps = []
            for h in range(width // HD_T):
                cols = slice(h * HD_T, (h + 1) * HD_T)
                scores = lax.dot_general(
                    keys[:, cols],
                    query[:, cols],
                    (((1,), (1,)), ((), ())),
                    preferred_element_type=jnp.float32,
                )
                one = key_softmax(scores, tokens)
                maps.append(one.astype(jnp.bfloat16).astype(jnp.float32))
            first = t * (blocks * (width // HD_T)) + b * (width // HD_T)
            for s in range(s_heads):
                total = acc[s]
                for h, one in enumerate(maps):
                    total += counts_ref[s, first + h].astype(jnp.float32) * one
                acc[s] = total
            return carry

        lax.fori_loop(0, blocks, attend, 0)

        def finish(s, carry):
            made[i, s] = (acc[s] / DIVISOR).astype(jnp.bfloat16)
            acc[s] = jnp.zeros(acc.shape[1:], jnp.float32)
            return carry

        lax.fori_loop(0, s_heads, finish, 0)
        for s in range(1, n_tensor):
            map_copy(s, i).start()

    def slot_of(image):
        found = jnp.int32(0)
        for d in range(n_dp):
            for j in range(images):
                here = jnp.where(slot_table[d, j, 0] == image, d * images + j, 0)
                found = jnp.maximum(found, here)
        return found

    left = lax.broadcasted_iota(jnp.int32, (pad, s_cols), 1) < HD_S

    def student_forward(i):
        slot = slot_of(dp * images + i)
        total = jnp.zeros((pad, s_here * s_cols), jnp.float32)
        for q in range(share):
            total += jnp.dot(
                student[q, slot],
                sw_ref[q * s_depth : (q + 1) * s_depth, :],
                preferred_element_type=jnp.float32,
            )
        for h in range(s_here):
            one = total[:, h * s_cols : (h + 1) * s_cols]
            one = jnp.where(left, one * HD_S ** (-0.5), one).astype(jnp.bfloat16)
            packed[i, h] = one
            keys, query, _ = apart(one)
            scores = lax.dot_general(
                keys, one[:QROWS], (((1,), (1,)), ((), ())), preferred_element_type=jnp.float32
            )
            probs[i, h] = key_softmax(scores, tokens)

    def apart(one):
        wide = one.astype(jnp.float32)
        turned = jnp.concatenate([wide[:, HD_S:], wide[:, :HD_S]], axis=1)
        keys = jnp.where(left, turned, 0.0).astype(jnp.bfloat16)
        query = jnp.where(left, 0.0, turned).astype(jnp.bfloat16)[:QROWS]
        return keys, query, turned

    def student_back(i):
        for s in range(1, n_tensor):
            map_copy(s, i).wait_recv()

        def head(h, carry):
            goal = made[i, t * s_here + h].astype(jnp.float32)
            for s in range(1, n_tensor):
                goal += landed[s - 1, i, h].astype(jnp.float32)
            goal = goal.astype(jnp.bfloat16).astype(jnp.float32)
            slope = probs[i, h] * jnp.sum(goal, axis=0, keepdims=True) - goal
            slope = slope.astype(jnp.bfloat16)
            keys, query, _ = apart(packed[i, h])
            for_query = (
                lax.dot_general(
                    slope, keys, (((0,), (0,)), ((), ())), preferred_element_type=jnp.float32
                )
                * HD_S ** (-0.5)
            )
            for_keys = jnp.dot(slope, query, preferred_element_type=jnp.float32)
            grads[i, dp, h, :QROWS] = (for_query + for_keys[:QROWS]).astype(jnp.bfloat16)
            grads[i, dp, h, QROWS:] = for_keys[QROWS:].astype(jnp.bfloat16)
            return carry

        lax.fori_loop(0, s_here, head, 0)
        for s in range(1, n_x):
            grad_copy(s, i).start()
        grad_mate(0, i).start()

    def add_images(i, source):
        slot = slot_of(source * images + i)
        right = jnp.concatenate([grads[i, source, h] for h in range(s_here)], axis=1)
        for q in range(share):
            rows = pl.ds(q * s_depth, s_depth)
            out_ref[rows, :] += lax.dot_general(
                student[q, slot], right, (((0,), (0,)), ((), ())), preferred_element_type=jnp.float32
            )

    def gather_grads(i):
        add_images(i, dp)
        grad_mate(0, i).wait_recv()
        add_images(i, mate)
        for s in range(1, n_x):
            grad_copy(s, i).wait_recv()
            grad_mate(s, i).start()
            add_images(i, x_source(s) * CORES + core)
        for s in range(1, n_x):
            grad_mate(s, i).wait_recv()
            add_images(i, x_source(s) * CORES + 1 - core)

    attend_image(0)
    for s in range(1, n_dp):
        slot_copy(s).wait_recv()
    table = pltpu.make_async_copy(slot_rows, slot_table, slot_sem)
    table.start()
    for s in range(1, n_x):
        for q in range(1, share):
            stu_z(s, q).wait_recv()
        stu_mate(s).start()
    table.wait()
    for s in range(n_x):
        stu_mate(s).wait_recv()
    for i in range(images):
        student_forward(i)
    out_ref[...] = jnp.zeros_like(out_ref)
    for i in range(1, images):
        attend_image(i)
    for i in range(images):
        student_back(i)
        gather_grads(i)

    def drain_half(half):
        for i in range(images):
            for n in range(2):
                for s in range(1, n_x):
                    for c in range(CORES):
                        row_x(s, c, i, half, n).wait_send()
                        row_z(s, c, i, half, n).wait_send()

    on_half(parity, drain_half)
    for s in range(1, n_dp):
        slot_copy(s).wait_send()
    for s in range(n_x):
        stu_mate(s).wait_send()
    for s in range(1, n_x):
        stu_x(s).wait_send()
        for q in range(1, share):
            stu_z(s, q).wait_send()
    for i in range(images):
        row_mate(i).wait_send()
        for s in range(1, n_tensor):
            map_copy(s, i).wait_send()
        for s in range(1, n_x):
            grad_copy(s, i).wait_send()
        for s in range(n_x):
            grad_mate(s, i).wait_send()

        def drain(b, carry):
            if before == (before[0], i):
                part_copy(before[0], i, b).wait_send()
            for s in range(1, n_x):
                sum_copy(s, i, b).wait_send()
            return carry

        lax.fori_loop(0, blocks, drain, 0)


def distill_by_heads(
    sizes,
    counts_ref,
    slots_ref,
    x_ref,
    gain_ref,
    w_ref,
    sx_ref,
    sgain_ref,
    sbias_ref,
    sw_ref,
    out_ref,
    wsplit,
    normed,
    rows_in,
    stage,
    from_mate,
    x_in,
    held,
    acc,
    made,
    landed,
    student,
    packed,
    probs,
    grads,
    slot_rows,
    slot_table,
    w_sem,
    x_sem,
    sx_sem,
    slot_sem,
    own_sem,
    s_row_mate,
    r_row_mate,
    s_row_x,
    r_row_x,
    s_row_z,
    r_row_z,
    s_part,
    r_part,
    s_sum,
    r_sum,
    s_map,
    r_map,
    s_grad,
    r_grad,
    s_grad_mate,
    r_grad_mate,
    fold_out,
    fold_in,
    s_fold,
    r_fold,
    s_slot,
    r_slot,
    s_stu_mate,
    r_stu_mate,
    s_stu_x,
    r_stu_x,
    s_stu_z,
    r_stu_z,
):
    n_dp, n_tensor, s_heads, images, tokens, pad, blocks, chunk = sizes
    n_x = n_dp // CORES
    depth = w_ref.shape[0]
    width = wsplit.shape[3]
    s_here = s_heads // n_tensor
    s_half = s_here // CORES
    mine = blocks // CORES
    everyone = images * CORES
    s_cols = 2 * HD_S
    share, s_depth = student.shape[0], student.shape[3]
    w_chunks = depth // chunk

    dp = lax.axis_index("dp")
    t = lax.axis_index("tensor")
    x = dp // CORES
    core = lax.rem(dp, CORES)
    mate = x * CORES + (1 - core)
    parity = lax.rem(t, 2)
    neighbour = t + 1 - 2 * parity
    quarter = lax.rem(t, share)

    def x_peer(s):
        return lax.rem(x + s, n_x)

    def x_source(s):
        return lax.rem(x + n_x - s, n_x)

    low = QROWS
    cut = (pad - low) // 32 * 16
    pieces = (
        ((0, low // 2), (low // 2, low // 2)),
        ((low, cut), (low + cut, pad - low - cut)),
    )

    def on_half(which, act):
        for half in range(2):

            @pl.when(which == half)
            def _():
                act(half)

    def slot_copy(s):
        return pltpu.make_async_remote_copy(
            src_ref=slot_rows.at[dp],
            dst_ref=slot_rows.at[dp],
            send_sem=s_slot.at[s - 1],
            recv_sem=r_slot.at[s - 1],
            device_id={"dp": lax.rem(dp + s, n_dp)},
            device_id_type=MESH,
        )

    def own_slots(source):
        return pl.ds(source * images, images)

    def stu_mate(s):
        where = student.at[:, own_slots(x_source(s) * CORES + core)]
        return pltpu.make_async_remote_copy(
            src_ref=where,
            dst_ref=where,
            send_sem=s_stu_mate.at[s],
            recv_sem=r_stu_mate.at[s],
            device_id={"dp": mate},
            device_id_type=MESH,
        )

    def stu_x(s):
        where = student.at[quarter, own_slots(dp)]
        return pltpu.make_async_remote_copy(
            src_ref=where,
            dst_ref=where,
            send_sem=s_stu_x.at[s - 1],
            recv_sem=r_stu_x.at[s - 1],
            device_id={"dp": x_peer(s) * CORES + core},
            device_id_type=MESH,
        )

    inner = (quarter == 1) | (quarter == 2)
    own_pair = quarter // 2 * 2

    def stu_z(s, step):
        source = own_slots(x_source(s) * CORES + core)
        if step == 0:
            where, to = student.at[quarter, source], neighbour
        elif step == 1:
            where, to = student.at[pl.ds(own_pair, 2), source], t + 3 - 2 * quarter
        else:
            where, to = student.at[pl.ds(2 - own_pair, 2), source], neighbour
        return pltpu.make_async_remote_copy(
            src_ref=where,
            dst_ref=where,
            send_sem=s_stu_z.at[s - 1, step],
            recv_sem=r_stu_z.at[s - 1, step],
            device_id={"tensor": to},
            device_id_type=MESH,
        )

    def spread(step):
        for s in range(1, n_x):
            if step == 0:
                stu_x(s).wait_recv()
                stu_z(s, 0).start()
            else:
                if step == 1:
                    stu_z(s, 0).wait_recv()

                @pl.when(inner)
                def _():
                    if step == 2:
                        stu_z(s, 1).wait_recv()
                    stu_z(s, step).start()

    def spread_end():
        for s in range(1, n_x):

            @pl.when(jnp.logical_not(inner))
            def _():
                stu_z(s, 2).wait_recv()

    def spread_sent():
        for s in range(1, n_x):
            stu_z(s, 0).wait_send()

            @pl.when(inner)
            def _():
                stu_z(s, 1).wait_send()
                stu_z(s, 2).wait_send()

    def row_mate(i):
        return pltpu.make_async_remote_copy(
            src_ref=normed.at[mate, i],
            dst_ref=rows_in.at[i, dp],
            send_sem=s_row_mate.at[i],
            recv_sem=r_row_mate.at[i],
            device_id={"dp": mate},
            device_id_type=MESH,
        )

    def row_own(i):
        return pltpu.make_async_copy(normed.at[dp, i], rows_in.at[i, dp], own_sem.at[i])

    def row_x(s, c, i, half, n):
        first, many = pieces[half][n]
        to = x_peer(s) * CORES + c
        return pltpu.make_async_remote_copy(
            src_ref=normed.at[to, i, pl.ds(first, many)],
            dst_ref=rows_in.at[i, dp, pl.ds(first, many)],
            send_sem=s_row_x.at[s - 1, c, i, n],
            recv_sem=r_row_x.at[s - 1, core, i, n],
            device_id={"dp": to},
            device_id_type=MESH,
        )

    def row_x_arrived(s, c, i, half, n):
        first, many = pieces[half][n]
        return pltpu.make_async_remote_copy(
            src_ref=normed.at[dp, i, pl.ds(first, many)],
            dst_ref=rows_in.at[i, x_source(s) * CORES + c, pl.ds(first, many)],
            send_sem=s_row_x.at[s - 1, c, i, n],
            recv_sem=r_row_x.at[s - 1, c, i, n],
            device_id={"dp": mate},
            device_id_type=MESH,
        )

    def row_z(s, c, i, half, n):
        first, many = pieces[half][n]
        where = rows_in.at[i, x_source(s) * CORES + c, pl.ds(first, many)]
        return pltpu.make_async_remote_copy(
            src_ref=where,
            dst_ref=where,
            send_sem=s_row_z.at[s - 1, c, i, n],
            recv_sem=r_row_z.at[s - 1, c, i, n],
            device_id={"tensor": neighbour},
            device_id_type=MESH,
        )

    def part_copy(u, i, b):
        return pltpu.make_async_remote_copy(
            src_ref=stage.at[b],
            dst_ref=from_mate.at[u, i, b],
            send_sem=s_part.at[u, i, b],
            recv_sem=r_part.at[u, i, b],
            device_id={"dp": mate},
            device_id_type=MESH,
        )

    def sum_copy(s, i, b):
        return pltpu.make_async_remote_copy(
            src_ref=from_mate.at[s, i, b],
            dst_ref=x_in.at[s - 1, i, b],
            send_sem=s_sum.at[s - 1, i, b],
            recv_sem=r_sum.at[s - 1, i, b],
            device_id={"dp": x_peer(s) * CORES + core},
            device_id_type=MESH,
        )

    def map_copy(s, i):
        to = lax.rem(t + s, n_tensor)
        return pltpu.make_async_remote_copy(
            src_ref=made.at[i, pl.ds(to * s_half, s_half)],
            dst_ref=landed.at[s - 1, i],
            send_sem=s_map.at[s - 1, i],
            recv_sem=r_map.at[s - 1, i],
            device_id={"tensor": to},
            device_id_type=MESH,
        )

    def grad_copy(s, i):
        own = grads.at[x, i, core]
        return pltpu.make_async_remote_copy(
            src_ref=own,
            dst_ref=own,
            send_sem=s_grad.at[s - 1, i],
            recv_sem=r_grad.at[s - 1, i],
            device_id={"dp": x_peer(s) * CORES + core},
            device_id_type=MESH,
        )

    def grad_mate(s, i):
        block = grads.at[x_source(s), i, core]
        return pltpu.make_async_remote_copy(
            src_ref=block,
            dst_ref=block,
            send_sem=s_grad_mate.at[s, i],
            recv_sem=r_grad_mate.at[s, i],
            device_id={"dp": mate},
            device_id_type=MESH,
        )

    def greet():
        barrier = pltpu.get_barrier_semaphore()
        waits = 0
        for s in range(1, n_dp):
            pl.semaphore_signal(
                barrier, inc=1, device_id={"dp": lax.rem(dp + s, n_dp)}, device_id_type=MESH
            )
            waits += 1
        for s in range(1, n_tensor):
            pl.semaphore_signal(
                barrier, inc=1, device_id={"tensor": lax.rem(t + s, n_tensor)}, device_id_type=MESH
            )
            waits += 1
        pl.semaphore_wait(barrier, waits)

    def prepare(xraw, wraw, sraw):
        def w_copy(n):
            slot = lax.rem(n, 2)
            return pltpu.make_async_copy(
                w_ref.at[pl.ds(n * chunk, chunk)], wraw.at[slot], w_sem.at[slot]
            )

        def x_fetch(half):
            first = pieces[half][0][0]
            last = pieces[half][-1][0] + pieces[half][-1][1]
            many = min(last, tokens) - first
            return pltpu.make_async_copy(
                x_ref.at[pl.ds(first, many)], xraw.at[pl.ds(0, many)], x_sem.at[half]
            )

        sx_fetch = pltpu.make_async_copy(sx_ref, sraw.at[pl.ds(0, tokens)], sx_sem)
        sx_fetch.start()
        on_half(parity, lambda half: x_fetch(half).start())
        w_copy(0).start()
        w_copy(1).start()
        def clear(half):
            first = pieces[half][0][0]
            stop = pieces[half][-1][0] + pieces[half][-1][1]
            if stop > tokens:
                xraw[tokens - first : stop - first] = jnp.zeros(
                    (stop - tokens,) + xraw.shape[1:], jnp.bfloat16
                )

        on_half(parity, clear)
        sraw[tokens:pad] = jnp.zeros((pad - tokens,) + sraw.shape[1:], jnp.bfloat16)
        for j in range(images):
            slot_rows[dp, j : j + 1, :] = jnp.full((1, 128), slots_ref[j], jnp.int32)
        greet()
        for s in range(1, n_dp):
            slot_copy(s).start()

        sx_fetch.wait()

        def student_rows(r, carry):
            spot = pl.ds(pl.multiple_of(r * 16, 16), 16)
            both = jnp.swapaxes(sraw[spot], 0, 1)
            for i in range(images):
                block = layer_norm(both[i], sgain_ref[...], sbias_ref[...]).astype(jnp.bfloat16)
                for q in range(share):
                    student[q, dp * images + i, spot, :] = block[:, q * s_depth : (q + 1) * s_depth]
            return carry

        lax.fori_loop(0, pad // 16, student_rows, 0)
        for s in range(1, n_x):
            stu_x(s).start()
        stu_mate(0).start()

        def norm_piece(base, first, many):
            def norm_rows(r, carry):
                spot = pl.multiple_of(first + r * 16, 16)
                both = jnp.swapaxes(xraw[pl.ds(spot - base, 16)], 0, 1)
                for i in range(images):
                    block = layer_norm(both[i], gain_ref[...], 0.0).astype(jnp.bfloat16)
                    for d in range(n_dp):
                        normed[d, i, pl.ds(spot, 16), :] = block[:, d * depth : (d + 1) * depth]
                return carry

            lax.fori_loop(0, many // 16, norm_rows, 0)

        def send_half(first):
            def act(half):
                x_fetch(half).wait()
                for n in range(2):
                    norm_piece(pieces[half][0][0], *pieces[half][n])
                    if first == 0:
                        for s in range(1, n_x):
                            for c in range(CORES):
                                row_x(s, c, 0, half, n).start()
                for i in range(1, images if first == 0 else 1):
                    for n in range(2):
                        for s in range(1, n_x):
                            for c in range(CORES):
                                row_x(s, c, i, half, n).start()

            return act

        on_half(parity, send_half(0))
        spread(0)

        def fetch_rest(half):
            clear(half)
            x_fetch(half).start()

        on_half(1 - parity, fetch_rest)

        def split(n, carry):
            w_copy(n).wait()
            slot = lax.rem(n, 2)
            spot = pl.ds(pl.multiple_of(n * chunk, chunk), chunk)
            for b in range(blocks):
                both = jnp.swapaxes(wraw[slot, :, :, b * width : (b + 1) * width], 0, 1)
                wsplit[0, b, spot, :] = both[0]
                wsplit[1, b, spot, :] = both[1]

            @pl.when(n + 2 < w_chunks)
            def _():
                w_copy(n + 2).start()

            return carry

        lax.fori_loop(0, w_chunks, split, 0)
        on_half(1 - parity, send_half(1))
        for i in range(images):
            row_mate(i).start()
            row_own(i).start()

    pl.run_scoped(
        prepare,
        pltpu.VMEM((pad - low,) + x_ref.shape[1:], jnp.bfloat16),
        pltpu.VMEM((2, chunk) + w_ref.shape[1:], jnp.bfloat16),
        pltpu.VMEM((pad,) + sx_ref.shape[1:], jnp.bfloat16),
    )

    acc[...] = jnp.zeros_like(acc)

    def project(lhs, b):
        keys = jnp.dot(lhs[...], wsplit[1, b], preferred_element_type=jnp.float32)
        query = jnp.dot(lhs[:QROWS], wsplit[0, b], preferred_element_type=jnp.float32)
        return keys, query

    def rows_of(place, a):
        return rows_in.at[a // CORES, place * CORES + a % CORES]

    def to_mate(u, a, b, before, lhs):
        keys, query = project(lhs, (1 - core) * mine + b)
        if before is not None:
            part_copy(*before, b).wait_send()
        stage[b, :pad] = keys.astype(jnp.bfloat16)
        stage[b, pad:] = query.astype(jnp.bfloat16)
        part_copy(u, a, b).start()

    def own_chip(a, before):
        def body(b, carry):
            to_mate(0, a, b, before, rows_of(x, a))
            return carry

        lax.fori_loop(0, mine, body, 0)

    def other_chip(s, a, before):
        def body(b, carry):
            @pl.when(b < mine)
            def _():
                lhs = rows_of(x_peer(s), a)
                to_mate(s, a, b, before, lhs)
                keys, query = project(lhs, core * mine + b)
                held[lax.rem(b, 2), :pad] = keys
                held[lax.rem(b, 2), pad:] = query

            @pl.when(b > 0)
            def _():
                j = b - 1
                part_copy(s, a, j).wait_recv()
                total = held[lax.rem(j, 2)] + from_mate[s, a, j].astype(jnp.float32)
                from_mate[s, a, j] = total.astype(jnp.bfloat16)
                sum_copy(s, a, j).start()

            return carry

        lax.fori_loop(0, mine + 1, body, 0)

    def pass_on(i, n):
        def act(half):
            for s in range(1, n_x):
                for c in range(CORES):
                    row_x_arrived(s, c, i, half, n).wait_recv()
                    row_z(s, c, i, half, n).start()

        on_half(parity, act)

    def passed_on(i):
        def act(half):
            for n in range(2):
                for s in range(1, n_x):
                    for c in range(CORES):
                        row_z(s, c, i, half, n).wait_recv()

        on_half(1 - parity, act)

    spread(1)
    for i in range(images):
        row_mate(i).wait_recv()
        row_own(i).wait()
    before = None
    for i in range(images):
        if i < 2:
            pass_on(0, i)
        for a in range(i * CORES, (i + 1) * CORES):
            own_chip(a, before)
            before = (0, a)
    for n in range(images, 2):
        pass_on(0, n)
    def fold_copy(a):
        return pltpu.make_async_remote_copy(
            src_ref=fold_out.at[a % 2],
            dst_ref=fold_in.at[a % 2],
            send_sem=s_fold.at[a],
            recv_sem=r_fold.at[a],
            device_id={"dp": mate},
            device_id_type=MESH,
        )

    def attend_image(a):
        def attend(b, carry):
            keys, query = project(rows_of(x, a), core * mine + b)
            part_copy(0, a, b).wait_recv()
            keys += from_mate[0, a, b, :pad].astype(jnp.float32)
            query += from_mate[0, a, b, pad:].astype(jnp.float32)
            for s in range(1, n_x):
                sum_copy(s, a, b).wait_recv()
                keys += x_in[s - 1, a, b, :pad].astype(jnp.float32)
                query += x_in[s - 1, a, b, pad:].astype(jnp.float32)
            keys = keys.astype(jnp.bfloat16)
            query = (query * HD_T ** (-0.5)).astype(jnp.bfloat16)
            maps = []
            for h in range(width // HD_T):
                cols = slice(h * HD_T, (h + 1) * HD_T)
                scores = lax.dot_general(
                    keys[:, cols],
                    query[:, cols],
                    (((1,), (1,)), ((), ())),
                    preferred_element_type=jnp.float32,
                )
                one = key_softmax(scores, tokens)
                maps.append(one.astype(jnp.bfloat16).astype(jnp.float32))
            first = (t * blocks + core * mine + b) * (width // HD_T)
            for s in range(s_heads):
                place, k = s // s_here, s % s_here
                spot = (k // s_half, place * s_half + k % s_half)
                total = jnp.where(b == 0, 0.0, acc[spot])
                for h, one in enumerate(maps):
                    total += counts_ref[s, first + h].astype(jnp.float32) * one
                acc[spot] = total
            return carry

        lax.fori_loop(0, mine, attend, 0)
        if a >= 2:
            fold_copy(a - 2).wait_send()

        def give(n, carry):
            fold_out[a % 2, n] = acc[1 - core, n].astype(jnp.bfloat16)
            return carry

        lax.fori_loop(0, n_tensor * s_half, give, 0)
        fold_copy(a).start()
        fold_copy(a).wait_recv()

        def finish(n, carry):
            total = acc[core, n] + fold_in[a % 2, n].astype(jnp.float32)
            made[a, n] = (total / DIVISOR).astype(jnp.bfloat16)
            return carry

        lax.fori_loop(0, n_tensor * s_half, finish, 0)
        for s in range(1, n_tensor):
            map_copy(s, a).start()

    def slot_of(image):
        found = jnp.int32(0)
        for d in range(n_dp):
            for j in range(images):
                here = jnp.where(slot_table[d, j, 0] == image, d * images + j, 0)
                found = jnp.maximum(found, here)
        return found

    left = lax.broadcasted_iota(jnp.int32, (pad, s_cols), 1) < HD_S

    def student_forward(a):
        slot = slot_of((x * CORES + a % CORES) * images + a // CORES)
        cols = pl.ds(pl.multiple_of(core * (s_half * s_cols), s_half * s_cols), s_half * s_cols)
        total = jnp.zeros((pad, s_half * s_cols), jnp.float32)
        for q in range(share):
            total += jnp.dot(
                student[q, slot],
                sw_ref[q * s_depth : (q + 1) * s_depth, cols],
                preferred_element_type=jnp.float32,
            )
        for h in range(s_half):
            one = total[:, h * s_cols : (h + 1) * s_cols]
            one = jnp.where(left, one * HD_S ** (-0.5), one).astype(jnp.bfloat16)
            packed[a, h] = one
            keys, query, _ = apart(one)
            scores = lax.dot_general(
                keys, one[:QROWS], (((1,), (1,)), ((), ())), preferred_element_type=jnp.float32
            )
            probs[a, h] = key_softmax(scores, tokens)

    def apart(one):
        wide = one.astype(jnp.float32)
        turned = jnp.concatenate([wide[:, HD_S:], wide[:, :HD_S]], axis=1)
        keys = jnp.where(left, turned, 0.0).astype(jnp.bfloat16)
        query = jnp.where(left, 0.0, turned).astype(jnp.bfloat16)[:QROWS]
        return keys, query, turned

    def student_back(i):
        for s in range(1, n_tensor):
            map_copy(s, i).wait_recv()

        def head(h, carry):
            goal = made[i, t * s_half + h].astype(jnp.float32)
            for s in range(1, n_tensor):
                goal += landed[s - 1, i, h].astype(jnp.float32)
            goal = goal.astype(jnp.bfloat16).astype(jnp.float32)
            slope = probs[i, h] * jnp.sum(goal, axis=0, keepdims=True) - goal
            slope = slope.astype(jnp.bfloat16)
            keys, query, _ = apart(packed[i, h])
            for_query = (
                lax.dot_general(
                    slope, keys, (((0,), (0,)), ((), ())), preferred_element_type=jnp.float32
                )
                * HD_S ** (-0.5)
            )
            for_keys = jnp.dot(slope, query, preferred_element_type=jnp.float32)
            grads[x, i, core, h, :QROWS] = (for_query + for_keys[:QROWS]).astype(jnp.bfloat16)
            grads[x, i, core, h, QROWS:] = for_keys[QROWS:].astype(jnp.bfloat16)
            return carry

        lax.fori_loop(0, s_half, head, 0)
        for s in range(1, n_x):
            grad_copy(s, i).start()
        grad_mate(0, i).start()

    def add_image(place, a):
        slot = slot_of((place * CORES + a % CORES) * images + a // CORES)
        right = jnp.concatenate(
            [grads[place, a, h // s_half, h % s_half] for h in range(s_here)], axis=1
        )
        for q in range(share):
            rows = pl.ds(q * s_depth, s_depth)
            out_ref[rows, :] += lax.dot_general(
                student[q, slot], right, (((0,), (0,)), ((), ())), preferred_element_type=jnp.float32
            )

    def gather_grads(a):
        grad_mate(0, a).wait_recv()
        add_image(x, a)
        for s in range(1, n_x):
            grad_copy(s, a).wait_recv()
            grad_mate(s, a).start()
        for s in range(1, n_x):
            grad_mate(s, a).wait_recv()
            add_image(x_source(s), a)

    def student_begin():
        for s in range(1, n_dp):
            slot_copy(s).wait_recv()
        table = pltpu.make_async_copy(slot_rows, slot_table, slot_sem)
        table.start()
        spread_end()
        for s in range(1, n_x):
            stu_mate(s).start()
        table.wait()
        out_ref[...] = jnp.zeros_like(out_ref)
        for s in range(n_x):
            stu_mate(s).wait_recv()
        for a in range(everyone):
            student_forward(a)

    for i in range(images):
        if i + 1 < images:
            pass_on(i + 1, 0)
        passed_on(i)
        for a in range(i * CORES, (i + 1) * CORES):
            for s in range(1, n_x):
                other_chip(s, a, before)
                before = (s, a)
            if a == i * CORES and i + 1 < images:
                pass_on(i + 1, 1)
        if i == 0:
            spread(2)
            attend_image(0)
    for a in range(1, everyone):
        attend_image(a)
        if a == 1:
            student_begin()
        student_back(a - 1)
    for a in range(everyone - 1):
        gather_grads(a)
    student_back(everyone - 1)
    gather_grads(everyone - 1)

    for i in range(images):

        def drain_half(half):
            for n in range(2):
                for s in range(1, n_x):
                    for c in range(CORES):
                        row_x(s, c, i, half, n).wait_send()
                        row_z(s, c, i, half, n).wait_send()

        on_half(parity, drain_half)
    for s in range(1, n_dp):
        slot_copy(s).wait_send()
    for s in range(n_x):
        stu_mate(s).wait_send()
    for s in range(1, n_x):
        stu_x(s).wait_send()
    spread_sent()
    for i in range(images):
        row_mate(i).wait_send()
    for a in range(everyone):
        if a >= everyone - 2:
            fold_copy(a).wait_send()
        for s in range(1, n_tensor):
            map_copy(s, a).wait_send()
        for s in range(1, n_x):
            grad_copy(s, a).wait_send()
        for s in range(n_x):
            grad_mate(s, a).wait_send()

        def drain(b, carry):
            if before == (before[0], a):
                part_copy(before[0], a, b).wait_send()
            for s in range(1, n_x):
                sum_copy(s, a, b).wait_send()
            return carry

        lax.fori_loop(0, mine, drain, 0)


def on_device(
    mesh_sizes,
    teacher_input,
    teacher_gain,
    teacher_weight,
    head_counts,
    assignment,
    student_input,
    student_gain,
    student_bias,
    student_weight,
):
    n_dp, n_tensor = mesh_sizes
    images, tokens, width = teacher_input.shape
    rows, _, width_here = teacher_weight.shape
    s_width, s_width_here = student_weight.shape
    heads_here = width_here // HD_T
    s_heads = head_counts.shape[1]
    s_here = s_heads // n_tensor
    pad = rounded_up(tokens, 16)
    n_x = n_dp // CORES
    others = max(n_x - 1, 1)
    per_block = 2 if heads_here % 2 == 0 else 1
    blocks = heads_here // per_block
    block_width = per_block * HD_T
    chunk = 192
    share = min(SHARE, n_tensor)
    both = pad + QROWS
    sizes = (n_dp, n_tensor, s_heads, images, tokens, pad, blocks, chunk)
    by_heads = blocks % CORES == 0 and s_here % CORES == 0 and n_tensor % SHARE == 0
    dma = pltpu.SemaphoreType.DMA
    half = jnp.bfloat16
    in_vmem = pl.BlockSpec(memory_space=pltpu.VMEM)
    in_smem = pl.BlockSpec(memory_space=pltpu.SMEM)
    anywhere = pl.BlockSpec(memory_space=pl.ANY)
    if by_heads:
        kernel, units, mine, s_mine = distill_by_heads, images * CORES, blocks // CORES, s_here // CORES
        grads = (n_x, units, CORES, s_mine, pad, 2 * HD_S)
        folds = (2, n_tensor * s_mine, pad, QROWS)
        acc = (CORES,) + folds[1:]
        extra_memory = [pltpu.VMEM(folds, half), pltpu.VMEM(folds, half), dma((units,)), dma((units,))]
        extra_sem = [dma((images,))]
    else:
        kernel, units, mine, s_mine = distill_by_images, images, blocks, s_here
        grads = (images, n_dp, s_here, pad, 2 * HD_S)
        acc = (s_heads, pad, QROWS)
        extra_memory, extra_sem = [], []
    return pl.pallas_call(
        functools.partial(kernel, sizes),
        out_shape=jax.ShapeDtypeStruct((s_width, s_width_here), jnp.float32),
        in_specs=[
            in_smem,
            in_smem,
            anywhere,
            in_vmem,
            anywhere,
            anywhere,
            in_vmem,
            in_vmem,
            in_vmem,
        ],
        out_specs=in_vmem,
        scratch_shapes=[
            pltpu.VMEM((2, blocks, rows, block_width), half),
            pltpu.VMEM((n_dp, images, pad, rows), half),
            pltpu.VMEM((images, n_dp, pad, rows), half),
            pltpu.VMEM((mine, both, block_width), half),
            pltpu.VMEM((n_x, units, mine, both, block_width), half),
            pltpu.VMEM((others, units, mine, both, block_width), half),
            pltpu.VMEM((2, both, block_width), jnp.float32),
            pltpu.VMEM(acc, jnp.float32),
            pltpu.VMEM((units, n_tensor * s_mine, pad, QROWS), half),
            pltpu.VMEM((n_tensor - 1, units, s_mine, pad, QROWS), half),
            pltpu.VMEM((share, n_dp * images, pad, s_width // share), half),
            pltpu.VMEM((units, s_mine, pad, 2 * HD_S), half),
            pltpu.VMEM((units, s_mine, pad, QROWS), jnp.float32),
            pltpu.VMEM(grads, half),
            pltpu.VMEM((n_dp, 8, 128), jnp.int32),
            pltpu.SMEM((n_dp, 8, 128), jnp.int32),
            dma((2,)),
            dma((2,)),
            dma,
            dma,
            *extra_sem,
            dma((images,)),
            dma((images,)),
            dma((others, CORES, images, 2)),
            dma((others, CORES, images, 2)),
            dma((others, CORES, images, 2)),
            dma((others, CORES, images, 2)),
            dma((n_x, units, mine)),
            dma((n_x, units, mine)),
            dma((others, units, mine)),
            dma((others, units, mine)),
            dma((n_tensor - 1, units)),
            dma((n_tensor - 1, units)),
            dma((others, units)),
            dma((others, units)),
            dma((n_x, units)),
            dma((n_x, units)),
            *extra_memory,
            dma((n_dp - 1,)),
            dma((n_dp - 1,)),
            dma((n_x,)),
            dma((n_x,)),
            dma((others,)),
            dma((others,)),
            dma((others, share - 1)),
            dma((others, share - 1)),
        ],
        compiler_params=pltpu.CompilerParams(
            collective_id=0, has_side_effects=True, vmem_limit_bytes=67043328
        ),
    )(
        jnp.transpose(head_counts),
        assignment,
        jnp.transpose(teacher_input, (1, 0, 2)),
        teacher_gain.reshape(1, width),
        teacher_weight,
        jnp.transpose(student_input, (1, 0, 2)),
        student_gain.reshape(1, s_width),
        student_bias.reshape(1, s_width),
        student_weight,
    )


def solution(mesh):
    placed = (
        P(("group", "dp"), None, None),
        P(),
        P("dp", None, "tensor"),
        P(),
        P(("group", "dp")),
        P(("group", "dp"), None, None),
        P(),
        P(),
        P(None, "tensor"),
    )
    mesh_sizes = (mesh.shape["dp"], mesh.shape["tensor"])
    return jax.shard_map(
        functools.partial(on_device, mesh_sizes),
        mesh=mesh,
        in_specs=placed,
        out_specs=P("group", "tensor"),
        check_vma=False,
    )
```
